32 devices in a mesh: grp: 4 (over z), seq: 8 (over y, x, core).
Axes of the slice: x: 2, y: 2, z: 4, core: 2. Of those that a mesh axis runs over, the one named last changes fastest.
Arguments:
- tokens: bfloat16 [4096, 2048], P(('grp', 'seq')), may hold values from -6 to 6
- norm_gains: float32 [2, 2048], replicated, may hold values from 0.5 to 1.5
- norm_biases: float32 [2, 2048], replicated, may hold values from -1 to 1
- mix_weight: bfloat16 [2048, 3, 2048], P(None, None, 'seq'), may hold values from -0.125 to 0.125
- mix_bias: bfloat16 [3, 2048], P(None, 'seq'), may hold values from -1.796875 to 1.796875
- out_weight: bfloat16 [2048, 2048], P('seq'), may hold values from -0.5 to 0.5
- gate_up_weight: bfloat16 [2048, 2, 5632], P(None, None, 'seq'), may hold values from -0.125 to 0.125
- down_weight: bfloat16 [5632, 2048], P('seq'), may hold values from -0.078125 to 0.078125
- row_lengths: int32 [8], replicated, may hold values from 128 to 1024, as said below
- row_group: int32 [8], replicated, may hold values from 0 to 3, as said below
- cotangent: bfloat16 [4096, 2048], P(('grp', 'seq')), may hold values from -6 to 6
Outputs:
- layer_out: bfloat16 [4096, 2048], P(('grp', 'seq'))
- tokens_grad: bfloat16 [4096, 2048], P(('grp', 'seq'))
- gains_grad: float32 [2, 2048], replicated
- biases_grad: float32 [2, 2048], replicated
- mix_grad: float32 [2048, 3, 2048], P(None, None, 'seq')
- mix_bias_grad: float32 [3, 2048], P(None, 'seq')
- out_grad: float32 [2048, 2048], P('seq')
- gate_up_grad: float32 [2048, 2, 5632], P(None, None, 'seq')
- down_grad: float32 [5632, 2048], P('seq')
The draws below stay inside these ranges and needn't reach their ends.
Inputs may be any that keep to these rules, and one draw needn't show every extreme that they name: `row_lengths`: rows 0 to 1 are 1024 long; every other row's length is a multiple of 128 and at most 256. `row_group`: each of rows 0 to 1 fills a group alone; every other group holds exactly three of the other rows.
All inputs are finite; a program needn't handle non-finite values.
Results may differ from the reference program's by a relative error of at most 0.02.
Values may be sent and summed in bfloat16 or wider, within the bound.
A program may use at most 320 MiB of HBM per device.

```python
import math
import jax
import jax.numpy as jnp
from jax import lax

D = 2048
HEAD_DIM = 64
ROT = 16
FF = 5632
CAP = 1024
SLOTS = 128
TOKENS = 4096
QBLOCK = 512
N_GRP = 4


def layout_rows(key):
    half = N_GRP // 2
    parts = CAP // SLOTS
    least = max(1, parts // 8)
    order = jax.random.permutation(jax.random.fold_in(key, 11), N_GRP).astype(jnp.int32)
    index = jnp.arange(3 * half, dtype=jnp.int32)
    long_groups = order[:half]
    short_groups = order[half + index // 3]
    units = jax.random.randint(jax.random.fold_in(key, 12), (3 * half,), least, parts // 4 + 1).astype(jnp.int32)
    units = jnp.where(index == 0, least, units)
    lengths = jnp.concatenate([jnp.full((half,), CAP, jnp.int32), units * SLOTS])
    return (lengths, jnp.concatenate([long_groups, short_groups]))


def draw_row_lengths(key, part):
    return layout_rows(key)[0]


def draw_row_group(key, part):
    return layout_rows(key)[1]


def levels(key, shape, cuts, smallest, largest):
    factor_of, own = 1.0, jax.random.fold_in(key, 6)
    for axis_at, shards_of in cuts:
        draws = jnp.exp(jax.random.uniform(jax.random.fold_in(own, axis_at), (shards_of,), jnp.float32, smallest / len(cuts), largest / len(cuts)))
        factor_of = factor_of * jnp.repeat(draws, shape[axis_at] // shards_of).reshape([-1 if axis == axis_at else 1 for axis in range(len(shape))])
    return factor_of


def gaussian(stream_key, shape, spread, limit, cuts=(), kind=jnp.bfloat16):
    level = levels(stream_key, shape, cuts, -0.22, 0.18) if cuts else 1.0
    result = jax.random.normal(stream_key, shape, jnp.float32) * spread * level
    return jnp.minimum(jnp.maximum(result, -limit), limit).astype(kind)


def setup_inputs(seed: int = 0) -> dict:
    seeds = jax.random.split(jax.random.key(seed), 12)
    return {
        "tokens": gaussian(seeds[0], (TOKENS, D), 1.0, 6.0, ((0, 32),)),
        "norm_gains": jnp.clip(1.0 + 0.1 * jax.random.normal(seeds[1], (2, D), jnp.float32), 0.5, 1.5),
        "norm_biases": gaussian(seeds[2], (2, D), 0.2, 1.0, (), jnp.float32),
        "mix_weight": gaussian(seeds[3], (D, 3, D), D ** -0.5, 0.125, ((2, 8),)),
        "mix_bias": gaussian(seeds[4], (3, D), 0.3, 1.796875, ((1, 8),)),
        "out_weight": gaussian(seeds[5], (D, D), (D // 16) ** -0.5, 0.5, ((0, 8),)),
        "gate_up_weight": gaussian(seeds[6], (D, 2, FF), D ** -0.5, 0.125, ((2, 8),)),
        "down_weight": gaussian(seeds[7], (FF, D), FF ** -0.5, 0.078125, ((0, 8),)),
        "row_lengths": draw_row_lengths(jax.random.fold_in(seeds[11], 71), 0),
        "row_group": draw_row_group(jax.random.fold_in(seeds[11], 71), 0),
        "cotangent": gaussian(seeds[10], (TOKENS, D), 1.0, 6.0, ((0, 32),)),
    }


EPS = 1e-05
NEG = -1e+30
BASE = 10000.0
HIGH = lax.Precision.HIGHEST

@jax.custom_vjp
def low(v):
    return lax.optimization_barrier(v.astype(jnp.bfloat16)).astype(jnp.float32)

@jax.custom_vjp
def low_back(v):
    return v

def low_keep(v):
    return (low(v), None)

def low_pass(kept, grad):
    return (grad,)

def back_keep(v):
    return (v, None)

def back_low(kept, grad):
    return (low(grad),)
low.defvjp(low_keep, low_pass)
low_back.defvjp(back_keep, back_low)

def layer_norm(values, gain, bias):
    centered = values - lax.optimization_barrier(jnp.mean(values, axis=-1, keepdims=True))
    scale = lax.rsqrt(lax.optimization_barrier(jnp.mean(centered * centered, axis=-1, keepdims=True)) + EPS)
    return centered * scale * gain + bias

def rotate(values, where):
    half = ROT // 2
    freq = BASE ** (-jnp.arange(half, dtype=jnp.float32) / half)
    angle = where.astype(jnp.float32)[:, None] * freq[None, :]
    cosine = jnp.cos(angle)[:, None, :]
    sine = jnp.sin(angle)[:, None, :]
    first = values[..., :half]
    second = values[..., half:ROT]
    return jnp.concatenate([first * cosine - second * sine, second * cosine + first * sine, values[..., ROT:]], axis=-1)

def slot_rows(row_lengths, row_group, group, slots):
    order = jnp.arange(row_lengths.shape[0], dtype=jnp.int32)
    same = row_group == group
    earlier = (order[:, None] > order[None, :]) & same[None, :]
    begin = lax.optimization_barrier(jnp.sum(jnp.where(earlier, row_lengths[None, :], 0), axis=1))
    finish = begin + row_lengths
    inside = same[None, :] & (slots[:, None] >= begin[None, :]) & (slots[:, None] < finish[None, :])
    label = lax.optimization_barrier(jnp.sum(jnp.where(inside, order[None, :] + 1, 0), axis=1)) - 1
    offset = lax.optimization_barrier(jnp.sum(jnp.where(inside, slots[:, None] - begin[None, :], 0), axis=1))
    load = jnp.sum(jnp.where(same, row_lengths, 0))
    return (label, jnp.where(label < 0, slots - load, offset))

def attention(query, key, value, label):
    total = query.shape[0]
    scale = 1.0 / math.sqrt(HEAD_DIM)
    columns = jnp.arange(total, dtype=jnp.int32)

    @jax.checkpoint
    def one_block(index):
        start = index * QBLOCK
        part = lax.dynamic_slice_in_dim(query, start, QBLOCK, 0)
        rows = start + jnp.arange(QBLOCK, dtype=jnp.int32)
        label_rows = lax.dynamic_slice_in_dim(label, start, QBLOCK, 0)
        allowed = (label_rows[:, None] == label[None, :]) & (rows[:, None] >= columns[None, :])
        scores = low_back(jnp.einsum('qhe,khe->hqk', part, key, precision=HIGH) * scale)
        scores = jnp.where(allowed[None], scores, NEG)
        top = lax.optimization_barrier(jnp.max(scores, axis=-1, keepdims=True))
        weights = jnp.exp(scores - top)
        probs = low(weights / lax.optimization_barrier(jnp.sum(weights, axis=-1, keepdims=True)))
        return jnp.einsum('hqk,khe->qhe', probs, value, precision=HIGH)
    mixed = lax.map(one_block, jnp.arange(total // QBLOCK, dtype=jnp.int32))
    return mixed.reshape(query.shape)

def forward(inputs, gains, biases, mix_weight, mix_bias, out_weight, gate_up_weight, down_weight, label, position):
    total = inputs.shape[0]
    normed = low(layer_norm(inputs, gains[0], biases[0]))
    mixin = low_back(jnp.einsum('td,dcf->tcf', normed, mix_weight, precision=HIGH) + mix_bias)
    split = mixin.reshape(total, 3, D // HEAD_DIM, HEAD_DIM)
    query = low(low_back(rotate(split[:, 0], position)))
    key = low(low_back(rotate(split[:, 1], position)))
    value = low(low_back(split[:, 2]))
    attended = low(low_back(attention(query, key, value, label).reshape(total, D)))
    resid = inputs + low_back(jnp.dot(attended, out_weight, precision=HIGH))
    normed_two = low(layer_norm(resid, gains[1], biases[1]))
    gate_up = low_back(jnp.einsum('td,dcf->tcf', normed_two, gate_up_weight, precision=HIGH))
    hidden = low(jax.nn.silu(gate_up[:, 0]) * gate_up[:, 1])
    return resid + low_back(jnp.dot(hidden, down_weight, precision=HIGH))

def reference(tokens, norm_gains, norm_biases, mix_weight, mix_bias, out_weight, gate_up_weight, down_weight, row_lengths, row_group, cotangent):
    params = tuple((item.astype(jnp.float32) for item in (norm_gains, norm_biases, mix_weight, mix_bias, out_weight, gate_up_weight, down_weight)))
    slots = jnp.arange(CAP, dtype=jnp.int32)

    def one_group(totals, inputs):
        block, upstream, group = inputs
        label, position = slot_rows(row_lengths, row_group, group, slots)

        def local(values, *weights):
            return forward(values, *weights, label, position)
        output, pullback = jax.vjp(local, block.astype(jnp.float32), *params)
        mask = (label >= 0).astype(jnp.float32)[:, None]
        grads = pullback(upstream.astype(jnp.float32) * mask)
        totals = tuple((total + grad for total, grad in zip(totals, grads[1:])))
        return (totals, (output.astype(jnp.bfloat16), grads[0].astype(jnp.bfloat16)))
    zeros = tuple((jnp.zeros_like(item) for item in params))
    groups = jnp.arange(N_GRP, dtype=jnp.int32)
    totals, (outputs, inputs_grad) = lax.scan(one_group, zeros, (tokens.reshape(N_GRP, CAP, D), cotangent.reshape(N_GRP, CAP, D), groups))
    return (outputs.reshape(TOKENS, D), inputs_grad.reshape(TOKENS, D), totals[0], totals[1], totals[2], totals[3], totals[4], totals[5], totals[6])
```

```python
import functools
import math

import jax
import jax.numpy as jnp
from jax import lax
from jax.experimental import pallas as pl
from jax.experimental.pallas import tpu as pltpu
from jax.sharding import PartitionSpec as P

HEAD_DIM = 64
ROT = 16


EPS = 1e-05
NEG = -1e30
BASE = 10000.0


def layer_norm(values, gain, bias):
    centered = values - jnp.mean(values, axis=-1, keepdims=True)
    scale = lax.rsqrt(jnp.mean(centered * centered, axis=-1, keepdims=True) + EPS)
    unit = centered * scale
    return (unit * gain + bias, unit, scale)


def norm_back(incoming, unit, scale, gain):
    along = incoming * gain
    inner = jnp.mean(along, axis=-1, keepdims=True)
    cross = jnp.mean(along * unit, axis=-1, keepdims=True)
    return (
        scale * (along - inner - unit * cross),
        jnp.sum(incoming * unit, axis=0),
        jnp.sum(incoming, axis=0),
    )


def rotate(values, where, sign):
    half = ROT // 2
    freq = BASE ** (-jnp.arange(half, dtype=jnp.float32) / half)
    angle = where.astype(jnp.float32)[:, None] * freq[None, :]
    cosine = jnp.cos(angle)[:, None, :]
    sine = sign * jnp.sin(angle)[:, None, :]
    first = values[..., :half]
    second = values[..., half:ROT]
    return jnp.concatenate(
        [first * cosine - second * sine, second * cosine + first * sine, values[..., ROT:]], axis=-1
    )


def unrotate(lowered, where):
    wide = lowered.astype(jnp.float32)
    turned = jnp.stack(
        [rotate(wide[:, 0], where, -1.0), rotate(wide[:, 1], where, -1.0), wide[:, 2]], axis=1
    )
    return turned.reshape(lowered.shape[0], 3, -1).astype(jnp.bfloat16)


def slot_rows(row_lengths, row_group, group, slots):
    order = jnp.arange(row_lengths.shape[0], dtype=jnp.int32)
    same = row_group == group
    earlier = (order[:, None] > order[None, :]) & same[None, :]
    begin = jnp.sum(jnp.where(earlier, row_lengths[None, :], 0), axis=1)
    finish = begin + row_lengths
    inside = same[None, :] & (slots[:, None] >= begin[None, :]) & (slots[:, None] < finish[None, :])
    label = jnp.sum(jnp.where(inside, order[None, :] + 1, 0), axis=1) - 1
    offset = jnp.sum(jnp.where(inside, slots[:, None] - begin[None, :], 0), axis=1)
    load = jnp.sum(jnp.where(same, row_lengths, 0))
    return (label, jnp.where(label < 0, slots - load, offset))


def block_scores(query, key, label, start, block):
    part = lax.dynamic_slice_in_dim(query, start, block, 0)
    rows = start + jnp.arange(block, dtype=jnp.int32)
    columns = jnp.arange(label.shape[0], dtype=jnp.int32)
    label_rows = lax.dynamic_slice_in_dim(label, start, block, 0)
    allowed = (label_rows[:, None] == label[None, :]) & (rows[:, None] >= columns[None, :])
    scores = jnp.einsum("qhe,khe->hqk", part, key, preferred_element_type=jnp.float32) * (
        1.0 / math.sqrt(query.shape[-1])
    )
    return (part, jnp.where(allowed[None], scores, NEG))


def attend(query, key, value, label, block):

    def one_block(index):
        part, scores = block_scores(query, key, label, index * block, block)
        top = jnp.max(scores, axis=-1, keepdims=True)
        weights = jnp.exp(scores - top)
        totals = jnp.sum(weights, axis=-1, keepdims=True)
        probs = (weights / totals).astype(jnp.bfloat16)
        mixed = jnp.einsum("hqk,khe->qhe", probs, value, preferred_element_type=jnp.float32)
        return (mixed, top[..., 0] + jnp.log(totals[..., 0]))

    mixed, log_totals = lax.map(one_block, jnp.arange(query.shape[0] // block, dtype=jnp.int32))
    return (mixed.reshape(query.shape), log_totals)


def attend_back(query, key, value, label, log_totals, mixed_back, block):
    scale = 1.0 / math.sqrt(query.shape[-1])

    def one_block(carry, index):
        key_back, value_back = carry
        start = index * block
        part, scores = block_scores(query, key, label, start, block)
        back_part = lax.dynamic_slice_in_dim(mixed_back, start, block, 0)
        probs = jnp.exp(scores - log_totals[index][..., None])
        value_back = value_back + jnp.einsum(
            "hqk,qhe->khe",
            probs.astype(jnp.bfloat16),
            back_part,
            preferred_element_type=jnp.float32,
        )
        probs_back = jnp.einsum(
            "qhe,khe->hqk", back_part, value, preferred_element_type=jnp.float32
        )
        inner = jnp.sum(probs_back * probs, axis=-1, keepdims=True)
        score_back = (probs * (probs_back - inner)).astype(jnp.bfloat16)
        query_back = (
            jnp.einsum("hqk,khe->qhe", score_back, key, preferred_element_type=jnp.float32) * scale
        )
        key_back = (
            key_back
            + jnp.einsum("hqk,qhe->khe", score_back, part, preferred_element_type=jnp.float32)
            * scale
        )
        return ((key_back, value_back), query_back)

    empty = jnp.zeros(key.shape, jnp.float32)
    (key_back, value_back), query_back = lax.scan(
        one_block, (empty, empty), jnp.arange(query.shape[0] // block, dtype=jnp.int32)
    )
    return (query_back.reshape(query.shape), key_back, value_back)


def silu_parts(gate_up):
    gate = gate_up[:, 0]
    upper = gate_up[:, 1]
    sigma = jax.nn.sigmoid(gate)
    return (gate * sigma * upper, gate, upper, sigma)


def gate_back(hidden_back, gate, upper, sigma):
    gate_part = hidden_back * upper * sigma * (1.0 + gate * (1.0 - sigma))
    up_part = hidden_back * gate * sigma
    return jnp.stack([gate_part, up_part], axis=1).astype(jnp.bfloat16)


def gather_rows(values):
    return lax.all_gather(values, "seq", axis=0, tiled=True)


def summed_rows(product, left):
    return lax.psum_scatter(
        product(left).astype(jnp.bfloat16), "seq", scatter_dimension=0, tiled=True
    ).astype(jnp.float32)


def plain_device(
    tokens,
    norm_gains,
    norm_biases,
    mix_weight,
    mix_bias,
    out_weight,
    gate_up_weight,
    down_weight,
    row_lengths,
    row_group,
    cotangent,
):
    seq_count = lax.axis_size("seq")
    shard = lax.axis_index("seq")
    group = lax.axis_index("grp")
    slots_dev = tokens.shape[0]
    width = tokens.shape[1]
    group_slots = slots_dev * seq_count
    block = min(512, group_slots)
    local_width = width // seq_count
    local_heads = local_width // HEAD_DIM
    mine = shard * slots_dev + jnp.arange(slots_dev, dtype=jnp.int32)
    label_mine, place_mine = slot_rows(row_lengths, row_group, group, mine)
    label_all, place_all = slot_rows(
        row_lengths, row_group, group, jnp.arange(group_slots, dtype=jnp.int32)
    )
    inputs = tokens.astype(jnp.float32)
    upstream = cotangent.astype(jnp.float32) * (label_mine >= 0).astype(jnp.float32)[:, None]
    upstream_low = upstream.astype(jnp.bfloat16)
    normed, unit_one, scale_one = layer_norm(inputs, norm_gains[0], norm_biases[0])
    normed_all = gather_rows(normed.astype(jnp.bfloat16))
    up_four = lax.all_gather(upstream_low, ("grp", "seq"), axis=0, tiled=True)
    upstream_all = lax.dynamic_slice_in_dim(up_four, group * group_slots, group_slots, 0)
    mixin = jnp.einsum(
        "td,dcf->tcf", normed_all, mix_weight, preferred_element_type=jnp.float32
    ) + mix_bias.astype(jnp.float32)
    heads_in = mixin.reshape(group_slots, 3, local_heads, HEAD_DIM)
    query = rotate(heads_in[:, 0], place_all, 1.0).astype(jnp.bfloat16)
    key = rotate(heads_in[:, 1], place_all, 1.0).astype(jnp.bfloat16)
    value = heads_in[:, 2].astype(jnp.bfloat16)
    mixed, log_totals = attend(query, key, value, label_all, block)
    attended = mixed.reshape(group_slots, local_width).astype(jnp.bfloat16)

    def out_product(part):
        return jnp.dot(part, out_weight, preferred_element_type=jnp.float32)

    resid = inputs + summed_rows(out_product, attended)
    normed_two, unit_two, scale_two = layer_norm(resid, norm_gains[1], norm_biases[1])
    normed_two_low = normed_two.astype(jnp.bfloat16)
    normed_two_all = gather_rows(normed_two_low)
    two_four = lax.all_gather(normed_two_low, ("grp", "seq"), axis=0, tiled=True)

    def up_to_back(two, up):
        gate_up = jnp.einsum("td,dcf->tcf", two, gate_up_weight, preferred_element_type=jnp.float32)
        hidden, gate, upper, sigma = silu_parts(gate_up)
        hidden_back = jnp.einsum("td,fd->tf", up, down_weight, preferred_element_type=jnp.float32)
        return hidden.astype(jnp.bfloat16), gate_back(hidden_back, gate, upper, sigma)

    hidden_low, gate_up_back = up_to_back(normed_two_all, upstream_all)

    def down_product(part):
        return jnp.dot(part, down_weight, preferred_element_type=jnp.float32)

    layer_out = resid + summed_rows(down_product, hidden_low)

    def gate_up_product(part):
        return jnp.einsum("tcf,dcf->td", part, gate_up_weight, preferred_element_type=jnp.float32)

    normed_two_back = summed_rows(gate_up_product, gate_up_back)
    hidden_four, back_four = up_to_back(two_four, up_four)
    down_grad = jnp.einsum("tf,td->fd", hidden_four, up_four, preferred_element_type=jnp.float32)
    gate_up_grad = jnp.einsum(
        "td,tcf->dcf", two_four, back_four, preferred_element_type=jnp.float32
    )
    resid_part, gain_two, bias_two = norm_back(normed_two_back, unit_two, scale_two, norm_gains[1])
    resid_back = upstream + resid_part
    branch_all = gather_rows(resid_back.astype(jnp.bfloat16))
    out_term = jnp.einsum("te,td->ed", attended, branch_all, preferred_element_type=jnp.float32)
    out_grad = lax.psum(out_term.astype(jnp.bfloat16), "grp").astype(jnp.float32)
    attended_back = jnp.einsum(
        "td,ed->te", branch_all, out_weight, preferred_element_type=jnp.float32
    ).astype(jnp.bfloat16)
    heads_back = attended_back.reshape(group_slots, local_heads, HEAD_DIM)
    query_back, key_back, value_back = attend_back(
        query, key, value, label_all, log_totals, heads_back, block
    )
    lowered = jnp.stack([query_back, key_back, value_back], axis=1).astype(jnp.bfloat16)
    mixin_back = unrotate(lowered, place_all)
    mix_term = jnp.einsum("td,tcf->dcf", normed_all, mixin_back, preferred_element_type=jnp.float32)
    mix_grad = lax.psum(mix_term.astype(jnp.bfloat16), "grp").astype(jnp.float32)
    bias_term = jnp.sum(mixin_back, axis=0, dtype=jnp.float32)
    mix_bias_grad = lax.psum(bias_term, "grp")

    def mix_product(part):
        return jnp.einsum("tcf,dcf->td", part, mix_weight, preferred_element_type=jnp.float32)

    normed_back = summed_rows(mix_product, mixin_back)
    tokens_part, gain_one, bias_one = norm_back(normed_back, unit_one, scale_one, norm_gains[0])
    tokens_grad = (resid_back + tokens_part).astype(jnp.bfloat16)
    gains_grad, biases_grad = lax.psum(
        (jnp.stack([gain_one, gain_two]), jnp.stack([bias_one, bias_two])), ("grp", "seq")
    )
    return (
        layer_out.astype(jnp.bfloat16),
        tokens_grad,
        gains_grad,
        biases_grad,
        mix_grad,
        mix_bias_grad,
        out_grad,
        gate_up_grad,
        down_grad,
    )


MESH_ID = pl.DeviceIdType.MESH
N_RS = 10
N_AG = 13


class Ring:
    def __init__(self):
        self.group = lax.axis_index("grp")
        self.me = lax.axis_index("seq")
        core = self.me % 2
        x = (self.me // 2) % 2
        y = self.me // 4
        self.flip = 1 - 2 * core
        self.twin = self.me + self.flip
        self.xn = self.me + 2 - 4 * x
        self.yn = self.me + 4 - 8 * y
        self.dn = self.xn + 4 - 8 * y

    def dev(self, seq):
        return (self.group, seq)

    def barrier(self, extra=()):
        sem = pltpu.get_barrier_semaphore()
        peers = [self.dev(self.twin), self.dev(self.xn), self.dev(self.yn)] + list(extra)
        for peer in peers:
            pl.semaphore_signal(sem, inc=1, device_id=peer, device_id_type=MESH_ID)
        pl.semaphore_wait(sem, len(peers))

    def copy(self, src, dst, send, recv, kind, seq):
        return pltpu.make_async_remote_copy(
            src_ref=src,
            dst_ref=dst,
            send_sem=send.at[kind],
            recv_sem=recv.at[kind],
            device_id=self.dev(seq),
            device_id_type=MESH_ID,
        )


def gather_steps(ring, own, out, send, recv, local):
    rows = own.shape[0]
    half = rows // 2

    def at(block, part=None):
        if part is None:
            return out.at[pl.ds(pl.multiple_of(block * rows, rows), rows), :]
        return out.at[pl.ds(pl.multiple_of(block * rows + part * half, half), half), :]

    def go(src, dst, kind, seq):
        copy = ring.copy(src, dst, send, recv, kind, seq)
        copy.start()
        return copy

    keep = pltpu.make_async_copy(own, at(ring.me), local)
    keep.start()
    lo, hi = own.at[pl.ds(0, half), :], own.at[pl.ds(half, half), :]
    x0 = go(lo, at(ring.me, 0), 0, ring.xn)
    y1 = go(hi, at(ring.me, 1), 1, ring.yn)
    x1 = go(hi, at(ring.me, 1), 2, ring.xn)
    y0 = go(lo, at(ring.me, 0), 3, ring.yn)
    t0 = go(own, at(ring.me), 4, ring.twin)
    x0.wait_recv()
    f0 = go(at(ring.xn, 0), at(ring.xn, 0), 5, ring.yn)
    t1 = go(at(ring.xn, 0), at(ring.xn, 0), 6, ring.twin)
    y1.wait_recv()
    f1 = go(at(ring.yn, 1), at(ring.yn, 1), 7, ring.xn)
    t2 = go(at(ring.yn, 1), at(ring.yn, 1), 8, ring.twin)
    x1.wait_recv()
    t3 = go(at(ring.xn, 1), at(ring.xn, 1), 9, ring.twin)
    y0.wait_recv()
    t4 = go(at(ring.yn, 0), at(ring.yn, 0), 10, ring.twin)
    f0.wait_recv()
    t5 = go(at(ring.dn, 0), at(ring.dn, 0), 11, ring.twin)
    f1.wait_recv()
    t6 = go(at(ring.dn, 1), at(ring.dn, 1), 12, ring.twin)
    keep.wait()
    for copy in (t0, t1, t2, t3, t4, t5, t6):
        copy.wait_recv()
    for copy in (x0, y1, x1, y0, f0, f1, t0, t1, t2, t3, t4, t5, t6):
        copy.wait_send()


def scatter_steps(ring, part, total, own, pair, rx, ry, fx, fy, stage, send, recv, local):
    rows, width = total.shape
    half = width // 2
    wide = jnp.float32
    order = [ring.dn, ring.xn, ring.yn, ring.me]

    def block(index):
        return part.at[pl.ds(pl.multiple_of(index * rows, rows), rows), :]

    pairs, keeps = [], []
    for slot, index in enumerate(order):
        copy = ring.copy(block(index + ring.flip), pair.at[slot], send, recv, slot, ring.twin)
        copy.start()
        pairs.append(copy)
        keep = pltpu.make_async_copy(block(index), own.at[slot], local.at[slot])
        keep.start()
        keeps.append(keep)

    def go(src, dst, kind, seq):
        copy = ring.copy(src, dst, send, recv, kind, seq)
        copy.start()
        return copy

    def added(slot):
        keeps[slot].wait()
        pairs[slot].wait_recv()
        return own[slot].astype(wide) + pair[slot].astype(wide)

    lo, hi = pl.ds(0, half), pl.ds(half, half)
    own[0] = added(0).astype(own.dtype)
    x0 = go(own.at[0, :, lo], rx.at[0], 4, ring.xn)
    y0 = go(own.at[0, :, hi], ry.at[0], 5, ring.yn)
    own[1] = added(1).astype(own.dtype)
    x1 = go(own.at[1, :, lo], rx.at[1], 6, ring.xn)
    own[2] = added(2).astype(own.dtype)
    y1 = go(own.at[2, :, hi], ry.at[1], 7, ring.yn)
    total[...] = added(3)
    x0.wait_recv()
    stage[0] = (own[2, :, lo].astype(wide) + rx[0].astype(wide)).astype(own.dtype)
    gy = go(stage.at[0], fy, 8, ring.yn)
    y0.wait_recv()
    stage[1] = (own[1, :, hi].astype(wide) + ry[0].astype(wide)).astype(own.dtype)
    gx = go(stage.at[1], fx, 9, ring.xn)
    x1.wait_recv()
    total[:, lo] += rx[1].astype(wide)
    y1.wait_recv()
    total[:, hi] += ry[1].astype(wide)
    gy.wait_recv()
    total[:, lo] += fy[...].astype(wide)
    gx.wait_recv()
    total[:, hi] += fx[...].astype(wide)
    for copy in pairs + [x0, y0, x1, y1, gy, gx]:
        copy.wait_send()


def scatter_scratch(rows, width):
    low = jnp.bfloat16
    half = width // 2
    return [
        pltpu.VMEM((rows, width), jnp.float32),
        pltpu.VMEM((4, rows, width), low),
        pltpu.VMEM((4, rows, width), low),
        pltpu.VMEM((2, rows, half), low),
        pltpu.VMEM((2, rows, half), low),
        pltpu.VMEM((rows, half), low),
        pltpu.VMEM((rows, half), low),
        pltpu.VMEM((2, rows, half), low),
        pltpu.SemaphoreType.DMA((N_RS,)),
        pltpu.SemaphoreType.DMA((N_RS,)),
        pltpu.SemaphoreType.DMA((4,)),
    ]


def gather_scratch(rows, width):
    return [
        pltpu.VMEM((rows, width), jnp.bfloat16),
        pltpu.SemaphoreType.DMA((N_AG,)),
        pltpu.SemaphoreType.DMA((N_AG,)),
        pltpu.SemaphoreType.DMA,
    ]


def unit_of(values):
    centered = values - jnp.mean(values, axis=-1, keepdims=True)
    scale = lax.rsqrt(jnp.mean(centered * centered, axis=-1, keepdims=True) + EPS)
    return centered * scale, scale


def back_of(incoming, unit, scale, gain):
    along = incoming * gain
    inner = jnp.mean(along, axis=-1, keepdims=True)
    cross = jnp.mean(along * unit, axis=-1, keepdims=True)
    return scale * (along - inner - unit * cross)


def first_kernel(tokens, gains, biases, normed_all, own, send, recv, local):
    ring = Ring()
    unit, _ = unit_of(tokens[...].astype(jnp.float32))
    own[...] = (unit * gains[0:1] + biases[0:1]).astype(own.dtype)
    ring.barrier()
    gather_steps(ring, own, normed_all, send, recv, local)


def second_kernel(part, tokens, gains, biases, resid, two_all, *scratch):
    rs, ag = scratch[:11], scratch[11:]
    ring = Ring()
    ring.barrier()
    scatter_steps(ring, part, *rs)
    total, own = rs[0], ag[0]
    resid[...] = total[...] + tokens[...].astype(jnp.float32)
    unit, _ = unit_of(resid[...])
    own[...] = (unit * gains[1:2] + biases[1:2]).astype(own.dtype)
    gather_steps(ring, own, two_all, *ag[1:])


def third_kernel(part, resid, upstream, gains, resid_back, branch_all, sums, *scratch):
    rs, ag = scratch[:11], scratch[11:]
    ring = Ring()
    ring.barrier()
    scatter_steps(ring, part, *rs)
    total, own = rs[0], ag[0]
    unit, scale = unit_of(resid[...])
    incoming = total[...]
    resid_back[...] = upstream[...].astype(jnp.float32) + back_of(incoming, unit, scale, gains[1:2])
    own[...] = resid_back[...].astype(own.dtype)
    sums[0:1] = jnp.sum(incoming * unit, axis=0, keepdims=True)
    sums[1:2] = jnp.sum(incoming, axis=0, keepdims=True)
    gather_steps(ring, own, branch_all, *ag[1:])


def fourth_kernel(part, tokens, resid_back, gains, sums, tokens_grad, four, *scratch):
    rs, (inbox, mail, send, recv) = scratch[:11], scratch[11:]
    ring = Ring()
    groups = lax.axis_size("grp")
    others = [(lax.rem(ring.group + k, groups), ring.me) for k in range(1, groups)]
    ring.barrier(others)
    scatter_steps(ring, part, *rs)
    unit, scale = unit_of(tokens[...].astype(jnp.float32))
    incoming = rs[0][...]
    tokens_grad[...] = (resid_back[...] + back_of(incoming, unit, scale, gains[0:1])).astype(
        tokens_grad.dtype
    )
    four[0:1] = jnp.sum(incoming * unit, axis=0, keepdims=True)
    four[1:2] = sums[0:1]
    four[2:3] = jnp.sum(incoming, axis=0, keepdims=True)
    four[3:4] = sums[1:2]
    for stage, peer in enumerate((ring.twin, ring.xn, ring.yn)):
        mail[stage] = four[...]
        copy = ring.copy(mail.at[stage], inbox.at[stage], send, recv, stage, peer)
        copy.start()
        copy.wait_recv()
        four[...] += inbox[stage]
        copy.wait_send()
    mail[3] = four[...]
    copies = []
    for k, peer in enumerate(others):
        copy = pltpu.make_async_remote_copy(
            src_ref=mail.at[3],
            dst_ref=inbox.at[3 + k],
            send_sem=send.at[3 + k],
            recv_sem=recv.at[3 + k],
            device_id=peer,
            device_id_type=MESH_ID,
        )
        copy.start()
        copies.append(copy)
    for copy in copies:
        copy.wait_recv()
    total = jnp.zeros(four.shape, jnp.float32)
    for group in range(groups):
        term = mail[3]
        for k in range(1, groups):
            source = lax.rem(ring.group + groups - k, groups)
            term = jnp.where(source == group, inbox[2 + k], term)
        total = total + term
    four[...] = total
    for copy in copies:
        copy.wait_send()


VM = pl.BlockSpec(memory_space=pltpu.VMEM)
ANY = pl.BlockSpec(memory_space=pl.ANY)


def call(kernel, number, ins, outs, scratch, cost=20_000_000):
    return pl.pallas_call(
        kernel,
        out_shape=tuple(jax.ShapeDtypeStruct(*shape) for shape, _ in outs),
        in_specs=[spec for _, spec in ins],
        out_specs=tuple(spec for _, spec in outs),
        scratch_shapes=scratch,
        compiler_params=pltpu.CompilerParams(
            collective_id=number, has_side_effects=True, vmem_limit_bytes=40 << 20
        ),
        cost_estimate=pl.CostEstimate(flops=0, bytes_accessed=cost, transcendentals=0),
    )(*[value for value, _ in ins])


def first(tokens, gains, biases, count):
    rows, width = tokens.shape
    low = jnp.bfloat16
    return call(
        first_kernel,
        1,
        [(tokens, VM), (gains, VM), (biases, VM)],
        [(((rows * count, width), low), ANY)],
        gather_scratch(rows, width),
    )[0]


def second(part, tokens, gains, biases, count):
    rows, width = tokens.shape
    return call(
        second_kernel,
        2,
        [(part, ANY), (tokens, VM), (gains, VM), (biases, VM)],
        [(((rows, width), jnp.float32), VM), (((rows * count, width), jnp.bfloat16), ANY)],
        scatter_scratch(rows, width) + gather_scratch(rows, width),
    )


def third(part, resid, upstream, gains, count):
    rows, width = resid.shape
    return call(
        third_kernel,
        3,
        [(part, ANY), (resid, VM), (upstream, VM), (gains, VM)],
        [
            (((rows, width), jnp.float32), VM),
            (((rows * count, width), jnp.bfloat16), ANY),
            (((2, width), jnp.float32), VM),
        ],
        scatter_scratch(rows, width) + gather_scratch(rows, width),
    )


def fourth(part, tokens, resid_back, gains, sums):
    rows, width = tokens.shape
    groups = lax.axis_size("grp")
    return call(
        fourth_kernel,
        4,
        [(part, ANY), (tokens, VM), (resid_back, VM), (gains, VM), (sums, VM)],
        [(((rows, width), jnp.bfloat16), VM), (((4, width), jnp.float32), VM)],
        scatter_scratch(rows, width)
        + [
            pltpu.VMEM((2 + groups, 4, width), jnp.float32),
            pltpu.VMEM((4, 4, width), jnp.float32),
            pltpu.SemaphoreType.DMA((2 + groups,)),
            pltpu.SemaphoreType.DMA((2 + groups,)),
        ],
    )


TILE = 256
WIDE = jnp.float32
LOW = jnp.bfloat16
NT = (((1,), (1,)), ((), ()))
TN = (((0,), (0,)), ((), ()))


def mm(a, b, dims=(((1,), (0,)), ((), ()))):
    return lax.dot_general(a, b, dims, preferred_element_type=WIDE)


def head_lanes(shape, head):
    return lax.broadcasted_iota(jnp.int32, shape, 1) // HEAD_DIM == head


def turn(u, tables, rows, sign):
    cosine, below, above = (
        jnp.concatenate([tables[i, rows, :]] * (u.shape[1] // 128), axis=1) for i in range(3)
    )
    side = pltpu.roll(u, 8, 1) * below + pltpu.roll(u, u.shape[1] - 8, 1) * above
    return u * cosine + side if sign > 0 else u * cosine - side


def load(pairs, sems):
    copies = []
    for i, (src, dst) in enumerate(pairs):
        copy = pltpu.make_async_copy(src, dst, sems.at[i])
        copy.start()
        copies.append(copy)
    return copies


def attend_kernel(
    normed_all, weight, out_weight, bias, tables, lab_col, lab_row,
    query, key, value, attended, lse, part,
    normed, w, mask, stats, stage, sems, outs,
):
    total, width = query.shape
    tiles = total // TILE
    loads = load(
        [(normed_all.at[pl.ds(i * TILE, TILE), :], normed.at[pl.ds(i * TILE, TILE), :]) for i in range(tiles)]
        + [(weight, w)],
        sems,
    )
    loads[-1].wait()
    for i in range(tiles):
        rows = pl.ds(i * TILE, TILE)
        loads[i].wait()
        x = normed[rows, :]
        u = mm(x, w[0]) + bias[0:1]
        query[rows, :] = (turn(u, tables, rows, 1).astype(LOW).astype(WIDE) * (1.0 / 8)).astype(LOW)
        u = mm(x, w[1]) + bias[1:2]
        key[rows, :] = turn(u, tables, rows, 1).astype(LOW)
        value[rows, :] = (mm(x, w[2]) + bias[2:3]).astype(LOW)
    copies = []
    for i in range(tiles):
        rows = pl.ds(i * TILE, TILE)
        span = (i + 1) * TILE
        q_at = i * TILE + lax.broadcasted_iota(jnp.int32, (TILE, span), 0)
        k_at = lax.broadcasted_iota(jnp.int32, (TILE, span), 1)
        allowed = (lab_col[rows, :] == lab_row[:, :span]) & (q_at >= k_at)
        mask[:, :span] = jnp.where(allowed, 0.0, NEG)
        q = query[rows, :]

        def one_head(head, carry):
            mixed, logs = carry
            mine = head_lanes(q.shape, head)
            s = mm(jnp.where(mine, q, jnp.zeros_like(q)), key[:span, :], NT) + mask[:, :span]
            top = jnp.max(s, axis=1, keepdims=True)
            p = jnp.exp(s - top)
            norm = jnp.sum(p, axis=1, keepdims=True)
            o = mm(p.astype(LOW), value[:span, :]) / norm
            mixed = jnp.where(mine, o, mixed)
            lane = lax.broadcasted_iota(jnp.int32, logs.shape, 1)
            logs = jnp.where(lane == head, top + jnp.log(norm), logs)
            return mixed, logs

        mixed, logs = lax.fori_loop(
            0, width // HEAD_DIM, one_head,
            (jnp.zeros((TILE, width), WIDE), jnp.zeros((TILE, 128), WIDE)),
        )
        low = mixed.astype(LOW)
        attended[rows, :] = low
        stats[rows, :] = logs
        stage[i] = mm(low, out_weight[...]).astype(LOW)
        copy = pltpu.make_async_copy(stage.at[i], part.at[rows, :], outs.at[i])
        copy.start()
        copies.append(copy)
    lse[...] = jnp.transpose(stats[...])[:8, :]
    for copy in copies:
        copy.wait()


def attend_heads(normed_all, weight, out_weight, bias, tables, lab_col, lab_row):
    total, width = normed_all.shape
    local = out_weight.shape[0]
    tiles = total // TILE
    slab = jax.ShapeDtypeStruct((total, local), LOW)
    return pl.pallas_call(
        attend_kernel,
        out_shape=(
            slab, slab, slab, slab,
            jax.ShapeDtypeStruct((8, total), WIDE),
            jax.ShapeDtypeStruct((total, width), LOW),
        ),
        in_specs=[ANY, ANY, VM, VM, VM, VM, VM],
        out_specs=(VM, VM, VM, VM, VM, ANY),
        scratch_shapes=[
            pltpu.VMEM((total, width), LOW),
            pltpu.VMEM((3, width, local), LOW),
            pltpu.VMEM((TILE, total), WIDE),
            pltpu.VMEM((total, 128), WIDE),
            pltpu.VMEM((tiles, TILE, width), LOW),
            pltpu.SemaphoreType.DMA((tiles + 1,)),
            pltpu.SemaphoreType.DMA((tiles,)),
        ],
        compiler_params=pltpu.CompilerParams(vmem_limit_bytes=48 << 20),
        cost_estimate=pl.CostEstimate(flops=7 << 30, bytes_accessed=16 << 20, transcendentals=4 << 20),
    )(normed_all, weight, out_weight, bias, tables, lab_col, lab_row)


def attend_back_kernel(
    branch_all, normed_all, weight, out_weight, tables, lab_col, lab_row,
    query, key, value, attended, lse,
    part, mix_term, out_term, bias_term,
    branch, normed, w, mask, inner, heads_back, query_back, key_back, value_back, mixin, stage, mixes,
    sems, outs,
):
    total, width = query.shape
    tiles = total // TILE
    heads = width // HEAD_DIM
    loads = load(
        [(branch_all.at[pl.ds(i * TILE, TILE), :], branch.at[pl.ds(i * TILE, TILE), :]) for i in range(tiles)]
        + [(normed_all, normed), (weight, w)],
        sems,
    )
    head_of = lax.broadcasted_iota(jnp.int32, (8, width), 1) // HEAD_DIM
    pick = (head_of == lax.broadcasted_iota(jnp.int32, (8, width), 0)).astype(LOW)
    for i in range(tiles):
        rows = pl.ds(i * TILE, TILE)
        loads[i].wait()
        low = mm(branch[rows, :], out_weight[...], NT).astype(LOW)
        heads_back[rows, :] = low
        prod = low.astype(WIDE) * attended[rows, :].astype(WIDE)
        high = prod.astype(LOW)
        rest = (prod - high.astype(WIDE)).astype(LOW)
        inner[:, rows] = mm(pick, high, NT) + mm(pick, rest, NT)
    out_term[...] = mm(attended[...], branch[...], TN).astype(LOW)
    key_back[...] = jnp.zeros_like(key_back)
    value_back[...] = jnp.zeros_like(value_back)
    for i in range(tiles):
        rows = pl.ds(i * TILE, TILE)
        span = (i + 1) * TILE
        k_at = lax.broadcasted_iota(jnp.int32, (span, TILE), 0)
        q_at = i * TILE + lax.broadcasted_iota(jnp.int32, (span, TILE), 1)
        allowed = (lab_col[:span, :] == lab_row[:, rows]) & (q_at >= k_at)
        mask[:span, :] = jnp.where(allowed, 0.0, NEG)
        q = query[rows, :]
        d_out = heads_back[rows, :]

        def one_head(head, q_back):
            mine = head_lanes(q.shape, head)
            q_h = jnp.where(mine, q, jnp.zeros_like(q))
            d_h = jnp.where(mine, d_out, jnp.zeros_like(q))
            k = key[:span, :]
            k_h = jnp.where(head_lanes(k.shape, head), k, jnp.zeros_like(k))
            p = jnp.exp(mm(k, q_h, NT) + mask[:span, :] - lse[pl.ds(head, 1), rows])
            d_p = mm(value[:span, :], d_h, NT)
            d_s = (p * (d_p - inner[pl.ds(head, 1), rows])).astype(LOW)
            value_back[:span, :] += mm(p.astype(LOW), d_h)
            key_back[:span, :] += mm(d_s, q_h)
            return q_back + mm(d_s, k_h, TN)

        query_back[rows, :] = lax.fori_loop(0, heads, one_head, jnp.zeros((TILE, width), WIDE))
    loads[-1].wait()
    loads[-2].wait()
    copies = []
    sums = [jnp.zeros((1, width), WIDE)] * 3
    for i in range(tiles):
        rows = pl.ds(i * TILE, TILE)
        q_b = (query_back[rows, :] * (1.0 / 8)).astype(LOW).astype(WIDE)
        k_b = key_back[rows, :].astype(LOW).astype(WIDE)
        trio = [
            turn(q_b, tables, rows, -1).astype(LOW),
            turn(k_b, tables, rows, -1).astype(LOW),
            value_back[rows, :].astype(LOW),
        ]
        product = jnp.zeros((TILE, normed.shape[1]), WIDE)
        for c, item in enumerate(trio):
            mixin[c, rows, :] = item
            sums[c] = sums[c] + jnp.sum(item.astype(WIDE), axis=0, keepdims=True)
            product = product + mm(item, w[c], NT)
        stage[i] = product.astype(LOW)
        copy = pltpu.make_async_copy(stage.at[i], part.at[rows, :], outs.at[i])
        copy.start()
        copies.append(copy)
    for c in range(3):
        bias_term[c : c + 1, :] = sums[c]
        mixes[c] = mm(normed[...], mixin[c], TN).astype(LOW)
        copy = pltpu.make_async_copy(mixes.at[c], mix_term.at[c], outs.at[tiles + c])
        copy.start()
        copies.append(copy)
    for copy in copies:
        copy.wait()


def attend_heads_back(branch_all, normed_all, weight, out_weight, tables, lab_col, lab_row, saved):
    total, width = normed_all.shape
    local = out_weight.shape[0]
    tiles = total // TILE
    return pl.pallas_call(
        attend_back_kernel,
        out_shape=(
            jax.ShapeDtypeStruct((total, width), LOW),
            jax.ShapeDtypeStruct((3, width, local), LOW),
            jax.ShapeDtypeStruct((local, width), LOW),
            jax.ShapeDtypeStruct((3, local), WIDE),
        ),
        in_specs=[ANY, ANY, ANY] + [VM] * 9,
        out_specs=(ANY, ANY, VM, VM),
        scratch_shapes=[
            pltpu.VMEM((total, width), LOW),
            pltpu.VMEM((total, width), LOW),
            pltpu.VMEM((3, width, local), LOW),
            pltpu.VMEM((total, TILE), WIDE),
            pltpu.VMEM((8, total), WIDE),
            pltpu.VMEM((total, local), LOW),
            pltpu.VMEM((total, local), WIDE),
            pltpu.VMEM((total, local), WIDE),
            pltpu.VMEM((total, local), WIDE),
            pltpu.VMEM((3, total, local), LOW),
            pltpu.VMEM((tiles, TILE, width), LOW),
            pltpu.VMEM((3, width, local), LOW),
            pltpu.SemaphoreType.DMA((tiles + 2,)),
            pltpu.SemaphoreType.DMA((tiles + 3,)),
        ],
        compiler_params=pltpu.CompilerParams(vmem_limit_bytes=60 << 20),
        cost_estimate=pl.CostEstimate(flops=16 << 30, bytes_accessed=30 << 20, transcendentals=4 << 20),
    )(branch_all, normed_all, weight, out_weight, tables, lab_col, lab_row, *saved)


def units(gate, upper, hidden_back):
    sigma = jax.nn.sigmoid(gate)
    silu = gate * sigma
    return (
        (silu * upper).astype(LOW),
        (hidden_back * upper * sigma * (1.0 + gate * (1.0 - sigma))).astype(LOW),
        (hidden_back * silu).astype(LOW),
    )


def forward_units(two, up, wide, down):
    return units(mm(wide[0], two, NT), mm(wide[1], two, NT), mm(down[...], up, NT))


def feed_kernel(two_all, up_all, wide_hbm, down_hbm, back_part, down_part, saved,
                two, up, wide, down, kept, stage, sems, outs):
    total = two_all.shape[0]
    tiles = total // TILE
    pairs = [(wide_hbm, wide), (down_hbm, down)]
    for i in range(tiles):
        rows = pl.ds(i * TILE, TILE)
        pairs += [(two_all.at[rows, :], two.at[rows, :]), (up_all.at[rows, :], up.at[rows, :])]
    loads = load(pairs, sems)
    loads[0].wait()
    loads[1].wait()
    copies = []
    for i in range(tiles):
        rows = pl.ds(i * TILE, TILE)
        loads[2 + 2 * i].wait()
        loads[3 + 2 * i].wait()
        trio = forward_units(two[rows, :], up[rows, :], wide, down)
        for c in range(3):
            kept[c, :, rows] = trio[c]
        stage[0, rows, :] = (mm(trio[1], wide[0], TN) + mm(trio[2], wide[1], TN)).astype(LOW)
        copy = pltpu.make_async_copy(stage.at[0, rows, :], back_part.at[rows, :], outs.at[2 * i])
        copy.start()
        copies.append(copy)
        stage[1, rows, :] = mm(trio[0], down[...], TN).astype(LOW)
        copy = pltpu.make_async_copy(stage.at[1, rows, :], down_part.at[rows, :], outs.at[2 * i + 1])
        copy.start()
        copies.append(copy)
    copy = pltpu.make_async_copy(kept, saved, outs.at[2 * tiles])
    copy.start()
    copy.wait()
    for copy in copies:
        copy.wait()


def feed(two_all, up_all, wide, down):
    total, width = two_all.shape
    units_local = down.shape[0]
    tiles = total // TILE
    part = jax.ShapeDtypeStruct((total, width), LOW)
    return pl.pallas_call(
        feed_kernel,
        out_shape=(part, part, jax.ShapeDtypeStruct((3, units_local, total), LOW)),
        in_specs=[ANY] * 4,
        out_specs=(ANY, ANY, ANY),
        scratch_shapes=[
            pltpu.VMEM((total, width), LOW),
            pltpu.VMEM((total, width), LOW),
            pltpu.VMEM((2, units_local, width), LOW),
            pltpu.VMEM((units_local, width), LOW),
            pltpu.VMEM((3, units_local, total), LOW),
            pltpu.VMEM((2, total, width), LOW),
            pltpu.SemaphoreType.DMA((2 + 2 * tiles,)),
            pltpu.SemaphoreType.DMA((1 + 2 * tiles,)),
        ],
        compiler_params=pltpu.CompilerParams(vmem_limit_bytes=56 << 20),
        cost_estimate=pl.CostEstimate(flops=18 << 30, bytes_accessed=40 << 20, transcendentals=1 << 20),
    )(two_all, up_all, wide, down)


BIG = 512


def grads_kernel(two_all, up_all, saved, two_four, up_four, wide_hbm, down_hbm, wide_grad, down_grad,
                 two, up, wide, down, kept, acc, sems, outs):
    total = two_all.shape[0]
    groups = two_four.shape[0] // total
    group = lax.axis_index("grp")
    per = total // BIG
    weights = load([(wide_hbm, wide), (down_hbm, down)], sems.at[4])
    keep = pltpu.make_async_copy(saved, kept, sems.at[4, 2])
    keep.start()

    def fetch(source_two, source_up, start, slot):
        return [
            pltpu.make_async_copy(source_two.at[pl.ds(pl.multiple_of(start, BIG), BIG), :], two.at[slot], sems.at[slot, 0]),
            pltpu.make_async_copy(source_up.at[pl.ds(pl.multiple_of(start, BIG), BIG), :], up.at[slot], sems.at[slot, 1]),
        ]

    def other_start(step):
        index = lax.rem(group + 1 + step // per, groups)
        return index * total + lax.rem(step, per) * BIG

    for copy in fetch(two_all, up_all, 0, 0):
        copy.start()
    keep.wait()
    acc[...] = jnp.zeros_like(acc)

    def add(slot, trio):
        acc[2] += mm(trio[0], up[slot])
        acc[0] += mm(trio[1], two[slot])
        acc[1] += mm(trio[2], two[slot])

    for i in range(per):
        slot = i % 2
        if i + 1 < per:
            nxt = fetch(two_all, up_all, (i + 1) * BIG, 1 - slot)
        else:
            nxt = fetch(two_four, up_four, other_start(0), 1 - slot)
        for copy in nxt:
            copy.start()
        for copy in fetch(two_all, up_all, 0, slot):
            copy.wait()
        add(slot, [kept[c, :, pl.ds(i * BIG, BIG)] for c in range(3)])
    for copy in weights:
        copy.wait()
    steps = (groups - 1) * per

    def body(step, carry):
        slot = lax.rem(step + per, 2)
        for copy in fetch(two_four, up_four, 0, slot):
            copy.wait()

        @pl.when(step + 1 < steps)
        def _():
            for copy in fetch(two_four, up_four, other_start(step + 1), 1 - slot):
                copy.start()

        add(slot, forward_units(two[slot], up[slot], wide, down))
        return carry

    lax.fori_loop(0, steps, body, 0)
    copies = load([(acc.at[pl.ds(0, 2)], wide_grad), (acc.at[2], down_grad)], outs)
    for copy in copies:
        copy.wait()


def grads(two_all, up_all, saved, two_four, up_four, wide, down):
    total, width = two_all.shape
    local = down.shape[0]
    return pl.pallas_call(
        grads_kernel,
        out_shape=(jax.ShapeDtypeStruct((2, local, width), WIDE), jax.ShapeDtypeStruct((local, width), WIDE)),
        in_specs=[ANY] * 7,
        out_specs=(ANY, ANY),
        scratch_shapes=[
            pltpu.VMEM((2, BIG, width), LOW),
            pltpu.VMEM((2, BIG, width), LOW),
            pltpu.VMEM((2, local, width), LOW),
            pltpu.VMEM((local, width), LOW),
            pltpu.VMEM((3, local, total), LOW),
            pltpu.VMEM((3, local, width), WIDE),
            pltpu.SemaphoreType.DMA((5, 3)),
            pltpu.SemaphoreType.DMA((2,)),
        ],
        compiler_params=pltpu.CompilerParams(vmem_limit_bytes=60 << 20),
        cost_estimate=pl.CostEstimate(flops=60 << 30, bytes_accessed=60 << 20, transcendentals=4 << 20),
    )(two_all, up_all, saved, two_four, up_four, wide, down)


RING = 8


def rope_tables(place):
    half = ROT // 2
    freq = BASE ** (-jnp.arange(half, dtype=jnp.float32) / half)
    angle = place.astype(jnp.float32)[:, None] * freq[None, :]
    cosine, sine = lax.optimization_barrier((jnp.cos(angle), jnp.sin(angle)))
    lane = jnp.arange(128) % HEAD_DIM
    cosine = jnp.where(lane < ROT, jnp.tile(cosine, (1, 128 // half)), 1.0)
    sine = jnp.tile(sine, (1, 128 // half))
    return jnp.stack(
        [
            cosine,
            jnp.where((lane >= half) & (lane < ROT), sine, 0.0),
            jnp.where(lane < half, -sine, 0.0),
        ]
    )


def on_device(
    tokens,
    norm_gains,
    norm_biases,
    mix_weight,
    mix_bias,
    out_weight,
    gate_up_weight,
    down_weight,
    row_lengths,
    row_group,
    cotangent,
):
    count = lax.axis_size("seq")
    shard = lax.axis_index("seq")
    group = lax.axis_index("grp")
    slots_dev = tokens.shape[0]
    group_slots = slots_dev * count
    label_all, place_all = slot_rows(
        row_lengths, row_group, group, jnp.arange(group_slots, dtype=jnp.int32)
    )
    label_mine = lax.dynamic_slice_in_dim(label_all, shard * slots_dev, slots_dev, 0)
    upstream = jnp.where(label_mine[:, None] >= 0, cotangent, jnp.zeros_like(cotangent))
    lab_col, lab_row = label_all[:, None], label_all[None, :]
    tables = rope_tables(place_all)
    mix_t = jnp.transpose(mix_weight, (1, 0, 2))
    wide_t = jnp.transpose(gate_up_weight, (1, 2, 0))

    normed_all = first(tokens, norm_gains, norm_biases, count)
    up_four = lax.all_gather(upstream, ("grp", "seq"), axis=0, tiled=True)
    query, key, value, attended, lse, part = attend_heads(
        normed_all, mix_t, out_weight, mix_bias.astype(jnp.float32), tables, lab_col, lab_row
    )
    resid, two_all = second(part, tokens, norm_gains, norm_biases, count)
    up_all = lax.dynamic_slice_in_dim(up_four, group * group_slots, group_slots, 0)
    two_mine = lax.dynamic_slice_in_dim(two_all, shard * slots_dev, slots_dev, 0)
    two_four = lax.all_gather(two_mine, ("grp", "seq"), axis=0, tiled=True)
    back_part, down_part, saved = feed(two_all, up_all, wide_t, down_weight)
    layer_out = resid + lax.psum_scatter(
        down_part, "seq", scatter_dimension=0, tiled=True
    ).astype(jnp.float32)
    resid_back, branch_all, sums = third(back_part, resid, upstream, norm_gains, count)
    mix_part, mix_term, out_term, bias_term = attend_heads_back(
        branch_all, normed_all, mix_t, out_weight, tables, lab_col, lab_row,
        (query, key, value, attended, lse),
    )
    mix_sum, out_sum = lax.psum((mix_term, out_term), "grp")
    bias_sum = lax.psum(bias_term, "grp")
    tokens_grad, four = fourth(mix_part, tokens, resid_back, norm_gains, sums)
    wide_grad, down_grad = grads(two_all, up_all, saved, two_four, up_four, wide_t, down_weight)
    return (
        layer_out.astype(jnp.bfloat16),
        tokens_grad,
        four[0:2],
        four[2:4],
        jnp.transpose(mix_sum, (1, 0, 2)).astype(jnp.float32),
        bias_sum,
        out_sum.astype(jnp.float32),
        jnp.transpose(wide_grad, (2, 0, 1)),
        down_grad,
    )


def solution(mesh):
    placed = (
        P(("grp", "seq"), None),
        P(),
        P(),
        P(None, None, "seq"),
        P(None, "seq"),
        P("seq", None),
        P(None, None, "seq"),
        P("seq", None),
        P(),
        P(),
        P(("grp", "seq"), None),
    )
    return jax.shard_map(
        on_device if mesh.shape["seq"] == RING else plain_device,
        mesh=mesh,
        in_specs=placed,
        out_specs=(
            P(("grp", "seq"), None),
            P(("grp", "seq"), None),
            P(),
            P(),
            P(None, None, "seq"),
            P(None, "seq"),
            P("seq", None),
            P(None, None, "seq"),
            P("seq", None),
        ),
        check_vma=False,
    )
```

```python
import functools
import math

import jax
import jax.numpy as jnp
from jax import lax
from jax.experimental import pallas as pl
from jax.experimental.pallas import tpu as pltpu
from jax.sharding import PartitionSpec as P

HEAD_DIM = 64
ROT = 16


EPS = 1e-05
NEG = -1e30
BASE = 10000.0


def layer_norm(values, gain, bias):
    centered = values - jnp.mean(values, axis=-1, keepdims=True)
    scale = lax.rsqrt(jnp.mean(centered * centered, axis=-1, keepdims=True) + EPS)
    unit = centered * scale
    return (unit * gain + bias, unit, scale)


def norm_back(incoming, unit, scale, gain):
    along = incoming * gain
    inner = jnp.mean(along, axis=-1, keepdims=True)
    cross = jnp.mean(along * unit, axis=-1, keepdims=True)
    return (
        scale * (along - inner - unit * cross),
        jnp.sum(incoming * unit, axis=0),
        jnp.sum(incoming, axis=0),
    )


def rotate(values, where, sign):
    half = ROT // 2
    freq = BASE ** (-jnp.arange(half, dtype=jnp.float32) / half)
    angle = where.astype(jnp.float32)[:, None] * freq[None, :]
    cosine = jnp.cos(angle)[:, None, :]
    sine = sign * jnp.sin(angle)[:, None, :]
    first = values[..., :half]
    second = values[..., half:ROT]
    return jnp.concatenate(
        [first * cosine - second * sine, second * cosine + first * sine, values[..., ROT:]], axis=-1
    )


def unrotate(lowered, where):
    wide = lowered.astype(jnp.float32)
    turned = jnp.stack(
        [rotate(wide[:, 0], where, -1.0), rotate(wide[:, 1], where, -1.0), wide[:, 2]], axis=1
    )
    return turned.reshape(lowered.shape[0], 3, -1).astype(jnp.bfloat16)


def slot_rows(row_lengths, row_group, group, slots):
    order = jnp.arange(row_lengths.shape[0], dtype=jnp.int32)
    same = row_group == group
    earlier = (order[:, None] > order[None, :]) & same[None, :]
    begin = jnp.sum(jnp.where(earlier, row_lengths[None, :], 0), axis=1)
    finish = begin + row_lengths
    inside = same[None, :] & (slots[:, None] >= begin[None, :]) & (slots[:, None] < finish[None, :])
    label = jnp.sum(jnp.where(inside, order[None, :] + 1, 0), axis=1) - 1
    offset = jnp.sum(jnp.where(inside, slots[:, None] - begin[None, :], 0), axis=1)
    load = jnp.sum(jnp.where(same, row_lengths, 0))
    return (label, jnp.where(label < 0, slots - load, offset))


def block_scores(query, key, label, start, block):
    part = lax.dynamic_slice_in_dim(query, start, block, 0)
    rows = start + jnp.arange(block, dtype=jnp.int32)
    columns = jnp.arange(label.shape[0], dtype=jnp.int32)
    label_rows = lax.dynamic_slice_in_dim(label, start, block, 0)
    allowed = (label_rows[:, None] == label[None, :]) & (rows[:, None] >= columns[None, :])
    scores = jnp.einsum("qhe,khe->hqk", part, key, preferred_element_type=jnp.float32) * (
        1.0 / math.sqrt(query.shape[-1])
    )
    return (part, jnp.where(allowed[None], scores, NEG))


def attend(query, key, value, label, block):

    def one_block(index):
        part, scores = block_scores(query, key, label, index * block, block)
        top = jnp.max(scores, axis=-1, keepdims=True)
        weights = jnp.exp(scores - top)
        totals = jnp.sum(weights, axis=-1, keepdims=True)
        probs = (weights / totals).astype(jnp.bfloat16)
        mixed = jnp.einsum("hqk,khe->qhe", probs, value, preferred_element_type=jnp.float32)
        return (mixed, top[..., 0] + jnp.log(totals[..., 0]))

    mixed, log_totals = lax.map(one_block, jnp.arange(query.shape[0] // block, dtype=jnp.int32))
    return (mixed.reshape(query.shape), log_totals)


def attend_back(query, key, value, label, log_totals, mixed_back, block):
    scale = 1.0 / math.sqrt(query.shape[-1])

    def one_block(carry, index):
        key_back, value_back = carry
        start = index * block
        part, scores = block_scores(query, key, label, start, block)
        back_part = lax.dynamic_slice_in_dim(mixed_back, start, block, 0)
        probs = jnp.exp(scores - log_totals[index][..., None])
        value_back = value_back + jnp.einsum(
            "hqk,qhe->khe",
            probs.astype(jnp.bfloat16),
            back_part,
            preferred_element_type=jnp.float32,
        )
        probs_back = jnp.einsum(
            "qhe,khe->hqk", back_part, value, preferred_element_type=jnp.float32
        )
        inner = jnp.sum(probs_back * probs, axis=-1, keepdims=True)
        score_back = (probs * (probs_back - inner)).astype(jnp.bfloat16)
        query_back = (
            jnp.einsum("hqk,khe->qhe", score_back, key, preferred_element_type=jnp.float32) * scale
        )
        key_back = (
            key_back
            + jnp.einsum("hqk,qhe->khe", score_back, part, preferred_element_type=jnp.float32)
            * scale
        )
        return ((key_back, value_back), query_back)

    empty = jnp.zeros(key.shape, jnp.float32)
    (key_back, value_back), query_back = lax.scan(
        one_block, (empty, empty), jnp.arange(query.shape[0] // block, dtype=jnp.int32)
    )
    return (query_back.reshape(query.shape), key_back, value_back)


def silu_parts(gate_up):
    gate = gate_up[:, 0]
    upper = gate_up[:, 1]
    sigma = jax.nn.sigmoid(gate)
    return (gate * sigma * upper, gate, upper, sigma)


def gate_back(hidden_back, gate, upper, sigma):
    gate_part = hidden_back * upper * sigma * (1.0 + gate * (1.0 - sigma))
    up_part = hidden_back * gate * sigma
    return jnp.stack([gate_part, up_part], axis=1).astype(jnp.bfloat16)


def gather_rows(values):
    return lax.all_gather(values, "seq", axis=0, tiled=True)


def summed_rows(product, left):
    return lax.psum_scatter(
        product(left).astype(jnp.bfloat16), "seq", scatter_dimension=0, tiled=True
    ).astype(jnp.float32)


def plain_device(
    tokens,
    norm_gains,
    norm_biases,
    mix_weight,
    mix_bias,
    out_weight,
    gate_up_weight,
    down_weight,
    row_lengths,
    row_group,
    cotangent,
):
    seq_count = lax.axis_size("seq")
    shard = lax.axis_index("seq")
    group = lax.axis_index("grp")
    slots_dev = tokens.shape[0]
    width = tokens.shape[1]
    group_slots = slots_dev * seq_count
    block = min(512, group_slots)
    local_width = width // seq_count
    local_heads = local_width // HEAD_DIM
    mine = shard * slots_dev + jnp.arange(slots_dev, dtype=jnp.int32)
    label_mine, place_mine = slot_rows(row_lengths, row_group, group, mine)
    label_all, place_all = slot_rows(
        row_lengths, row_group, group, jnp.arange(group_slots, dtype=jnp.int32)
    )
    inputs = tokens.astype(jnp.float32)
    upstream = cotangent.astype(jnp.float32) * (label_mine >= 0).astype(jnp.float32)[:, None]
    upstream_low = upstream.astype(jnp.bfloat16)
    normed, unit_one, scale_one = layer_norm(inputs, norm_gains[0], norm_biases[0])
    normed_all = gather_rows(normed.astype(jnp.bfloat16))
    up_four = lax.all_gather(upstream_low, ("grp", "seq"), axis=0, tiled=True)
    upstream_all = lax.dynamic_slice_in_dim(up_four, group * group_slots, group_slots, 0)
    mixin = jnp.einsum(
        "td,dcf->tcf", normed_all, mix_weight, preferred_element_type=jnp.float32
    ) + mix_bias.astype(jnp.float32)
    heads_in = mixin.reshape(group_slots, 3, local_heads, HEAD_DIM)
    query = rotate(heads_in[:, 0], place_all, 1.0).astype(jnp.bfloat16)
    key = rotate(heads_in[:, 1], place_all, 1.0).astype(jnp.bfloat16)
    value = heads_in[:, 2].astype(jnp.bfloat16)
    mixed, log_totals = attend(query, key, value, label_all, block)
    attended = mixed.reshape(group_slots, local_width).astype(jnp.bfloat16)

    def out_product(part):
        return jnp.dot(part, out_weight, preferred_element_type=jnp.float32)

    resid = inputs + summed_rows(out_product, attended)
    normed_two, unit_two, scale_two = layer_norm(resid, norm_gains[1], norm_biases[1])
    normed_two_low = normed_two.astype(jnp.bfloat16)
    normed_two_all = gather_rows(normed_two_low)
    two_four = lax.all_gather(normed_two_low, ("grp", "seq"), axis=0, tiled=True)

    def up_to_back(two, up):
        gate_up = jnp.einsum("td,dcf->tcf", two, gate_up_weight, preferred_element_type=jnp.float32)
        hidden, gate, upper, sigma = silu_parts(gate_up)
        hidden_back = jnp.einsum("td,fd->tf", up, down_weight, preferred_element_type=jnp.float32)
        return hidden.astype(jnp.bfloat16), gate_back(hidden_back, gate, upper, sigma)

    hidden_low, gate_up_back = up_to_back(normed_two_all, upstream_all)

    def down_product(part):
        return jnp.dot(part, down_weight, preferred_element_type=jnp.float32)

    layer_out = resid + summed_rows(down_product, hidden_low)

    def gate_up_product(part):
        return jnp.einsum("tcf,dcf->td", part, gate_up_weight, preferred_element_type=jnp.float32)

    normed_two_back = summed_rows(gate_up_product, gate_up_back)
    hidden_four, back_four = up_to_back(two_four, up_four)
    down_grad = jnp.einsum("tf,td->fd", hidden_four, up_four, preferred_element_type=jnp.float32)
    gate_up_grad = jnp.einsum(
        "td,tcf->dcf", two_four, back_four, preferred_element_type=jnp.float32
    )
    resid_part, gain_two, bias_two = norm_back(normed_two_back, unit_two, scale_two, norm_gains[1])
    resid_back = upstream + resid_part
    branch_all = gather_rows(resid_back.astype(jnp.bfloat16))
    out_term = jnp.einsum("te,td->ed", attended, branch_all, preferred_element_type=jnp.float32)
    out_grad = lax.psum(out_term.astype(jnp.bfloat16), "grp").astype(jnp.float32)
    attended_back = jnp.einsum(
        "td,ed->te", branch_all, out_weight, preferred_element_type=jnp.float32
    ).astype(jnp.bfloat16)
    heads_back = attended_back.reshape(group_slots, local_heads, HEAD_DIM)
    query_back, key_back, value_back = attend_back(
        query, key, value, label_all, log_totals, heads_back, block
    )
    lowered = jnp.stack([query_back, key_back, value_back], axis=1).astype(jnp.bfloat16)
    mixin_back = unrotate(lowered, place_all)
    mix_term = jnp.einsum("td,tcf->dcf", normed_all, mixin_back, preferred_element_type=jnp.float32)
    mix_grad = lax.psum(mix_term.astype(jnp.bfloat16), "grp").astype(jnp.float32)
    bias_term = jnp.sum(mixin_back, axis=0, dtype=jnp.float32)
    mix_bias_grad = lax.psum(bias_term, "grp")

    def mix_product(part):
        return jnp.einsum("tcf,dcf->td", part, mix_weight, preferred_element_type=jnp.float32)

    normed_back = summed_rows(mix_product, mixin_back)
    tokens_part, gain_one, bias_one = norm_back(normed_back, unit_one, scale_one, norm_gains[0])
    tokens_grad = (resid_back + tokens_part).astype(jnp.bfloat16)
    gains_grad, biases_grad = lax.psum(
        (jnp.stack([gain_one, gain_two]), jnp.stack([bias_one, bias_two])), ("grp", "seq")
    )
    return (
        layer_out.astype(jnp.bfloat16),
        tokens_grad,
        gains_grad,
        biases_grad,
        mix_grad,
        mix_bias_grad,
        out_grad,
        gate_up_grad,
        down_grad,
    )


MESH_ID = pl.DeviceIdType.MESH
N_RS = 10
N_AG = 13


class Ring:
    def __init__(self):
        self.group = lax.axis_index("grp")
        self.me = lax.axis_index("seq")
        core = self.me % 2
        x = (self.me // 2) % 2
        y = self.me // 4
        self.flip = 1 - 2 * core
        self.twin = self.me + self.flip
        self.xn = self.me + 2 - 4 * x
        self.yn = self.me + 4 - 8 * y
        self.dn = self.xn + 4 - 8 * y

    def dev(self, seq):
        return (self.group, seq)

    def barrier(self, extra=()):
        sem = pltpu.get_barrier_semaphore()
        peers = [self.dev(self.twin), self.dev(self.xn), self.dev(self.yn)] + list(extra)
        for peer in peers:
            pl.semaphore_signal(sem, inc=1, device_id=peer, device_id_type=MESH_ID)
        pl.semaphore_wait(sem, len(peers))

    def copy(self, src, dst, send, recv, kind, seq):
        return pltpu.make_async_remote_copy(
            src_ref=src,
            dst_ref=dst,
            send_sem=send.at[kind],
            recv_sem=recv.at[kind],
            device_id=self.dev(seq),
            device_id_type=MESH_ID,
        )


class Gather:
    def __init__(self, ring, own, out, send, recv, local):
        self.ring, self.own, self.out = ring, own, out
        self.send, self.recv, self.local = send, recv, local
        self.rows = own.shape[0]
        self.half = self.rows // 2

    def at(self, block, part=None):
        rows, half = self.rows, self.half
        if part is None:
            return self.out.at[pl.ds(pl.multiple_of(block * rows, rows), rows), :]
        return self.out.at[pl.ds(pl.multiple_of(block * rows + part * half, half), half), :]

    def copy(self, kind):
        ring, half = self.ring, self.half
        if kind < 4:
            part, seq = ((0, ring.xn), (1, ring.yn), (1, ring.xn), (0, ring.yn))[kind]
            src, dst = self.own.at[pl.ds(part * half, half), :], self.at(ring.me, part)
        elif kind == 4:
            src, dst, seq = self.own, self.at(ring.me), ring.twin
        else:
            block, part, seq = (
                (ring.xn, 0, ring.yn),
                (ring.xn, 0, ring.twin),
                (ring.yn, 1, ring.xn),
                (ring.yn, 1, ring.twin),
                (ring.xn, 1, ring.twin),
                (ring.yn, 0, ring.twin),
                (ring.dn, 0, ring.twin),
                (ring.dn, 1, ring.twin),
            )[kind - 5]
            src = dst = self.at(block, part)
        return ring.copy(src, dst, self.send, self.recv, kind, seq)

    def keep(self):
        return pltpu.make_async_copy(self.own, self.at(self.ring.me), self.local)

    def stage(self, number):
        if number == 0:
            self.keep().start()
            for kind in range(5):
                self.copy(kind).start()
        elif number == 1:
            self.copy(0).wait_recv()
            self.copy(5).start()
            self.copy(6).start()
            self.copy(1).wait_recv()
            self.copy(7).start()
            self.copy(8).start()
        elif number == 2:
            self.copy(2).wait_recv()
            self.copy(9).start()
            self.copy(3).wait_recv()
            self.copy(10).start()
        elif number == 3:
            self.copy(5).wait_recv()
            self.copy(11).start()
            self.copy(7).wait_recv()
            self.copy(12).start()
        else:
            self.keep().wait()
            for kind in (4, 6, 8, 9, 10, 11, 12):
                self.copy(kind).wait_recv()
            for kind in range(N_AG):
                self.copy(kind).wait_send()

    def all(self):
        for number in range(5):
            self.stage(number)


class Scatter:
    def __init__(self, ring, part, total, own, pair, rx, ry, fx, fy, mid, send, recv, local):
        self.ring, self.part, self.total = ring, part, total
        self.own, self.pair, self.rx, self.ry = own, pair, rx, ry
        self.fx, self.fy, self.mid = fx, fy, mid
        self.send, self.recv, self.local = send, recv, local
        self.rows, self.width = total.shape

    def block(self, index):
        return self.part.at[pl.ds(pl.multiple_of(index * self.rows, self.rows), self.rows), :]

    def index(self, slot):
        ring = self.ring
        return (ring.dn, ring.xn, ring.yn, ring.me)[slot]

    def keep(self, slot):
        return pltpu.make_async_copy(self.block(self.index(slot)), self.own.at[slot], self.local.at[slot])

    def copy(self, kind):
        ring, half = self.ring, self.width // 2
        lo, hi = pl.ds(0, half), pl.ds(half, half)
        if kind < 4:
            src, dst, seq = self.block(self.index(kind) + ring.flip), self.pair.at[kind], ring.twin
        else:
            src, dst, seq = (
                (self.own.at[0, :, lo], self.rx.at[0], ring.xn),
                (self.own.at[0, :, hi], self.ry.at[0], ring.yn),
                (self.own.at[1, :, lo], self.rx.at[1], ring.xn),
                (self.own.at[2, :, hi], self.ry.at[1], ring.yn),
                (self.mid.at[0], self.fy, ring.yn),
                (self.mid.at[1], self.fx, ring.xn),
            )[kind - 4]
        return ring.copy(src, dst, self.send, self.recv, kind, seq)

    def added(self, slot):
        self.keep(slot).wait()
        self.copy(slot).wait_recv()
        return self.own[slot].astype(jnp.float32) + self.pair[slot].astype(jnp.float32)

    def stage(self, number):
        wide, low, half = jnp.float32, self.own.dtype, self.width // 2
        lo, hi = pl.ds(0, half), pl.ds(half, half)
        own, total = self.own, self.total
        if number == 0:
            for slot in range(4):
                self.copy(slot).start()
                self.keep(slot).start()
        elif number == 1:
            own[0] = self.added(0).astype(low)
            self.copy(4).start()
            self.copy(5).start()
            own[1] = self.added(1).astype(low)
            self.copy(6).start()
            own[2] = self.added(2).astype(low)
            self.copy(7).start()
            total[...] = self.added(3)
        elif number == 2:
            self.copy(4).wait_recv()
            self.mid[0] = (own[2, :, lo].astype(wide) + self.rx[0].astype(wide)).astype(low)
            self.copy(8).start()
            self.copy(5).wait_recv()
            self.mid[1] = (own[1, :, hi].astype(wide) + self.ry[0].astype(wide)).astype(low)
            self.copy(9).start()
        else:
            self.copy(6).wait_recv()
            total[:, lo] += self.rx[1].astype(wide)
            self.copy(7).wait_recv()
            total[:, hi] += self.ry[1].astype(wide)
            self.copy(8).wait_recv()
            total[:, lo] += self.fy[...].astype(wide)
            self.copy(9).wait_recv()
            total[:, hi] += self.fx[...].astype(wide)
            for kind in range(N_RS):
                self.copy(kind).wait_send()

    def all(self):
        for number in range(4):
            self.stage(number)


def scatter_buffers(rows, width):
    low = jnp.bfloat16
    half = width // 2
    return [
        pltpu.VMEM((rows, width), jnp.float32),
        pltpu.VMEM((4, rows, width), low),
        pltpu.VMEM((4, rows, width), low),
        pltpu.VMEM((2, rows, half), low),
        pltpu.VMEM((2, rows, half), low),
        pltpu.VMEM((rows, half), low),
        pltpu.VMEM((rows, half), low),
        pltpu.VMEM((2, rows, half), low),
    ]


def scatter_sems():
    return [
        pltpu.SemaphoreType.DMA((N_RS,)),
        pltpu.SemaphoreType.DMA((N_RS,)),
        pltpu.SemaphoreType.DMA((4,)),
    ]


def scatter_scratch(rows, width):
    return scatter_buffers(rows, width) + scatter_sems()


def gather_sems():
    return [
        pltpu.SemaphoreType.DMA((N_AG,)),
        pltpu.SemaphoreType.DMA((N_AG,)),
        pltpu.SemaphoreType.DMA,
    ]


def gather_scratch(rows, width):
    return [pltpu.VMEM((rows, width), jnp.bfloat16)] + gather_sems()


def unit_of(values):
    centered = values - jnp.mean(values, axis=-1, keepdims=True)
    scale = lax.rsqrt(jnp.mean(centered * centered, axis=-1, keepdims=True) + EPS)
    return centered * scale, scale


def back_of(incoming, unit, scale, gain):
    along = incoming * gain
    inner = jnp.mean(along, axis=-1, keepdims=True)
    cross = jnp.mean(along * unit, axis=-1, keepdims=True)
    return scale * (along - inner - unit * cross)


def first_kernel(tokens, gains, biases, normed_all, own, send, recv, local):
    ring = Ring()
    unit, _ = unit_of(tokens[...].astype(jnp.float32))
    own[...] = (unit * gains[0:1] + biases[0:1]).astype(own.dtype)
    ring.barrier()
    Gather(ring, own, normed_all, send, recv, local).all()


def second_kernel(part, tokens, gains, biases, resid, two_all, two_own, *scratch):
    rs, ag = scratch[:11], scratch[11:]
    ring = Ring()
    ring.barrier()
    Scatter(ring, part, *rs).all()
    total = rs[0]
    resid[...] = total[...] + tokens[...].astype(jnp.float32)
    unit, _ = unit_of(resid[...])
    two_own[...] = (unit * gains[1:2] + biases[1:2]).astype(two_own.dtype)
    Gather(ring, two_own, two_all, *ag).all()


def third_kernel(part, resid, upstream, gains, resid_back, branch_all, sums, *scratch):
    rs, ag = scratch[:11], scratch[11:]
    ring = Ring()
    ring.barrier()
    Scatter(ring, part, *rs).all()
    total, own = rs[0], ag[0]
    unit, scale = unit_of(resid[...])
    incoming = total[...]
    resid_back[...] = upstream[...].astype(jnp.float32) + back_of(incoming, unit, scale, gains[1:2])
    own[...] = resid_back[...].astype(own.dtype)
    gather = Gather(ring, own, branch_all, *ag[1:])
    gather.stage(0)
    sums[0:1] = jnp.sum(incoming * unit, axis=0, keepdims=True)
    sums[1:2] = jnp.sum(incoming, axis=0, keepdims=True)
    for number in range(1, 5):
        gather.stage(number)


VM = pl.BlockSpec(memory_space=pltpu.VMEM)
ANY = pl.BlockSpec(memory_space=pltpu.HBM)


def call(kernel, number, ins, outs, scratch, limit=60, flops=0, cost=20_000_000, scratch_in=None):
    return pl.pallas_call(
        kernel,
        out_shape=tuple(jax.ShapeDtypeStruct(*shape) for shape, _ in outs),
        in_specs=[spec for _, spec in ins],
        out_specs=tuple(spec for _, spec in outs),
        scratch_shapes=scratch,
        compiler_params=pltpu.CompilerParams(
            collective_id=number,
            has_side_effects=True,
            vmem_limit_bytes=limit << 20,
        ),
        cost_estimate=pl.CostEstimate(flops=flops, bytes_accessed=cost, transcendentals=0),
    )(*[value for value, _ in ins])


def first(tokens, gains, biases, count):
    rows, width = tokens.shape
    low = jnp.bfloat16
    return call(
        first_kernel,
        1,
        [(tokens, VM), (gains, VM), (biases, VM)],
        [(((rows * count, width), low), ANY)],
        gather_scratch(rows, width),
    )[0]


def second(part, tokens, gains, biases, count):
    rows, width = tokens.shape
    return call(
        second_kernel,
        2,
        [(part, ANY), (tokens, VM), (gains, VM), (biases, VM)],
        [
            (((rows, width), jnp.float32), VM),
            (((rows * count, width), jnp.bfloat16), ANY),
            (((rows, width), jnp.bfloat16), VM),
        ],
        scatter_scratch(rows, width) + gather_sems(),
    )


def third(part, resid, upstream, gains, count):
    rows, width = resid.shape
    return call(
        third_kernel,
        3,
        [(part, ANY), (resid, VM), (upstream, VM), (gains, VM)],
        [
            (((rows, width), jnp.float32), VM),
            (((rows * count, width), jnp.bfloat16), ANY),
            (((2, width), jnp.float32), VM),
        ],
        scatter_scratch(rows, width) + gather_scratch(rows, width),
    )


TILE = 256
WIDE = jnp.float32
LOW = jnp.bfloat16
NT = (((1,), (1,)), ((), ()))
TN = (((0,), (0,)), ((), ()))


def mm(a, b, dims=(((1,), (0,)), ((), ()))):
    return lax.dot_general(a, b, dims, preferred_element_type=WIDE)


def far_rows(far, ring, away, total):
    groups = lax.axis_size("grp")
    rows = far.shape[0] // groups
    index = lax.rem(ring.group + away, groups)
    return far.at[pl.ds(pl.multiple_of(index * rows, rows), rows), :]


def head_lanes(shape, head):
    return lax.broadcasted_iota(jnp.int32, shape, 1) // HEAD_DIM == head


def turn(u, tables, rows, sign):
    cosine, below, above = (
        jnp.concatenate([tables[i, rows, :]] * (u.shape[1] // 128), axis=1) for i in range(3)
    )
    side = pltpu.roll(u, 8, 1) * below + pltpu.roll(u, u.shape[1] - 8, 1) * above
    return u * cosine + side if sign > 0 else u * cosine - side


def load(pairs, sems):
    copies = []
    for i, (src, dst) in enumerate(pairs):
        copy = pltpu.make_async_copy(src, dst, sems.at[i])
        copy.start()
        copies.append(copy)
    return copies


def attend_kernel(
    normed_all, weight, out_weight, bias, tables, lab_col, lab_row,
    upstream, query, key, value, attended, lse, part, up_all,
    normed, w, mask, stats, stage, sems, outs, send, recv, local,
):
    total, width = query.shape
    tiles = total // TILE
    ring = Ring()
    ring.barrier()
    gather = Gather(ring, upstream, up_all, send, recv, local)
    gather.stage(0)
    loads = load(
        [(normed_all.at[pl.ds(i * TILE, TILE), :], normed.at[pl.ds(i * TILE, TILE), :]) for i in range(tiles)]
        + [(weight, w)],
        sems,
    )
    loads[-1].wait()
    for i in range(tiles):
        rows = pl.ds(i * TILE, TILE)
        loads[i].wait()
        x = normed[rows, :]
        u = mm(x, w[0]) + bias[0:1]
        query[rows, :] = (turn(u, tables, rows, 1).astype(LOW).astype(WIDE) * (1.0 / 8)).astype(LOW)
        u = mm(x, w[1]) + bias[1:2]
        key[rows, :] = turn(u, tables, rows, 1).astype(LOW)
        value[rows, :] = (mm(x, w[2]) + bias[2:3]).astype(LOW)
    gather.stage(1)
    copies = []
    for i in range(tiles):
        rows = pl.ds(i * TILE, TILE)
        span = (i + 1) * TILE
        q_at = i * TILE + lax.broadcasted_iota(jnp.int32, (TILE, span), 0)
        k_at = lax.broadcasted_iota(jnp.int32, (TILE, span), 1)
        allowed = (lab_col[rows, :] == lab_row[:, :span]) & (q_at >= k_at)
        mask[:, :span] = jnp.where(allowed, 0.0, NEG)
        q = query[rows, :]

        def one_head(head, carry):
            mixed, logs = carry
            mine = head_lanes(q.shape, head)
            s = mm(jnp.where(mine, q, jnp.zeros_like(q)), key[:span, :], NT) + mask[:, :span]
            top = jnp.max(s, axis=1, keepdims=True)
            p = jnp.exp(s - top)
            norm = jnp.sum(p, axis=1, keepdims=True)
            o = mm(p.astype(LOW), value[:span, :]) / norm
            mixed = jnp.where(mine, o, mixed)
            lane = lax.broadcasted_iota(jnp.int32, logs.shape, 1)
            logs = jnp.where(lane == head, top + jnp.log(norm), logs)
            return mixed, logs

        mixed, logs = lax.fori_loop(
            0, width // HEAD_DIM, one_head,
            (jnp.zeros((TILE, width), WIDE), jnp.zeros((TILE, 128), WIDE)),
        )
        low = mixed.astype(LOW)
        attended[rows, :] = low
        stats[rows, :] = logs
        stage[i] = mm(low, out_weight[...]).astype(LOW)
        copy = pltpu.make_async_copy(stage.at[i], part.at[rows, :], outs.at[i])
        copy.start()
        copies.append(copy)
        if i >= 2:
            gather.stage(i)
    gather.stage(4)
    lse[...] = jnp.transpose(stats[...])[:8, :]
    for copy in copies:
        copy.wait()


def attend_heads(normed_all, weight, out_weight, bias, tables, lab_col, lab_row, upstream):
    total, width = normed_all.shape
    local = out_weight.shape[0]
    tiles = total // TILE
    slab = (((total, local), LOW), VM)
    tall = (((total, width), LOW), ANY)
    return call(
        attend_kernel,
        5,
        [(normed_all, ANY), (weight, ANY), (out_weight, VM), (bias, VM), (tables, VM), (lab_col, VM),
         (lab_row, VM), (upstream, VM)],
        [slab, slab, slab, slab, (((8, total), WIDE), VM), tall, tall],
        [
            pltpu.VMEM((total, width), LOW),
            pltpu.VMEM((3, width, local), LOW),
            pltpu.VMEM((TILE, total), WIDE),
            pltpu.VMEM((total, 128), WIDE),
            pltpu.VMEM((tiles, TILE, width), LOW),
            pltpu.SemaphoreType.DMA((tiles + 1,)),
            pltpu.SemaphoreType.DMA((tiles,)),
        ]
        + gather_sems(),
        limit=60,
        flops=7 << 30,
    )


def attend_back_kernel(
    branch_all, normed_all, weight, out_weight, tables, lab_col, lab_row,
    query, key, value, attended, lse, far,
    part, terms, out_term, bias_term, far_all,
    branch, normed, w, mask, inner, heads_back, query_back, key_back, value_back, mixin, stage, mixes,
    sems, outs, send, recv, local,
):
    total, width = query.shape
    tiles = total // TILE
    heads = width // HEAD_DIM
    ring = Ring()
    ring.barrier()
    gather = Gather(ring, far_rows(far, ring, 1, far_all.shape[0]), far_all, send, recv, local)
    gather.stage(0)
    loads = load(
        [(branch_all.at[pl.ds(i * TILE, TILE), :], branch.at[pl.ds(i * TILE, TILE), :]) for i in range(tiles)]
        + [(normed_all, normed), (weight, w)],
        sems,
    )
    head_of = lax.broadcasted_iota(jnp.int32, (8, width), 1) // HEAD_DIM
    pick = (head_of == lax.broadcasted_iota(jnp.int32, (8, width), 0)).astype(LOW)
    for i in range(tiles):
        rows = pl.ds(i * TILE, TILE)
        loads[i].wait()
        low = mm(branch[rows, :], out_weight[...], NT).astype(LOW)
        heads_back[rows, :] = low
        prod = low.astype(WIDE) * attended[rows, :].astype(WIDE)
        high = prod.astype(LOW)
        rest = (prod - high.astype(WIDE)).astype(LOW)
        inner[:, rows] = mm(pick, high, NT) + mm(pick, rest, NT)
    out_term[...] = mm(attended[...], branch[...], TN).astype(LOW)
    gather.stage(1)
    key_back[...] = jnp.zeros_like(key_back)
    value_back[...] = jnp.zeros_like(value_back)
    for i in range(tiles):
        rows = pl.ds(i * TILE, TILE)
        span = (i + 1) * TILE
        k_at = lax.broadcasted_iota(jnp.int32, (span, TILE), 0)
        q_at = i * TILE + lax.broadcasted_iota(jnp.int32, (span, TILE), 1)
        allowed = (lab_col[:span, :] == lab_row[:, rows]) & (q_at >= k_at)
        mask[:span, :] = jnp.where(allowed, 0.0, NEG)
        q = query[rows, :]
        d_out = heads_back[rows, :]

        def one_head(head, q_back):
            mine = head_lanes(q.shape, head)
            q_h = jnp.where(mine, q, jnp.zeros_like(q))
            d_h = jnp.where(mine, d_out, jnp.zeros_like(q))
            k = key[:span, :]
            k_h = jnp.where(head_lanes(k.shape, head), k, jnp.zeros_like(k))
            p = jnp.exp(mm(k, q_h, NT) + mask[:span, :] - lse[pl.ds(head, 1), rows])
            d_p = mm(value[:span, :], d_h, NT)
            d_s = (p * (d_p - inner[pl.ds(head, 1), rows])).astype(LOW)
            value_back[:span, :] += mm(p.astype(LOW), d_h)
            key_back[:span, :] += mm(d_s, q_h)
            return q_back + mm(d_s, k_h, TN)

        query_back[rows, :] = lax.fori_loop(0, heads, one_head, jnp.zeros((TILE, width), WIDE))
        if i >= 2:
            gather.stage(i)
    loads[-1].wait()
    loads[-2].wait()
    copies = []
    sums = [jnp.zeros((1, width), WIDE)] * 3
    for i in range(tiles):
        rows = pl.ds(i * TILE, TILE)
        q_b = (query_back[rows, :] * (1.0 / 8)).astype(LOW).astype(WIDE)
        k_b = key_back[rows, :].astype(LOW).astype(WIDE)
        trio = [
            turn(q_b, tables, rows, -1).astype(LOW),
            turn(k_b, tables, rows, -1).astype(LOW),
            value_back[rows, :].astype(LOW),
        ]
        product = jnp.zeros((TILE, normed.shape[1]), WIDE)
        for c, item in enumerate(trio):
            mixin[c, rows, :] = item
            sums[c] = sums[c] + jnp.sum(item.astype(WIDE), axis=0, keepdims=True)
            product = product + mm(item, w[c], NT)
        stage[i] = product.astype(LOW)
        copy = pltpu.make_async_copy(stage.at[i], part.at[rows, :], outs.at[i])
        copy.start()
        copies.append(copy)
    for c in range(3):
        bias_term[c : c + 1, :] = sums[c]
        mixes[c] = mm(normed[...], mixin[c], TN).astype(LOW)
        copy = pltpu.make_async_copy(mixes.at[c], terms.at[c], outs.at[tiles + c])
        copy.start()
        copies.append(copy)
    gather.stage(4)
    for copy in copies:
        copy.wait()


def attend_heads_back(
    branch_all, normed_all, weight, out_weight, tables, lab_col, lab_row, saved, far
):
    total, width = normed_all.shape
    local = out_weight.shape[0]
    tiles = total // TILE
    tall = (((total, width), LOW), ANY)
    return call(
        attend_back_kernel,
        6,
        [(item, ANY) for item in (branch_all, normed_all, weight)]
        + [(item, VM) for item in (out_weight, tables, lab_col, lab_row) + tuple(saved)]
        + [(far, ANY)],
        [
            tall,
            (((3, width, local), LOW), ANY),
            (((local, width), LOW), VM),
            (((3, local), WIDE), VM),
            tall,
        ],
        [
            pltpu.VMEM((total, width), LOW),
            pltpu.VMEM((total, width), LOW),
            pltpu.VMEM((3, width, local), LOW),
            pltpu.VMEM((total, TILE), WIDE),
            pltpu.VMEM((8, total), WIDE),
            pltpu.VMEM((total, local), LOW),
            pltpu.VMEM((total, local), WIDE),
            pltpu.VMEM((total, local), WIDE),
            pltpu.VMEM((total, local), WIDE),
            pltpu.VMEM((3, total, local), LOW),
            pltpu.VMEM((tiles, TILE, width), LOW),
            pltpu.VMEM((3, width, local), LOW),
            pltpu.SemaphoreType.DMA((tiles + 2,)),
            pltpu.SemaphoreType.DMA((tiles + 3,)),
        ]
        + gather_sems(),
        limit=60,
        flops=16 << 30,
    )


def units(gate, upper, hidden_back):
    sigma = jax.nn.sigmoid(gate)
    silu = gate * sigma
    return (
        (silu * upper).astype(LOW),
        (hidden_back * upper * sigma * (1.0 + gate * (1.0 - sigma))).astype(LOW),
        (hidden_back * silu).astype(LOW),
    )


def forward_units(two, up, wide, down):
    return units(mm(wide[0], two, NT), mm(wide[1], two, NT), mm(down[...], up, NT))


def feed_kernel(two_all, up_all, wide_hbm, down_hbm, far, back_part, down_part, saved, far_one,
                two, up, wide, down, kept, stage, sems, outs, *ag):
    total = two_all.shape[0]
    tiles = total // TILE
    ring = Ring()
    ring.barrier()
    gather = Gather(ring, far_rows(far, ring, 1, total), far_one, *ag)
    plan = {1: 1, 3: 2, 5: 3}

    def events(at):
        if at in plan:
            gather.stage(plan[at])

    gather.stage(0)
    pairs = [(wide_hbm, wide), (down_hbm, down)]
    for i in range(tiles):
        rows = pl.ds(i * TILE, TILE)
        pairs += [(two_all.at[rows, :], two.at[rows, :]), (up_all.at[rows, :], up.at[rows, :])]
    loads = load(pairs, sems)
    loads[0].wait()
    loads[1].wait()
    copies = []
    for i in range(tiles):
        rows = pl.ds(i * TILE, TILE)
        loads[2 + 2 * i].wait()
        loads[3 + 2 * i].wait()
        trio = forward_units(two[rows, :], up[rows, :], wide, down)
        for c in range(3):
            kept[c, :, rows] = trio[c]
        events(2 * i)
        stage[0, rows, :] = (mm(trio[1], wide[0], TN) + mm(trio[2], wide[1], TN)).astype(LOW)
        copy = pltpu.make_async_copy(stage.at[0, rows, :], back_part.at[rows, :], outs.at[2 * i])
        copy.start()
        copies.append(copy)
        events(2 * i + 1)
        stage[1, rows, :] = mm(trio[0], down[...], TN).astype(LOW)
        copy = pltpu.make_async_copy(stage.at[1, rows, :], down_part.at[rows, :], outs.at[2 * i + 1])
        copy.start()
        copies.append(copy)
    copy = pltpu.make_async_copy(kept, saved, outs.at[2 * tiles])
    copy.start()
    gather.stage(4)
    copy.wait()
    for copy in copies:
        copy.wait()


def feed(two_all, up_all, wide, down, far):
    total, width = two_all.shape
    units_local = down.shape[0]
    tiles = total // TILE
    tall = (((total, width), LOW), ANY)
    return call(
        feed_kernel,
        7,
        [(item, ANY) for item in (two_all, up_all, wide, down, far)],
        [tall, tall, (((3, units_local, total), LOW), ANY), tall],
        [
            pltpu.VMEM((total, width), LOW),
            pltpu.VMEM((total, width), LOW),
            pltpu.VMEM((2, units_local, width), LOW),
            pltpu.VMEM((units_local, width), LOW),
            pltpu.VMEM((3, units_local, total), LOW),
            pltpu.VMEM((2, total, width), LOW),
            pltpu.SemaphoreType.DMA((2 + 2 * tiles,)),
            pltpu.SemaphoreType.DMA((1 + 2 * tiles,)),
        ]
        + gather_sems(),
        limit=60,
        flops=18 << 30,
    )


N_LAST_GATHERS = 4


def last_kernel(
    mix_part, down_part, tokens, resid, resid_back, gains, sums, bias_term,
    two_all, up_all, saved, two_far, up_far, up_one, two_one, wide_hbm, down_hbm,
    tokens_grad, layer_out, four, wide_grad, down_grad, two_two, two_three, up_two, up_three,
    two, up, kept, wide, down, acc, inbox, mail, sems, outs, mail_send, mail_recv, *scratch,
):
    total = two_all.shape[0]
    per = total // TILE
    one_scratch, two_scratch, ag = scratch[:11], scratch[11:22], scratch[22:]
    ring = Ring()
    group, groups = ring.group, lax.axis_size("grp")
    others = [(lax.rem(group + k, groups), ring.me) for k in range(1, groups)]
    ring.barrier(others)

    one = Scatter(ring, mix_part, *one_scratch)
    second_sum = Scatter(ring, down_part, *two_scratch)
    u2, g2, u3, g3 = [
        Gather(ring, far_rows(far, ring, k, total), dst, *ag[3 * i : 3 * i + 3])
        for i, (far, k, dst) in enumerate(
            ((up_far, 2, up_two), (two_far, 2, two_two), (up_far, 3, up_three), (two_far, 3, two_three))
        )
    ]
    two_sources = (two_all, two_one, two_two, two_three)
    up_sources = (up_all, up_one, up_two, up_three)

    def first_norm():
        unit, scale = unit_of(tokens[...].astype(WIDE))
        incoming = one.total[...]
        tokens_grad[...] = (resid_back[...] + back_of(incoming, unit, scale, gains[0:1])).astype(LOW)
        four[...] = jnp.zeros_like(four)
        four[0:1] = jnp.sum(incoming * unit, axis=0, keepdims=True)
        four[1:2] = sums[0:1]
        four[2:3] = jnp.sum(incoming, axis=0, keepdims=True)
        four[3:4] = sums[1:2]

    def mail_copy(stage):
        peer = (ring.twin, ring.xn, ring.yn)[stage]
        return ring.copy(mail.at[stage], inbox.at[stage], mail_send, mail_recv, stage, peer)

    def mail_start(stage):
        mail[stage] = four[...]
        mail_copy(stage).start()

    def mail_wait(stage):
        mail_copy(stage).wait_recv()
        four[...] += inbox[stage]

    def group_copy(k):
        return pltpu.make_async_remote_copy(
            src_ref=mail.at[3],
            dst_ref=inbox.at[2 + k],
            send_sem=mail_send.at[2 + k],
            recv_sem=mail_recv.at[2 + k],
            device_id=others[k - 1],
            device_id_type=MESH_ID,
        )

    def group_start():
        four[4:5] = jnp.zeros((1, four.shape[1]), WIDE)
        local = bias_term.shape[1]
        for c in range(3):
            four[4:5, c * local : (c + 1) * local] = bias_term[c : c + 1, :]
        mail[3] = four[...]
        for k in range(1, groups):
            group_copy(k).start()

    def group_wait():
        for k in range(1, groups):
            group_copy(k).wait_recv()
        summed = jnp.zeros(four.shape, WIDE)
        for number in range(groups):
            term = mail[3]
            for k in range(1, groups):
                source = lax.rem(group + groups - k, groups)
                term = jnp.where(source == number, inbox[2 + k], term)
            summed = summed + term
        four[...] = summed
        for stage in range(3):
            mail_copy(stage).wait_send()
        for k in range(1, groups):
            group_copy(k).wait_send()

    def layer_end():
        layer_out[...] = (resid[...] + second_sum.total[...]).astype(LOW)

    def stage(item, number):
        return lambda: item.stage(number)

    plan = {
        0: [stage(u2, 0)],
        3: [stage(u2, 1), stage(g2, 0)],
        4: [stage(u2, 2)],
        5: [stage(u2, 3)],
        6: [stage(g2, 1), stage(u3, 0)],
        7: [stage(g2, 2), stage(u2, 4)],
        8: [stage(g2, 3), stage(g2, 4), stage(u3, 1), stage(g3, 0)],
        9: [stage(u3, 2)],
        10: [stage(u3, 3), stage(one, 0)],
        11: [stage(g3, 1), stage(one, 1), stage(u3, 4)],
        12: [stage(g3, 2), stage(g3, 3), stage(g3, 4), stage(second_sum, 0)],
        13: [stage(one, 2), stage(second_sum, 1)],
        14: [stage(one, 3), first_norm, lambda: mail_start(0)],
        15: [lambda: mail_wait(0), lambda: mail_start(1), stage(second_sum, 2)],
    }

    def fetch(source, tile, side):
        start = tile * TILE if isinstance(tile, int) else pl.multiple_of(tile * TILE, TILE)
        rows = pl.ds(start, TILE)
        return [
            pltpu.make_async_copy(two_sources[source].at[rows, :], two.at[side], sems.at[side, 0]),
            pltpu.make_async_copy(up_sources[source].at[rows, :], up.at[side], sems.at[side, 1]),
        ]

    def fetch_kept(tile, side):
        start = tile * TILE if isinstance(tile, int) else pl.multiple_of(tile * TILE, TILE)
        return pltpu.make_async_copy(saved.at[:, :, pl.ds(start, TILE)], kept.at[side], sems.at[side, 2])

    weights = load([(wide_hbm, wide), (down_hbm, down)], sems.at[2])
    for copy in fetch(0, 0, 0) + [fetch_kept(0, 0)]:
        copy.start()
    acc[...] = jnp.zeros_like(acc)

    def add(side, trio):
        acc[2] += mm(trio[0], up[side])
        acc[0] += mm(trio[1], two[side])
        acc[1] += mm(trio[2], two[side])

    steps = per * groups

    def start_fetch(step):
        side = lax.rem(step, 2)
        for source in range(groups):

            @pl.when((step < steps) & (step // per == source))
            def _():
                for copy in fetch(source, lax.rem(step, per), side):
                    copy.start()
                if source == 0:
                    fetch_kept(lax.rem(step, per), side).start()

    def events(step):
        for at, acts in plan.items():

            @pl.when(step == at)
            def _():
                for act in acts:
                    act()


    def own_body(step, carry):
        events(step)
        side = lax.rem(step, 2)
        for copy in fetch(0, 0, side) + [fetch_kept(0, side)]:
            copy.wait()

        @pl.when(step + 1 < per)
        def _():
            start_fetch(step + 1)

        add(side, [kept[side, c] for c in range(3)])
        return carry

    lax.fori_loop(0, per, own_body, 0)
    for copy in weights:
        copy.wait()

    def body(step, carry):
        events(step)
        side = lax.rem(step, 2)

        @pl.when(lax.rem(step, per) == 0)
        def _():
            start_fetch(step)

        for copy in fetch(0, 0, side):
            copy.wait()

        @pl.when(lax.rem(step + 1, per) != 0)
        def _():
            start_fetch(step + 1)

        trio = forward_units(two[side], up[side], wide, down)
        add(side, trio)
        return carry

    lax.fori_loop(per, steps, body, 0)
    mail_wait(1)
    mail_start(2)
    wide[...] = acc[0:2].astype(LOW)
    copies = load([(wide, wide_grad)], outs)
    mail_wait(2)
    group_start()
    down[...] = acc[2].astype(LOW)
    copies += load([(down, down_grad)], outs.at[pl.ds(1, 1)])
    second_sum.stage(3)
    layer_end()
    group_wait()
    for copy in copies:
        copy.wait()


def last(mix_part, down_part, tokens, resid, resid_back, gains, sums, bias_term,
         two_all, up_all, saved, two_far, up_far, up_one, two_one, wide, down):
    total, width = two_all.shape
    rows = tokens.shape[0]
    local = down.shape[0]
    groups = lax.axis_size("grp")
    tall = (((total, width), LOW), ANY)
    block = (((rows, width), LOW), VM)
    return call(
        last_kernel,
        8,
        [(mix_part, ANY), (down_part, ANY)]
        + [(item, VM) for item in (tokens, resid, resid_back, gains, sums, bias_term)]
        + [(item, ANY) for item in (two_all, up_all, saved, two_far, up_far, up_one, two_one, wide, down)],
        [
            block,
            block,
            (((8, width), WIDE), VM),
            (((2, local, width), LOW), ANY),
            (((local, width), LOW), ANY),
            tall, tall, tall, tall,
        ],
        [
            pltpu.VMEM((2, TILE, width), LOW),
            pltpu.VMEM((2, TILE, width), LOW),
            pltpu.VMEM((2, 3, local, TILE), LOW),
            pltpu.VMEM((2, local, width), LOW),
            pltpu.VMEM((local, width), LOW),
            pltpu.VMEM((3, local, width), WIDE),
            pltpu.VMEM((2 + groups, 8, width), WIDE),
            pltpu.VMEM((4, 8, width), WIDE),
            pltpu.SemaphoreType.DMA((3, 3)),
            pltpu.SemaphoreType.DMA((2,)),
            pltpu.SemaphoreType.DMA((2 + groups,)),
            pltpu.SemaphoreType.DMA((2 + groups,)),
        ]
        + scatter_scratch(rows, width) * 2
        + gather_sems() * N_LAST_GATHERS,
        limit=62,
        flops=72 << 30,
        cost=120 << 20,
    )


RING = 8


def rope_tables(place):
    half = ROT // 2
    freq = BASE ** (-jnp.arange(half, dtype=jnp.float32) / half)
    angle = place.astype(jnp.float32)[:, None] * freq[None, :]
    cosine, sine = lax.optimization_barrier((jnp.cos(angle), jnp.sin(angle)))
    lane = jnp.arange(128) % HEAD_DIM
    cosine = jnp.where(lane < ROT, jnp.tile(cosine, (1, 128 // half)), 1.0)
    sine = jnp.tile(sine, (1, 128 // half))
    return jnp.stack(
        [
            cosine,
            jnp.where((lane >= half) & (lane < ROT), sine, 0.0),
            jnp.where(lane < half, -sine, 0.0),
        ]
    )


def on_device(
    tokens,
    norm_gains,
    norm_biases,
    mix_weight,
    mix_bias,
    out_weight,
    gate_up_weight,
    down_weight,
    row_lengths,
    row_group,
    cotangent,
):
    count = lax.axis_size("seq")
    shard = lax.axis_index("seq")
    group = lax.axis_index("grp")
    slots_dev = tokens.shape[0]
    group_slots = slots_dev * count
    label_all, place_all = slot_rows(
        row_lengths, row_group, group, jnp.arange(group_slots, dtype=jnp.int32)
    )
    label_mine = lax.dynamic_slice_in_dim(label_all, shard * slots_dev, slots_dev, 0)
    upstream = jnp.where(label_mine[:, None] >= 0, cotangent, jnp.zeros_like(cotangent))
    lab_col, lab_row = label_all[:, None], label_all[None, :]
    tables = rope_tables(place_all)
    mix_t = jnp.transpose(mix_weight, (1, 0, 2))
    wide_t = jnp.transpose(gate_up_weight, (1, 2, 0))

    up_far = lax.all_gather(upstream, "grp", axis=0, tiled=True)
    normed_all = first(tokens, norm_gains, norm_biases, count)
    query, key, value, attended, lse, part, up_all = attend_heads(
        normed_all, mix_t, out_weight, mix_bias.astype(jnp.float32), tables, lab_col, lab_row, upstream
    )
    resid, two_all, two_mine = second(part, tokens, norm_gains, norm_biases, count)
    two_far = lax.all_gather(two_mine, "grp", axis=0, tiled=True)
    back_part, down_part, saved, up_one = feed(two_all, up_all, wide_t, down_weight, up_far)
    resid_back, branch_all, sums = third(back_part, resid, upstream, norm_gains, count)
    mix_part, mix_term, out_term, bias_term, two_one = attend_heads_back(
        branch_all, normed_all, mix_t, out_weight, tables, lab_col, lab_row,
        (query, key, value, attended, lse), two_far,
    )
    mix_grad, out_grad = lax.psum((mix_term, out_term), "grp")
    tokens_grad, layer_out, four, wide_grad, down_grad = last(
        mix_part, down_part, tokens, resid, resid_back, norm_gains, sums, bias_term,
        two_all, up_all, saved, two_far, up_far, up_one, two_one, wide_t, down_weight,
    )[:5]
    local = mix_bias.shape[1]
    return (
        layer_out,
        tokens_grad,
        four[0:2],
        four[2:4],
        jnp.transpose(mix_grad, (1, 0, 2)).astype(jnp.float32),
        four[4, : 3 * local].reshape(3, local),
        out_grad.astype(jnp.float32),
        jnp.transpose(wide_grad, (2, 0, 1)).astype(jnp.float32),
        down_grad.astype(jnp.float32),
    )


def solution(mesh):
    placed = (
        P(("grp", "seq"), None),
        P(),
        P(),
        P(None, None, "seq"),
        P(None, "seq"),
        P("seq", None),
        P(None, None, "seq"),
        P("seq", None),
        P(),
        P(),
        P(("grp", "seq"), None),
    )
    return jax.shard_map(
        on_device if mesh.shape["seq"] == RING else plain_device,
        mesh=mesh,
        in_specs=placed,
        out_specs=(
            P(("grp", "seq"), None),
            P(("grp", "seq"), None),
            P(),
            P(),
            P(None, None, "seq"),
            P(None, "seq"),
            P("seq", None),
            P(None, None, "seq"),
            P("seq", None),
        ),
        check_vma=False,
    )
```

```python
import functools
import math

import jax
import jax.numpy as jnp
from jax import lax
from jax.experimental import pallas as pl
from jax.experimental.pallas import tpu as pltpu
from jax.sharding import PartitionSpec as P

HEAD_DIM = 64
ROT = 16


EPS = 1e-05
NEG = -1e30
BASE = 10000.0


def layer_norm(values, gain, bias):
    centered = values - jnp.mean(values, axis=-1, keepdims=True)
    scale = lax.rsqrt(jnp.mean(centered * centered, axis=-1, keepdims=True) + EPS)
    unit = centered * scale
    return (unit * gain + bias, unit, scale)


def norm_back(incoming, unit, scale, gain):
    along = incoming * gain
    inner = jnp.mean(along, axis=-1, keepdims=True)
    cross = jnp.mean(along * unit, axis=-1, keepdims=True)
    return (
        scale * (along - inner - unit * cross),
        jnp.sum(incoming * unit, axis=0),
        jnp.sum(incoming, axis=0),
    )


def rotate(values, where, sign):
    half = ROT // 2
    freq = BASE ** (-jnp.arange(half, dtype=jnp.float32) / half)
    angle = where.astype(jnp.float32)[:, None] * freq[None, :]
    cosine = jnp.cos(angle)[:, None, :]
    sine = sign * jnp.sin(angle)[:, None, :]
    first = values[..., :half]
    second = values[..., half:ROT]
    return jnp.concatenate(
        [first * cosine - second * sine, second * cosine + first * sine, values[..., ROT:]], axis=-1
    )


def unrotate(lowered, where):
    wide = lowered.astype(jnp.float32)
    turned = jnp.stack(
        [rotate(wide[:, 0], where, -1.0), rotate(wide[:, 1], where, -1.0), wide[:, 2]], axis=1
    )
    return turned.reshape(lowered.shape[0], 3, -1).astype(jnp.bfloat16)


def slot_rows(row_lengths, row_group, group, slots):
    order = jnp.arange(row_lengths.shape[0], dtype=jnp.int32)
    same = row_group == group
    earlier = (order[:, None] > order[None, :]) & same[None, :]
    begin = jnp.sum(jnp.where(earlier, row_lengths[None, :], 0), axis=1)
    finish = begin + row_lengths
    inside = same[None, :] & (slots[:, None] >= begin[None, :]) & (slots[:, None] < finish[None, :])
    label = jnp.sum(jnp.where(inside, order[None, :] + 1, 0), axis=1) - 1
    offset = jnp.sum(jnp.where(inside, slots[:, None] - begin[None, :], 0), axis=1)
    load = jnp.sum(jnp.where(same, row_lengths, 0))
    return (label, jnp.where(label < 0, slots - load, offset))


def block_scores(query, key, label, start, block):
    part = lax.dynamic_slice_in_dim(query, start, block, 0)
    rows = start + jnp.arange(block, dtype=jnp.int32)
    columns = jnp.arange(label.shape[0], dtype=jnp.int32)
    label_rows = lax.dynamic_slice_in_dim(label, start, block, 0)
    allowed = (label_rows[:, None] == label[None, :]) & (rows[:, None] >= columns[None, :])
    scores = jnp.einsum("qhe,khe->hqk", part, key, preferred_element_type=jnp.float32) * (
        1.0 / math.sqrt(query.shape[-1])
    )
    return (part, jnp.where(allowed[None], scores, NEG))


def attend(query, key, value, label, block):

    def one_block(index):
        part, scores = block_scores(query, key, label, index * block, block)
        top = jnp.max(scores, axis=-1, keepdims=True)
        weights = jnp.exp(scores - top)
        totals = jnp.sum(weights, axis=-1, keepdims=True)
        probs = (weights / totals).astype(jnp.bfloat16)
        mixed = jnp.einsum("hqk,khe->qhe", probs, value, preferred_element_type=jnp.float32)
        return (mixed, top[..., 0] + jnp.log(totals[..., 0]))

    mixed, log_totals = lax.map(one_block, jnp.arange(query.shape[0] // block, dtype=jnp.int32))
    return (mixed.reshape(query.shape), log_totals)


def attend_back(query, key, value, label, log_totals, mixed_back, block):
    scale = 1.0 / math.sqrt(query.shape[-1])

    def one_block(carry, index):
        key_back, value_back = carry
        start = index * block
        part, scores = block_scores(query, key, label, start, block)
        back_part = lax.dynamic_slice_in_dim(mixed_back, start, block, 0)
        probs = jnp.exp(scores - log_totals[index][..., None])
        value_back = value_back + jnp.einsum(
            "hqk,qhe->khe",
            probs.astype(jnp.bfloat16),
            back_part,
            preferred_element_type=jnp.float32,
        )
        probs_back = jnp.einsum(
            "qhe,khe->hqk", back_part, value, preferred_element_type=jnp.float32
        )
        inner = jnp.sum(probs_back * probs, axis=-1, keepdims=True)
        score_back = (probs * (probs_back - inner)).astype(jnp.bfloat16)
        query_back = (
            jnp.einsum("hqk,khe->qhe", score_back, key, preferred_element_type=jnp.float32) * scale
        )
        key_back = (
            key_back
            + jnp.einsum("hqk,qhe->khe", score_back, part, preferred_element_type=jnp.float32)
            * scale
        )
        return ((key_back, value_back), query_back)

    empty = jnp.zeros(key.shape, jnp.float32)
    (key_back, value_back), query_back = lax.scan(
        one_block, (empty, empty), jnp.arange(query.shape[0] // block, dtype=jnp.int32)
    )
    return (query_back.reshape(query.shape), key_back, value_back)


def silu_parts(gate_up):
    gate = gate_up[:, 0]
    upper = gate_up[:, 1]
    sigma = jax.nn.sigmoid(gate)
    return (gate * sigma * upper, gate, upper, sigma)


def gate_back(hidden_back, gate, upper, sigma):
    gate_part = hidden_back * upper * sigma * (1.0 + gate * (1.0 - sigma))
    up_part = hidden_back * gate * sigma
    return jnp.stack([gate_part, up_part], axis=1).astype(jnp.bfloat16)


def gather_rows(values):
    return lax.all_gather(values, "seq", axis=0, tiled=True)


def summed_rows(product, left):
    return lax.psum_scatter(
        product(left).astype(jnp.bfloat16), "seq", scatter_dimension=0, tiled=True
    ).astype(jnp.float32)


def plain_device(
    tokens,
    norm_gains,
    norm_biases,
    mix_weight,
    mix_bias,
    out_weight,
    gate_up_weight,
    down_weight,
    row_lengths,
    row_group,
    cotangent,
):
    seq_count = lax.axis_size("seq")
    shard = lax.axis_index("seq")
    group = lax.axis_index("grp")
    slots_dev = tokens.shape[0]
    width = tokens.shape[1]
    group_slots = slots_dev * seq_count
    block = min(512, group_slots)
    local_width = width // seq_count
    local_heads = local_width // HEAD_DIM
    mine = shard * slots_dev + jnp.arange(slots_dev, dtype=jnp.int32)
    label_mine, place_mine = slot_rows(row_lengths, row_group, group, mine)
    label_all, place_all = slot_rows(
        row_lengths, row_group, group, jnp.arange(group_slots, dtype=jnp.int32)
    )
    inputs = tokens.astype(jnp.float32)
    upstream = cotangent.astype(jnp.float32) * (label_mine >= 0).astype(jnp.float32)[:, None]
    upstream_low = upstream.astype(jnp.bfloat16)
    normed, unit_one, scale_one = layer_norm(inputs, norm_gains[0], norm_biases[0])
    normed_all = gather_rows(normed.astype(jnp.bfloat16))
    up_four = lax.all_gather(upstream_low, ("grp", "seq"), axis=0, tiled=True)
    upstream_all = lax.dynamic_slice_in_dim(up_four, group * group_slots, group_slots, 0)
    mixin = jnp.einsum(
        "td,dcf->tcf", normed_all, mix_weight, preferred_element_type=jnp.float32
    ) + mix_bias.astype(jnp.float32)
    heads_in = mixin.reshape(group_slots, 3, local_heads, HEAD_DIM)
    query = rotate(heads_in[:, 0], place_all, 1.0).astype(jnp.bfloat16)
    key = rotate(heads_in[:, 1], place_all, 1.0).astype(jnp.bfloat16)
    value = heads_in[:, 2].astype(jnp.bfloat16)
    mixed, log_totals = attend(query, key, value, label_all, block)
    attended = mixed.reshape(group_slots, local_width).astype(jnp.bfloat16)

    def out_product(part):
        return jnp.dot(part, out_weight, preferred_element_type=jnp.float32)

    resid = inputs + summed_rows(out_product, attended)
    normed_two, unit_two, scale_two = layer_norm(resid, norm_gains[1], norm_biases[1])
    normed_two_low = normed_two.astype(jnp.bfloat16)
    normed_two_all = gather_rows(normed_two_low)
    two_four = lax.all_gather(normed_two_low, ("grp", "seq"), axis=0, tiled=True)

    def up_to_back(two, up):
        gate_up = jnp.einsum("td,dcf->tcf", two, gate_up_weight, preferred_element_type=jnp.float32)
        hidden, gate, upper, sigma = silu_parts(gate_up)
        hidden_back = jnp.einsum("td,fd->tf", up, down_weight, preferred_element_type=jnp.float32)
        return hidden.astype(jnp.bfloat16), gate_back(hidden_back, gate, upper, sigma)

    hidden_low, gate_up_back = up_to_back(normed_two_all, upstream_all)

    def down_product(part):
        return jnp.dot(part, down_weight, preferred_element_type=jnp.float32)

    layer_out = resid + summed_rows(down_product, hidden_low)

    def gate_up_product(part):
        return jnp.einsum("tcf,dcf->td", part, gate_up_weight, preferred_element_type=jnp.float32)

    normed_two_back = summed_rows(gate_up_product, gate_up_back)
    hidden_four, back_four = up_to_back(two_four, up_four)
    down_grad = jnp.einsum("tf,td->fd", hidden_four, up_four, preferred_element_type=jnp.float32)
    gate_up_grad = jnp.einsum(
        "td,tcf->dcf", two_four, back_four, preferred_element_type=jnp.float32
    )
    resid_part, gain_two, bias_two = norm_back(normed_two_back, unit_two, scale_two, norm_gains[1])
    resid_back = upstream + resid_part
    branch_all = gather_rows(resid_back.astype(jnp.bfloat16))
    out_term = jnp.einsum("te,td->ed", attended, branch_all, preferred_element_type=jnp.float32)
    out_grad = lax.psum(out_term.astype(jnp.bfloat16), "grp").astype(jnp.float32)
    attended_back = jnp.einsum(
        "td,ed->te", branch_all, out_weight, preferred_element_type=jnp.float32
    ).astype(jnp.bfloat16)
    heads_back = attended_back.reshape(group_slots, local_heads, HEAD_DIM)
    query_back, key_back, value_back = attend_back(
        query, key, value, label_all, log_totals, heads_back, block
    )
    lowered = jnp.stack([query_back, key_back, value_back], axis=1).astype(jnp.bfloat16)
    mixin_back = unrotate(lowered, place_all)
    mix_term = jnp.einsum("td,tcf->dcf", normed_all, mixin_back, preferred_element_type=jnp.float32)
    mix_grad = lax.psum(mix_term.astype(jnp.bfloat16), "grp").astype(jnp.float32)
    bias_term = jnp.sum(mixin_back, axis=0, dtype=jnp.float32)
    mix_bias_grad = lax.psum(bias_term, "grp")

    def mix_product(part):
        return jnp.einsum("tcf,dcf->td", part, mix_weight, preferred_element_type=jnp.float32)

    normed_back = summed_rows(mix_product, mixin_back)
    tokens_part, gain_one, bias_one = norm_back(normed_back, unit_one, scale_one, norm_gains[0])
    tokens_grad = (resid_back + tokens_part).astype(jnp.bfloat16)
    gains_grad, biases_grad = lax.psum(
        (jnp.stack([gain_one, gain_two]), jnp.stack([bias_one, bias_two])), ("grp", "seq")
    )
    return (
        layer_out.astype(jnp.bfloat16),
        tokens_grad,
        gains_grad,
        biases_grad,
        mix_grad,
        mix_bias_grad,
        out_grad,
        gate_up_grad,
        down_grad,
    )


MESH_ID = pl.DeviceIdType.MESH
N_RS = 10
N_AG = 13


class Ring:
    def __init__(self):
        self.group = lax.axis_index("grp")
        self.me = lax.axis_index("seq")
        core = self.me % 2
        x = (self.me // 2) % 2
        y = self.me // 4
        self.flip = 1 - 2 * core
        self.twin = self.me + self.flip
        self.xn = self.me + 2 - 4 * x
        self.yn = self.me + 4 - 8 * y
        self.dn = self.xn + 4 - 8 * y

    def dev(self, seq):
        return (self.group, seq)

    def greet(self, extra=()):
        sem = pltpu.get_barrier_semaphore()
        peers = [self.dev(self.twin), self.dev(self.xn), self.dev(self.yn)] + list(extra)
        for peer in peers:
            pl.semaphore_signal(sem, inc=1, device_id=peer, device_id_type=MESH_ID)
        return lambda: pl.semaphore_wait(sem, len(peers))

    def barrier(self, extra=()):
        self.greet(extra)()

    def chips(self):
        return [self.dn // 2, self.xn // 2, self.yn // 2, self.me // 2]

    def copy(self, src, dst, send, recv, kind, seq):
        return pltpu.make_async_remote_copy(
            src_ref=src,
            dst_ref=dst,
            send_sem=send.at[kind],
            recv_sem=recv.at[kind],
            device_id=self.dev(seq),
            device_id_type=MESH_ID,
        )


class Line:
    def __init__(self, ring, send, recv):
        self.ring, self.send, self.recv = ring, send, recv
        self.groups = lax.axis_size("grp")
        self.peers = [(self.away(k), ring.me) for k in range(1, self.groups)]

    def away(self, k):
        return lax.rem(self.ring.group + k, self.groups)

    def copy(self, k, src, dst):
        return pltpu.make_async_remote_copy(
            src_ref=src,
            dst_ref=dst,
            send_sem=self.send.at[k - 1],
            recv_sem=self.recv.at[k - 1],
            device_id=self.peers[k - 1],
            device_id_type=MESH_ID,
        )


def line_sems():
    return [pltpu.SemaphoreType.DMA((lax.axis_size("grp"),)), pltpu.SemaphoreType.DMA((lax.axis_size("grp"),))]


class Gather:
    def __init__(self, ring, own, out, send, recv, local):
        self.ring, self.own, self.out = ring, own, out
        self.send, self.recv, self.local = send, recv, local
        self.rows = own.shape[0]
        self.half = self.rows // 2

    def at(self, block, part=None):
        rows, half = self.rows, self.half
        if part is None:
            return self.out.at[pl.ds(pl.multiple_of(block * rows, rows), rows), :]
        return self.out.at[pl.ds(pl.multiple_of(block * rows + part * half, half), half), :]

    def copy(self, kind):
        ring, half = self.ring, self.half
        if kind < 4:
            part, seq = ((0, ring.xn), (1, ring.yn), (1, ring.xn), (0, ring.yn))[kind]
            src, dst = self.own.at[pl.ds(part * half, half), :], self.at(ring.me, part)
        elif kind == 4:
            src, dst, seq = self.own, self.at(ring.me), ring.twin
        else:
            block, part, seq = (
                (ring.xn, 0, ring.yn),
                (ring.xn, 0, ring.twin),
                (ring.yn, 1, ring.xn),
                (ring.yn, 1, ring.twin),
                (ring.xn, 1, ring.twin),
                (ring.yn, 0, ring.twin),
                (ring.dn, 0, ring.twin),
                (ring.dn, 1, ring.twin),
            )[kind - 5]
            src = dst = self.at(block, part)
        return ring.copy(src, dst, self.send, self.recv, kind, seq)

    def keep(self):
        return pltpu.make_async_copy(self.own, self.at(self.ring.me), self.local)

    def stage(self, number):
        if number == 0:
            self.keep().start()
            for kind in range(5):
                self.copy(kind).start()
        elif number == 1:
            self.copy(0).wait_recv()
            self.copy(5).start()
            self.copy(6).start()
            self.copy(1).wait_recv()
            self.copy(7).start()
            self.copy(8).start()
        elif number == 2:
            self.copy(2).wait_recv()
            self.copy(9).start()
            self.copy(3).wait_recv()
            self.copy(10).start()
        elif number == 3:
            self.copy(5).wait_recv()
            self.copy(11).start()
            self.copy(7).wait_recv()
            self.copy(12).start()
        else:
            self.arrive(4, 6, 8, 9, 10, 11, 12)
            self.close()

    def arrive(self, *kinds):
        for kind in kinds:
            self.copy(kind).wait_recv()

    def close_sends(self):
        for kind in range(N_AG):
            self.copy(kind).wait_send()

    def close(self):
        self.keep().wait()
        self.close_sends()

    def all(self):
        for number in range(5):
            self.stage(number)


class Scatter:
    def __init__(self, ring, part, total, own, pair, rx, ry, fx, fy, mid, send, recv, local):
        self.ring, self.part, self.total = ring, part, total
        self.own, self.pair, self.rx, self.ry = own, pair, rx, ry
        self.fx, self.fy, self.mid = fx, fy, mid
        self.send, self.recv, self.local = send, recv, local
        self.rows, self.width = total.shape

    def block(self, index):
        return self.part.at[pl.ds(pl.multiple_of(index * self.rows, self.rows), self.rows), :]

    def index(self, slot):
        ring = self.ring
        return (ring.dn, ring.xn, ring.yn, ring.me)[slot]

    def keep(self, slot):
        return pltpu.make_async_copy(self.block(self.index(slot)), self.own.at[slot], self.local.at[slot])

    def copy(self, kind):
        ring, half = self.ring, self.width // 2
        lo, hi = pl.ds(0, half), pl.ds(half, half)
        if kind < 4:
            src, dst, seq = self.block(self.index(kind) + ring.flip), self.pair.at[kind], ring.twin
        else:
            src, dst, seq = (
                (self.own.at[0, :, lo], self.rx.at[0], ring.xn),
                (self.own.at[0, :, hi], self.ry.at[0], ring.yn),
                (self.own.at[1, :, lo], self.rx.at[1], ring.xn),
                (self.own.at[2, :, hi], self.ry.at[1], ring.yn),
                (self.mid.at[0], self.fy, ring.yn),
                (self.mid.at[1], self.fx, ring.xn),
            )[kind - 4]
        return ring.copy(src, dst, self.send, self.recv, kind, seq)

    def added(self, slot):
        self.keep(slot).wait()
        self.copy(slot).wait_recv()
        return self.own[slot].astype(jnp.float32) + self.pair[slot].astype(jnp.float32)

    def stage(self, number):
        wide, low, half = jnp.float32, self.own.dtype, self.width // 2
        lo, hi = pl.ds(0, half), pl.ds(half, half)
        own, total = self.own, self.total
        if number == 0:
            for slot in range(4):
                self.copy(slot).start()
                self.keep(slot).start()
        elif number == 1:
            own[0] = self.added(0).astype(low)
            self.copy(4).start()
            self.copy(5).start()
            own[1] = self.added(1).astype(low)
            self.copy(6).start()
            own[2] = self.added(2).astype(low)
            self.copy(7).start()
            total[...] = self.added(3)
        elif number == 2:
            self.copy(4).wait_recv()
            self.mid[0] = (own[2, :, lo].astype(wide) + self.rx[0].astype(wide)).astype(low)
            self.copy(8).start()
            self.copy(5).wait_recv()
            self.mid[1] = (own[1, :, hi].astype(wide) + self.ry[0].astype(wide)).astype(low)
            self.copy(9).start()
        else:
            self.copy(6).wait_recv()
            total[:, lo] += self.rx[1].astype(wide)
            self.copy(7).wait_recv()
            total[:, hi] += self.ry[1].astype(wide)
            self.copy(8).wait_recv()
            total[:, lo] += self.fy[...].astype(wide)
            self.copy(9).wait_recv()
            total[:, hi] += self.fx[...].astype(wide)
            for kind in range(N_RS):
                self.copy(kind).wait_send()

    def all(self):
        for number in range(4):
            self.stage(number)


class Stream:
    def __init__(self, ring, tiles, total, pair, rx, ry, fx, fy, mid, send, recv):
        self.ring, self.tiles, self.total, self.pair = ring, tiles, total, pair
        self.rx, self.ry, self.fx, self.fy, self.mid = rx, ry, fx, fy, mid
        self.send, self.recv = send, recv
        self.rows, self.width = total.shape
        self.at = ring.chips()

    def rows_of(self, twin):
        core = self.ring.me % 2
        core = 1 - core if twin else core
        return pl.ds(pl.multiple_of(core * self.rows, self.rows), self.rows)

    def copy(self, kind):
        ring, half = self.ring, self.width // 2
        lo, hi = pl.ds(0, half), pl.ds(half, half)
        mine = self.rows_of(False)
        dn, xn, yn, _ = self.at
        src, dst, seq = (
            (self.tiles.at[dn, mine, lo], self.rx.at[0], ring.xn),
            (self.tiles.at[dn, mine, hi], self.ry.at[0], ring.yn),
            (self.tiles.at[xn, mine, lo], self.rx.at[1], ring.xn),
            (self.tiles.at[yn, mine, hi], self.ry.at[1], ring.yn),
            (self.mid.at[0], self.fy, ring.yn),
            (self.mid.at[1], self.fx, ring.xn),
        )[kind - 4]
        return ring.copy(src, dst, self.send, self.recv, kind, seq)

    def pair_copy(self, chip):
        return self.ring.copy(
            self.tiles.at[chip, self.rows_of(True), :],
            self.pair.at[chip],
            self.send,
            self.recv,
            chip,
            self.ring.twin,
        )

    def ready(self, chip):
        self.pair_copy(chip).start()

    def added(self, chip):
        self.pair_copy(chip).wait_recv()
        mine = self.rows_of(False)
        return self.tiles[chip, mine, :].astype(jnp.float32) + self.pair[chip].astype(jnp.float32)

    def go(self, which):
        chip = self.at[which]
        self.tiles[chip, self.rows_of(False), :] = self.added(chip).astype(self.tiles.dtype)
        for kind in ((4, 5), (6,), (7,))[which]:
            self.copy(kind).start()

    def cross(self):
        wide, low, half = jnp.float32, self.tiles.dtype, self.width // 2
        lo, hi = pl.ds(0, half), pl.ds(half, half)
        mine = self.rows_of(False)
        _, xn, yn, _ = self.at
        self.copy(4).wait_recv()
        self.mid[0] = (self.tiles[yn, mine, lo].astype(wide) + self.rx[0].astype(wide)).astype(low)
        self.copy(8).start()
        self.copy(5).wait_recv()
        self.mid[1] = (self.tiles[xn, mine, hi].astype(wide) + self.ry[0].astype(wide)).astype(low)
        self.copy(9).start()

    def finish(self):
        wide, half = jnp.float32, self.width // 2
        lo, hi = pl.ds(0, half), pl.ds(half, half)
        total = self.total
        total[...] = self.added(self.at[3])
        self.copy(6).wait_recv()
        total[:, lo] += self.rx[1].astype(wide)
        self.copy(7).wait_recv()
        total[:, hi] += self.ry[1].astype(wide)
        self.copy(8).wait_recv()
        total[:, lo] += self.fy[...].astype(wide)
        self.copy(9).wait_recv()
        total[:, hi] += self.fx[...].astype(wide)

    def close(self):
        for chip in range(4):
            self.pair_copy(chip).wait_send()
        for kind in range(4, N_RS):
            self.copy(kind).wait_send()


def stream_scratch(rows, width):
    low = jnp.bfloat16
    half = width // 2
    return [
        pltpu.VMEM((4, 2 * rows, width), low),
        pltpu.VMEM((rows, width), jnp.float32),
        pltpu.VMEM((4, rows, width), low),
        pltpu.VMEM((2, rows, half), low),
        pltpu.VMEM((2, rows, half), low),
        pltpu.VMEM((rows, half), low),
        pltpu.VMEM((rows, half), low),
        pltpu.VMEM((2, rows, half), low),
        pltpu.SemaphoreType.DMA((N_RS,)),
        pltpu.SemaphoreType.DMA((N_RS,)),
    ]


N_STREAM = 10


def scatter_buffers(rows, width):
    low = jnp.bfloat16
    half = width // 2
    return [
        pltpu.VMEM((rows, width), jnp.float32),
        pltpu.VMEM((4, rows, width), low),
        pltpu.VMEM((4, rows, width), low),
        pltpu.VMEM((2, rows, half), low),
        pltpu.VMEM((2, rows, half), low),
        pltpu.VMEM((rows, half), low),
        pltpu.VMEM((rows, half), low),
        pltpu.VMEM((2, rows, half), low),
    ]


def scatter_sems():
    return [
        pltpu.SemaphoreType.DMA((N_RS,)),
        pltpu.SemaphoreType.DMA((N_RS,)),
        pltpu.SemaphoreType.DMA((4,)),
    ]


def scatter_scratch(rows, width):
    return scatter_buffers(rows, width) + scatter_sems()


def gather_sems():
    return [
        pltpu.SemaphoreType.DMA((N_AG,)),
        pltpu.SemaphoreType.DMA((N_AG,)),
        pltpu.SemaphoreType.DMA,
    ]


def gather_scratch(rows, width):
    return [pltpu.VMEM((rows, width), jnp.bfloat16)] + gather_sems()


def unit_of(values):
    centered = values - jnp.mean(values, axis=-1, keepdims=True)
    scale = lax.rsqrt(jnp.mean(centered * centered, axis=-1, keepdims=True) + EPS)
    return centered * scale, scale


def back_of(incoming, unit, scale, gain):
    along = incoming * gain
    inner = jnp.mean(along, axis=-1, keepdims=True)
    cross = jnp.mean(along * unit, axis=-1, keepdims=True)
    return scale * (along - inner - unit * cross)


VM = pl.BlockSpec(memory_space=pltpu.VMEM)
ANY = pl.BlockSpec(memory_space=pltpu.HBM)
SM = pl.BlockSpec(memory_space=pltpu.SMEM)


def call(kernel, number, ins, outs, scratch, limit=60, flops=0, cost=20_000_000, scratch_in=None):
    return pl.pallas_call(
        kernel,
        out_shape=tuple(jax.ShapeDtypeStruct(*shape) for shape, _ in outs),
        in_specs=[spec for _, spec in ins],
        out_specs=tuple(spec for _, spec in outs),
        scratch_shapes=scratch,
        compiler_params=pltpu.CompilerParams(
            collective_id=number,
            has_side_effects=True,
            vmem_limit_bytes=limit << 20,
        ),
        cost_estimate=pl.CostEstimate(flops=flops, bytes_accessed=cost, transcendentals=0),
    )(*[value for value, _ in ins])


TILE = 256
WIDE = jnp.float32
LOW = jnp.bfloat16
NT = (((1,), (1,)), ((), ()))
TN = (((0,), (0,)), ((), ()))


def mm(a, b, dims=(((1,), (0,)), ((), ()))):
    return lax.dot_general(a, b, dims, preferred_element_type=WIDE)


def far_rows(far, ring, away, total):
    groups = lax.axis_size("grp")
    rows = far.shape[0] // groups
    index = lax.rem(ring.group + away, groups)
    return far.at[pl.ds(pl.multiple_of(index * rows, rows), rows), :]


def head_lanes(shape, head):
    return lax.broadcasted_iota(jnp.int32, shape, 1) // HEAD_DIM == head


def turn(u, tables, rows, sign):
    cosine, below, above = (
        jnp.concatenate([tables[i, rows, :]] * (u.shape[1] // 128), axis=1) for i in range(3)
    )
    side = pltpu.roll(u, 8, 1) * below + pltpu.roll(u, u.shape[1] - 8, 1) * above
    return u * cosine + side if sign > 0 else u * cosine - side


def load(pairs, sems):
    copies = []
    for i, (src, dst) in enumerate(pairs):
        copy = pltpu.make_async_copy(src, dst, sems.at[i])
        copy.start()
        copies.append(copy)
    return copies


def rows_layout(row_lengths, row_group, group, tables, lab_col, lab_row):
    total = lab_col.shape[0]
    rows, begin = [], jnp.int32(0)
    for row in range(row_lengths.shape[0]):
        mine = row_group[row] == group
        rows.append((row, mine, begin, begin + row_lengths[row]))
        begin = begin + jnp.where(mine, row_lengths[row], 0)

    def lay(slots):
        label, base = jnp.full(slots.shape, -1, jnp.int32), jnp.full(slots.shape, begin, jnp.int32)
        for row, mine, first, end in rows:
            first, end = jnp.where(mine, first, -1), jnp.where(mine, end, -1)
            inside = (slots >= first) & (slots < end)
            label = jnp.where(inside, row, label)
            base = jnp.where(inside, first, base)
        return label, slots - base

    lab_row[...] = lay(lax.broadcasted_iota(jnp.int32, (1, total), 1))[0]
    half = ROT // 2

    def body(i, carry):
        at = pl.ds(pl.multiple_of(i * TILE, TILE), TILE)
        label, place = lay(i * TILE + lax.broadcasted_iota(jnp.int32, (TILE, 1), 0))
        lab_col[at, :] = label
        lane = lax.broadcasted_iota(jnp.int32, (TILE, 128), 1) % HEAD_DIM
        freq = jnp.ones((TILE, 128), WIDE)
        for e in range(1, half):
            freq = jnp.where(lane % half == e, BASE ** (-e / half), freq)
        angle = place.astype(WIDE) * freq
        cosine, sine = jnp.cos(angle), jnp.sin(angle)
        tables[0, at, :] = jnp.where(lane < ROT, cosine, 1.0)
        tables[1, at, :] = jnp.where((lane >= half) & (lane < ROT), sine, 0.0)
        tables[2, at, :] = jnp.where(lane < half, -sine, 0.0)
        return carry

    lax.fori_loop(0, total // TILE, body, 0)


def attend_kernel(
    row_lengths, row_group, tokens, gains, biases, upstream, weight, out_weight, bias,
    query, key, value, attended, lse, normed_all, up_all, resid, two_all, two_own, tables, lab_col, lab_row,
    normed, own, w, mask, stats, sems, *scratch,
):
    total, width = query.shape
    tiles = total // TILE
    ring = Ring()
    met = ring.greet()
    copy_w = pltpu.make_async_copy(weight, w, sems.at[0])
    copy_w.start()
    stream = Stream(ring, *scratch[:N_STREAM])
    scratch = scratch[N_STREAM:]
    gather = Gather(ring, own, normed, *scratch[0:3])
    upper = Gather(ring, upstream, up_all, *scratch[3:6])
    after = Gather(ring, two_own, two_all, *scratch[6:9])
    unit, _ = unit_of(tokens[...].astype(WIDE))
    own[...] = (unit * gains[0:1] + biases[0:1]).astype(LOW)
    met()
    gather.stage(0)
    rows_layout(row_lengths, row_group, ring.group, tables, lab_col, lab_row)
    gather.keep().wait()
    copy_w.wait()

    def mix(chip):
        rows = pl.ds(pl.multiple_of(chip * TILE, TILE), TILE)
        x = normed[rows, :]
        u = mm(x, w[0]) + bias[0:1].astype(WIDE)
        query[rows, :] = (turn(u, tables, rows, 1).astype(LOW).astype(WIDE) * (1.0 / 8)).astype(LOW)
        u = mm(x, w[1]) + bias[1:2].astype(WIDE)
        key[rows, :] = turn(u, tables, rows, 1).astype(LOW)
        value[rows, :] = (mm(x, w[2]) + bias[2:3].astype(WIDE)).astype(LOW)

    chips = ring.chips()

    def mix_body(step, carry):
        for i, acts in enumerate(
            (
                ((4,), ()),
                ((6, 9), (1, 2)),
                ((8, 10), (3,)),
                ((11, 12), ()),
            )
        ):

            @pl.when(step == i)
            def _():
                for number in acts[1]:
                    gather.stage(number)
                if i == 2:
                    upper.stage(0)
                gather.arrive(*acts[0])

        chip = chips[0]
        for i in range(1, tiles):
            chip = jnp.where(step == tiles - 1 - i, chips[(3, 1, 2)[tiles - 1 - i]], chip)
        mix(chip)
        return carry

    lax.fori_loop(0, tiles, mix_body, 0)
    keep = pltpu.make_async_copy(normed, normed_all, sems.at[1])
    keep.start()
    for i in range(tiles):
        rows = pl.ds(i * TILE, TILE)
        span = (i + 1) * TILE
        q_at = i * TILE + lax.broadcasted_iota(jnp.int32, (TILE, span), 0)
        k_at = lax.broadcasted_iota(jnp.int32, (TILE, span), 1)
        allowed = (lab_col[rows, :] == lab_row[:, :span]) & (q_at >= k_at)
        mask[:, :span] = jnp.where(allowed, 0.0, NEG)
        q = query[rows, :]

        def one_head(head, carry):
            mixed, logs = carry
            mine = head_lanes(q.shape, head)
            s = mm(jnp.where(mine, q, jnp.zeros_like(q)), key[:span, :], NT) + mask[:, :span]
            top = jnp.max(s, axis=1, keepdims=True)
            p = jnp.exp(s - top)
            norm = jnp.sum(p, axis=1, keepdims=True)
            o = mm(p.astype(LOW), value[:span, :]) / norm
            mixed = jnp.where(mine, o, mixed)
            lane = lax.broadcasted_iota(jnp.int32, logs.shape, 1)
            logs = jnp.where(lane == head, top + jnp.log(norm), logs)
            return mixed, logs

        mixed, logs = lax.fori_loop(
            0, width // HEAD_DIM, one_head,
            (jnp.zeros((TILE, width), WIDE), jnp.zeros((TILE, 128), WIDE)),
        )
        low = mixed.astype(LOW)
        attended[rows, :] = low
        stats[rows, :] = logs
        stream.tiles[i] = mm(low, out_weight[...]).astype(LOW)
        stream.ready(i)
        if i >= 1:
            upper.stage(i)
    for which in range(3):
        stream.go(which)
    lse[...] = jnp.transpose(stats[...])[:8, :]
    stream.cross()
    stream.finish()
    resid[...] = stream.total[...] + tokens[...].astype(WIDE)
    unit, _ = unit_of(resid[...])
    two_own[...] = (unit * gains[1:2] + biases[1:2]).astype(LOW)
    after.all()
    upper.stage(4)
    gather.close_sends()
    stream.close()
    keep.wait()


def attend_heads(
    row_lengths, row_group, tokens, gains, biases, upstream, weight, out_weight, bias, count
):
    rows, width = tokens.shape
    total = rows * count
    local = out_weight.shape[0]
    slab = (((total, local), LOW), VM)
    tall = (((total, width), LOW), ANY)
    return call(
        attend_kernel,
        5,
        [(row_lengths, SM), (row_group, SM), (tokens, VM), (gains, VM), (biases, VM), (upstream, VM)]
        + [(weight, ANY), (out_weight, VM), (bias, VM)],
        [
            slab, slab, slab, slab,
            (((8, total), WIDE), VM),
            tall,
            tall,
            (((rows, width), WIDE), VM),
            tall,
            (((rows, width), LOW), VM),
            (((3, total, 128), WIDE), VM),
            (((total, 1), jnp.int32), VM),
            (((1, total), jnp.int32), VM),
        ],
        [
            pltpu.VMEM((total, width), LOW),
            pltpu.VMEM((rows, width), LOW),
            pltpu.VMEM((3, width, local), LOW),
            pltpu.VMEM((TILE, total), WIDE),
            pltpu.VMEM((total, 128), WIDE),
            pltpu.SemaphoreType.DMA((2,)),
        ]
        + stream_scratch(rows, width)
        + gather_sems() * 3,
        limit=60,
        flops=7 << 30,
    )


def attend_back_kernel(
    branch_all, normed_all, out_weight, tables, lab_col, lab_row,
    query, key, value, attended, lse, far,
    mixin_out, terms, out_sum, bias_term, far_all,
    branch, normed, mask, inner, heads_back, query_back, key_back, value_back, mixin, mixes,
    sems, outs, out_term, out_inbox, *scratch,
):
    total, width = query.shape
    tiles = total // TILE
    heads = width // HEAD_DIM
    ring = Ring()
    line = Line(ring, *scratch[3:5])
    ring.barrier(line.peers)
    gather = Gather(ring, far_rows(far, ring, 1, total), far_all, *scratch[0:3])
    share = out_term.shape[0] // line.groups

    def share_of(group):
        return pl.ds(pl.multiple_of(group * share, share), share)

    def out_copy(k):
        return line.copy(k, out_term.at[share_of(line.away(k)), :], out_inbox.at[k - 1])

    gather.stage(0)
    loads = load(
        [(branch_all.at[pl.ds(i * TILE, TILE), :], branch.at[pl.ds(i * TILE, TILE), :]) for i in range(tiles)]
        + [(normed_all, normed)],
        sems,
    )
    head_of = lax.broadcasted_iota(jnp.int32, (8, width), 1) // HEAD_DIM
    pick = (head_of == lax.broadcasted_iota(jnp.int32, (8, width), 0)).astype(LOW)
    for i in range(tiles):
        rows = pl.ds(i * TILE, TILE)
        loads[i].wait()
        low = mm(branch[rows, :], out_weight[...], NT).astype(LOW)
        heads_back[rows, :] = low
        prod = low.astype(WIDE) * attended[rows, :].astype(WIDE)
        high = prod.astype(LOW)
        rest = (prod - high.astype(WIDE)).astype(LOW)
        inner[:, rows] = mm(pick, high, NT) + mm(pick, rest, NT)
    out_term[...] = mm(attended[...], branch[...], TN).astype(LOW)
    for k in range(1, line.groups):
        out_copy(k).start()
    gather.stage(1)
    key_back[...] = jnp.zeros_like(key_back)
    value_back[...] = jnp.zeros_like(value_back)
    for i in range(tiles):
        rows = pl.ds(i * TILE, TILE)
        span = (i + 1) * TILE
        k_at = lax.broadcasted_iota(jnp.int32, (span, TILE), 0)
        q_at = i * TILE + lax.broadcasted_iota(jnp.int32, (span, TILE), 1)
        allowed = (lab_col[:span, :] == lab_row[:, rows]) & (q_at >= k_at)
        mask[:span, :] = jnp.where(allowed, 0.0, NEG)
        q = query[rows, :]
        d_out = heads_back[rows, :]

        def one_head(head, q_back):
            mine = head_lanes(q.shape, head)
            q_h = jnp.where(mine, q, jnp.zeros_like(q))
            d_h = jnp.where(mine, d_out, jnp.zeros_like(q))
            k = key[:span, :]
            k_h = jnp.where(head_lanes(k.shape, head), k, jnp.zeros_like(k))
            p = jnp.exp(mm(k, q_h, NT) + mask[:span, :] - lse[pl.ds(head, 1), rows])
            d_p = mm(value[:span, :], d_h, NT)
            d_s = (p * (d_p - inner[pl.ds(head, 1), rows])).astype(LOW)
            value_back[:span, :] += mm(p.astype(LOW), d_h)
            key_back[:span, :] += mm(d_s, q_h)
            return q_back + mm(d_s, k_h, TN)

        query_back[rows, :] = lax.fori_loop(0, heads, one_head, jnp.zeros((TILE, width), WIDE))
        if i >= 2:
            gather.stage(i)
    loads[-1].wait()
    copies = []
    sums = [jnp.zeros((1, width), WIDE)] * 3
    for i in range(tiles):
        rows = pl.ds(i * TILE, TILE)
        q_b = (query_back[rows, :] * (1.0 / 8)).astype(LOW).astype(WIDE)
        k_b = key_back[rows, :].astype(LOW).astype(WIDE)
        trio = [
            turn(q_b, tables, rows, -1).astype(LOW),
            turn(k_b, tables, rows, -1).astype(LOW),
            value_back[rows, :].astype(LOW),
        ]
        for c, item in enumerate(trio):
            mixin[c, rows, :] = item
            sums[c] = sums[c] + jnp.sum(item.astype(WIDE), axis=0, keepdims=True)
    copy = pltpu.make_async_copy(mixin, mixin_out, outs.at[3])
    copy.start()
    copies.append(copy)
    for c in range(3):
        bias_term[c : c + 1, :] = sums[c]
        mixes[c] = mm(normed[...], mixin[c], TN).astype(LOW)
        copy = pltpu.make_async_copy(mixes.at[c], terms.at[c], outs.at[c])
        copy.start()
        copies.append(copy)
    summed = out_term[share_of(ring.group), :].astype(WIDE)
    for k in range(1, line.groups):
        out_copy(k).wait_recv()
        summed = summed + out_inbox[k - 1].astype(WIDE)
    out_sum[...] = summed.astype(LOW)
    gather.stage(4)
    for k in range(1, line.groups):
        out_copy(k).wait_send()
    for copy in copies:
        copy.wait()


def attend_heads_back(
    branch_all, normed_all, out_weight, tables, lab_col, lab_row, saved, far
):
    total, width = normed_all.shape
    local = out_weight.shape[0]
    tiles = total // TILE
    groups = lax.axis_size("grp")
    tall = (((total, width), LOW), ANY)
    return call(
        attend_back_kernel,
        6,
        [(item, ANY) for item in (branch_all, normed_all)]
        + [(item, VM) for item in (out_weight, tables, lab_col, lab_row) + tuple(saved)]
        + [(far, ANY)],
        [
            (((3, total, local), LOW), ANY),
            (((3, width, local), LOW), ANY),
            (((local // groups, width), LOW), VM),
            (((3, local), WIDE), VM),
            tall,
        ],
        [
            pltpu.VMEM((total, width), LOW),
            pltpu.VMEM((total, width), LOW),
            pltpu.VMEM((total, TILE), WIDE),
            pltpu.VMEM((8, total), WIDE),
            pltpu.VMEM((total, local), LOW),
            pltpu.VMEM((total, local), WIDE),
            pltpu.VMEM((total, local), WIDE),
            pltpu.VMEM((total, local), WIDE),
            pltpu.VMEM((3, total, local), LOW),
            pltpu.VMEM((3, width, local), LOW),
            pltpu.SemaphoreType.DMA((tiles + 1,)),
            pltpu.SemaphoreType.DMA((4,)),
            pltpu.VMEM((local, width), LOW),
            pltpu.VMEM((groups - 1, local // groups, width), LOW),
        ]
        + gather_sems()
        + line_sems(),
        limit=60,
        flops=16 << 30,
    )


def units(gate, upper, hidden_back):
    sigma = jax.nn.sigmoid(gate)
    silu = gate * sigma
    return (
        (silu * upper).astype(LOW),
        (hidden_back * (upper * (sigma + silu * (1.0 - sigma)))).astype(LOW),
        (hidden_back * silu).astype(LOW),
    )


def forward_units(two, up, wide, down):
    return units(mm(wide[0], two, NT), mm(wide[1], two, NT), mm(down[...], up, NT))


def feed_kernel(
    two_all, up_all, wide_hbm, down_hbm, far, resid, upstream, gains,
    down_part, saved, far_one, resid_back, branch_all, sums,
    two, up, wide, down, kept, stage, own, sems, outs, *scratch,
):
    total = two_all.shape[0]
    tiles = total // TILE
    ring = Ring()
    met = ring.greet()
    stream = Stream(ring, *scratch[:N_STREAM])
    gather = Gather(ring, far_rows(far, ring, 1, total), far_one, *scratch[N_STREAM : N_STREAM + 3])
    branch = Gather(ring, own, branch_all, *scratch[N_STREAM + 3 :])
    chips = ring.chips()

    def rows_of(chip):
        return pl.ds(pl.multiple_of(chip * TILE, TILE), TILE)

    def tile_loads(step, chip):
        return [
            pltpu.make_async_copy(two_all.at[rows_of(chip), :], two.at[step], sems.at[0, step]),
            pltpu.make_async_copy(up_all.at[rows_of(chip), :], up.at[step], sems.at[1, step]),
        ]

    weights = load([(wide_hbm, wide), (down_hbm, down)], sems.at[2])
    for step in range(tiles):
        for copy in tile_loads(step, chips[step]):
            copy.start()
    met()
    gather.stage(0)
    for copy in weights:
        copy.wait()

    def chip_at(step):
        chip = chips[tiles - 1]
        for i in range(tiles - 1):
            chip = jnp.where(step == i, chips[i], chip)
        return chip

    def body(step, carry):
        chip = chip_at(step)
        for copy in tile_loads(step, chip):
            copy.wait()
        trio = forward_units(two[step], up[step], wide, down)
        for c in range(3):
            kept[c, :, rows_of(chip)] = trio[c]
        for i in range(1, tiles):

            @pl.when(step == i)
            def _():
                stream.go(i - 1)
                if i == tiles - 1:
                    stream.cross()

        stream.tiles[chip] = (mm(trio[1], wide[0], TN) + mm(trio[2], wide[1], TN)).astype(LOW)
        stream.ready(chip)
        for i in range(tiles):

            @pl.when(step == i)
            def _():
                if i < 3:
                    gather.stage(i + 1)

        return carry

    lax.fori_loop(0, tiles, body, 0)
    keep = pltpu.make_async_copy(kept, saved, outs.at[tiles])
    keep.start()
    unit, scale = unit_of(resid[...])
    stream.finish()
    incoming = stream.total[...]
    back = upstream[...].astype(WIDE) + back_of(incoming, unit, scale, gains[1:2])
    resid_back[...] = back
    own[...] = back.astype(LOW)
    branch.stage(0)
    sums[0:1] = jnp.sum(incoming * unit, axis=0, keepdims=True)
    sums[1:2] = jnp.sum(incoming, axis=0, keepdims=True)

    def down_copy(i):
        start = i * TILE if isinstance(i, int) else pl.multiple_of(i * TILE, TILE)
        rows = pl.ds(start, TILE)
        return pltpu.make_async_copy(stage.at[i], down_part.at[rows, :], outs.at[i])

    def down_body(i, carry):
        stage[i] = mm(kept[0, :, rows_of(i)], down[...], TN).astype(LOW)
        down_copy(i).start()
        for number in (1, 2, 3):

            @pl.when(i == number)
            def _():
                branch.stage(number)

        return carry

    lax.fori_loop(0, tiles, down_body, 0)
    branch.stage(4)
    gather.stage(4)
    stream.close()
    keep.wait()
    for i in range(tiles):
        down_copy(i).wait()


def feed(two_all, up_all, wide, down, far, resid, upstream, gains):
    total, width = two_all.shape
    rows = resid.shape[0]
    local = down.shape[0]
    tiles = total // TILE
    tall = (((total, width), LOW), ANY)
    return call(
        feed_kernel,
        7,
        [(item, ANY) for item in (two_all, up_all, wide, down, far)]
        + [(item, VM) for item in (resid, upstream, gains)],
        [
            tall,
            (((3, local, total), LOW), ANY),
            tall,
            (((rows, width), WIDE), VM),
            tall,
            (((2, width), WIDE), VM),
        ],
        [
            pltpu.VMEM((tiles, TILE, width), LOW),
            pltpu.VMEM((tiles, TILE, width), LOW),
            pltpu.VMEM((2, local, width), LOW),
            pltpu.VMEM((local, width), LOW),
            pltpu.VMEM((3, local, total), LOW),
            pltpu.VMEM((tiles, TILE, width), LOW),
            pltpu.VMEM((rows, width), LOW),
            pltpu.SemaphoreType.DMA((3, tiles)),
            pltpu.SemaphoreType.DMA((1 + tiles,)),
        ]
        + stream_scratch(rows, width)
        + gather_sems() * 2,
        limit=60,
        flops=18 << 30,
    )


N_LAST_GATHERS = 4


def last_kernel(
    mix_part, down_part, tokens, resid, resid_back, gains, sums, bias_term, out_sum,
    two_all, up_all, saved, two_far, up_far, up_one, two_one, wide_hbm, down_hbm,
    tokens_grad, layer_out, four, out_grad, wide_grad, down_grad, two_two, two_three, up_two, up_three,
    two, up, kept, wide, down, acc, inbox, mail, sems, outs, mail_send, mail_recv, *scratch,
):
    total = two_all.shape[0]
    per = total // TILE
    one_scratch, two_scratch, ag = scratch[:11], scratch[11:22], scratch[22:34]
    ring = Ring()
    group, groups = ring.group, lax.axis_size("grp")
    line = Line(ring, *scratch[34:36])
    others = line.peers
    ring.barrier(others)

    one = Scatter(ring, mix_part, *one_scratch)
    second_sum = Scatter(ring, down_part, *two_scratch)
    u2, g2, u3, g3 = [
        Gather(ring, far_rows(far, ring, k, total), dst, *ag[3 * i : 3 * i + 3])
        for i, (far, k, dst) in enumerate(
            ((up_far, 2, up_two), (two_far, 2, two_two), (up_far, 3, up_three), (two_far, 3, two_three))
        )
    ]
    two_sources = (two_all, two_one, two_two, two_three)
    up_sources = (up_all, up_one, up_two, up_three)

    def first_norm():
        unit, scale = unit_of(tokens[...].astype(WIDE))
        incoming = one.total[...]
        tokens_grad[...] = (resid_back[...] + back_of(incoming, unit, scale, gains[0:1])).astype(LOW)
        four[...] = jnp.zeros_like(four)
        four[0:1] = jnp.sum(incoming * unit, axis=0, keepdims=True)
        four[1:2] = sums[0:1]
        four[2:3] = jnp.sum(incoming, axis=0, keepdims=True)
        four[3:4] = sums[1:2]

    def mail_copy(stage):
        peer = (ring.twin, ring.xn, ring.yn)[stage]
        return ring.copy(mail.at[stage], inbox.at[stage], mail_send, mail_recv, stage, peer)

    def mail_start(stage):
        mail[stage] = four[...]
        mail_copy(stage).start()

    def mail_wait(stage):
        mail_copy(stage).wait_recv()
        four[...] += inbox[stage]

    def group_copy(k):
        return pltpu.make_async_remote_copy(
            src_ref=mail.at[3],
            dst_ref=inbox.at[2 + k],
            send_sem=mail_send.at[2 + k],
            recv_sem=mail_recv.at[2 + k],
            device_id=others[k - 1],
            device_id_type=MESH_ID,
        )

    def group_start():
        four[4:5] = jnp.zeros((1, four.shape[1]), WIDE)
        local = bias_term.shape[1]
        for c in range(3):
            four[4:5, c * local : (c + 1) * local] = bias_term[c : c + 1, :]
        mail[3] = four[...]
        for k in range(1, groups):
            group_copy(k).start()

    def group_wait():
        for k in range(1, groups):
            group_copy(k).wait_recv()
        summed = jnp.zeros(four.shape, WIDE)
        for number in range(groups):
            term = mail[3]
            for k in range(1, groups):
                source = lax.rem(group + groups - k, groups)
                term = jnp.where(source == number, inbox[2 + k], term)
            summed = summed + term
        four[...] = summed
        for stage in range(3):
            mail_copy(stage).wait_send()
        for k in range(1, groups):
            group_copy(k).wait_send()

    share = out_sum.shape[0]

    def out_rows():
        return out_grad.at[pl.ds(pl.multiple_of(group * share, share), share), :]

    def out_keep():
        return pltpu.make_async_copy(out_sum, out_rows(), sems.at[2, 2])

    def out_start():
        for k in range(1, groups):
            line.copy(k, out_sum, out_rows()).start()
        out_keep().start()

    def layer_end():
        layer_out[...] = (resid[...] + second_sum.total[...]).astype(LOW)

    def stage(item, number):
        return lambda: item.stage(number)

    plan = {
        0: [out_start, stage(u2, 0)],
        3: [stage(u2, 1), stage(g2, 0)],
        4: [stage(u2, 2)],
        5: [stage(u2, 3)],
        6: [stage(g2, 1), stage(u3, 0)],
        7: [stage(g2, 2), stage(u2, 4)],
        8: [stage(g2, 3), stage(g2, 4), stage(u3, 1), stage(g3, 0)],
        9: [stage(u3, 2)],
        10: [stage(u3, 3), stage(one, 0)],
        11: [stage(g3, 1), stage(one, 1), stage(u3, 4)],
        12: [stage(g3, 2), stage(g3, 3), stage(g3, 4), stage(second_sum, 0)],
        13: [stage(one, 2), stage(second_sum, 1)],
        14: [stage(one, 3), first_norm, lambda: mail_start(0)],
        15: [lambda: mail_wait(0), lambda: mail_start(1), stage(second_sum, 2)],
    }

    def fetch(source, tile, side):
        start = tile * TILE if isinstance(tile, int) else pl.multiple_of(tile * TILE, TILE)
        rows = pl.ds(start, TILE)
        return [
            pltpu.make_async_copy(two_sources[source].at[rows, :], two.at[side], sems.at[side, 0]),
            pltpu.make_async_copy(up_sources[source].at[rows, :], up.at[side], sems.at[side, 1]),
        ]

    def fetch_kept(tile, side):
        start = tile * TILE if isinstance(tile, int) else pl.multiple_of(tile * TILE, TILE)
        return pltpu.make_async_copy(saved.at[:, :, pl.ds(start, TILE)], kept.at[side], sems.at[side, 2])

    weights = load([(wide_hbm, wide), (down_hbm, down)], sems.at[2])
    for copy in fetch(0, 0, 0) + [fetch_kept(0, 0)]:
        copy.start()
    acc[...] = jnp.zeros_like(acc)

    def add(side, trio):
        acc[2] += mm(trio[0], up[side])
        acc[0] += mm(trio[1], two[side])
        acc[1] += mm(trio[2], two[side])

    steps = per * groups

    def start_fetch(step):
        side = lax.rem(step, 2)
        for source in range(groups):

            @pl.when((step < steps) & (step // per == source))
            def _():
                for copy in fetch(source, lax.rem(step, per), side):
                    copy.start()
                if source == 0:
                    fetch_kept(lax.rem(step, per), side).start()

    def events(step):
        for at, acts in plan.items():

            @pl.when(step == at)
            def _():
                for act in acts:
                    act()


    def own_body(step, carry):
        events(step)
        side = lax.rem(step, 2)
        for copy in fetch(0, 0, side) + [fetch_kept(0, side)]:
            copy.wait()

        @pl.when(step + 1 < per)
        def _():
            start_fetch(step + 1)

        add(side, [kept[side, c] for c in range(3)])
        return carry

    lax.fori_loop(0, per, own_body, 0)
    for copy in weights:
        copy.wait()

    def body(step, carry):
        events(step)
        side = lax.rem(step, 2)

        @pl.when(lax.rem(step, per) == 0)
        def _():
            start_fetch(step)

        for copy in fetch(0, 0, side):
            copy.wait()

        @pl.when(lax.rem(step + 1, per) != 0)
        def _():
            start_fetch(step + 1)

        trio = forward_units(two[side], up[side], wide, down)
        add(side, trio)
        return carry

    lax.fori_loop(per, steps, body, 0)
    mail_wait(1)
    mail_start(2)
    wide[...] = acc[0:2].astype(LOW)
    copies = load([(wide, wide_grad)], outs)
    mail_wait(2)
    group_start()
    down[...] = acc[2].astype(LOW)
    copies += load([(down, down_grad)], outs.at[pl.ds(1, 1)])
    second_sum.stage(3)
    layer_end()
    group_wait()
    out_keep().wait()
    for k in range(1, groups):
        line.copy(k, out_sum, out_rows()).wait()
    for copy in copies:
        copy.wait()


def last(mix_part, down_part, tokens, resid, resid_back, gains, sums, bias_term, out_sum,
         two_all, up_all, saved, two_far, up_far, up_one, two_one, wide, down):
    total, width = two_all.shape
    rows = tokens.shape[0]
    local = down.shape[0]
    groups = lax.axis_size("grp")
    tall = (((total, width), LOW), ANY)
    block = (((rows, width), LOW), VM)
    return call(
        last_kernel,
        8,
        [(mix_part, ANY), (down_part, ANY)]
        + [(item, VM) for item in (tokens, resid, resid_back, gains, sums, bias_term, out_sum)]
        + [(item, ANY) for item in (two_all, up_all, saved, two_far, up_far, up_one, two_one, wide, down)],
        [
            block,
            block,
            (((8, width), WIDE), VM),
            (((out_sum.shape[0] * groups, width), LOW), ANY),
            (((2, local, width), LOW), ANY),
            (((local, width), LOW), ANY),
            tall, tall, tall, tall,
        ],
        [
            pltpu.VMEM((2, TILE, width), LOW),
            pltpu.VMEM((2, TILE, width), LOW),
            pltpu.VMEM((2, 3, local, TILE), LOW),
            pltpu.VMEM((2, local, width), LOW),
            pltpu.VMEM((local, width), LOW),
            pltpu.VMEM((3, local, width), WIDE),
            pltpu.VMEM((2 + groups, 8, width), WIDE),
            pltpu.VMEM((4, 8, width), WIDE),
            pltpu.SemaphoreType.DMA((3, 3)),
            pltpu.SemaphoreType.DMA((2,)),
            pltpu.SemaphoreType.DMA((2 + groups,)),
            pltpu.SemaphoreType.DMA((2 + groups,)),
        ]
        + scatter_scratch(rows, width) * 2
        + gather_sems() * N_LAST_GATHERS
        + line_sems(),
        limit=62,
        flops=72 << 30,
        cost=120 << 20,
    )


RING = 8


def on_device(
    tokens,
    norm_gains,
    norm_biases,
    mix_weight,
    mix_bias,
    out_weight,
    gate_up_weight,
    down_weight,
    row_lengths,
    row_group,
    cotangent,
):
    count = lax.axis_size("seq")
    shard = lax.axis_index("seq")
    group = lax.axis_index("grp")
    slots_dev = tokens.shape[0]
    load = jnp.sum(jnp.where(row_group == group, row_lengths, 0))
    slots = shard * slots_dev + jnp.arange(slots_dev, dtype=jnp.int32)
    upstream = jnp.where(slots[:, None] < load, cotangent, jnp.zeros_like(cotangent))
    mix_t = jnp.transpose(mix_weight, (1, 0, 2))
    wide_t = jnp.transpose(gate_up_weight, (1, 2, 0))

    up_far = lax.all_gather(upstream, "grp", axis=0, tiled=True)
    (
        query, key, value, attended, lse, normed_all, up_all, resid, two_all, two_mine,
        tables, lab_col, lab_row,
    ) = attend_heads(
        row_lengths, row_group, tokens, norm_gains, norm_biases, upstream, mix_t, out_weight, mix_bias, count
    )
    two_far = lax.all_gather(two_mine, "grp", axis=0, tiled=True)
    down_part, saved, up_one, resid_back, branch_all, sums = feed(
        two_all, up_all, wide_t, down_weight, up_far, resid, upstream, norm_gains
    )
    mixin, mix_term, out_sum, bias_term, two_one = attend_heads_back(
        branch_all, normed_all, out_weight, tables, lab_col, lab_row,
        (query, key, value, attended, lse), two_far,
    )
    mix_grad = lax.psum(mix_term, "grp")
    mix_part = jnp.einsum(
        "ctf,cdf->td", mixin, mix_t, preferred_element_type=jnp.float32
    ).astype(jnp.bfloat16)
    tokens_grad, layer_out, four, out_grad, wide_grad, down_grad = last(
        mix_part, down_part, tokens, resid, resid_back, norm_gains, sums, bias_term, out_sum,
        two_all, up_all, saved, two_far, up_far, up_one, two_one, wide_t, down_weight,
    )[:6]
    local = mix_bias.shape[1]
    return (
        layer_out,
        tokens_grad,
        four[0:2],
        four[2:4],
        jnp.transpose(mix_grad, (1, 0, 2)).astype(jnp.float32),
        four[4, : 3 * local].reshape(3, local),
        out_grad.astype(jnp.float32),
        jnp.transpose(wide_grad, (2, 0, 1)).astype(jnp.float32),
        down_grad.astype(jnp.float32),
    )


def solution(mesh):
    placed = (
        P(("grp", "seq"), None),
        P(),
        P(),
        P(None, None, "seq"),
        P(None, "seq"),
        P("seq", None),
        P(None, None, "seq"),
        P("seq", None),
        P(),
        P(),
        P(("grp", "seq"), None),
    )
    return jax.shard_map(
        on_device if mesh.shape["seq"] == RING else plain_device,
        mesh=mesh,
        in_specs=placed,
        out_specs=(
            P(("grp", "seq"), None),
            P(("grp", "seq"), None),
            P(),
            P(),
            P(None, None, "seq"),
            P(None, "seq"),
            P("seq", None),
            P(None, None, "seq"),
            P("seq", None),
        ),
        check_vma=False,
    )
```

```python
import functools
import math

import jax
import jax.numpy as jnp
from jax import lax
from jax.experimental import pallas as pl
from jax.experimental.pallas import tpu as pltpu
from jax.sharding import PartitionSpec as P

HEAD_DIM = 64
ROT = 16


EPS = 1e-05
NEG = -1e30
BASE = 10000.0


def layer_norm(values, gain, bias):
    centered = values - jnp.mean(values, axis=-1, keepdims=True)
    scale = lax.rsqrt(jnp.mean(centered * centered, axis=-1, keepdims=True) + EPS)
    unit = centered * scale
    return (unit * gain + bias, unit, scale)


def norm_back(incoming, unit, scale, gain):
    along = incoming * gain
    inner = jnp.mean(along, axis=-1, keepdims=True)
    cross = jnp.mean(along * unit, axis=-1, keepdims=True)
    return (
        scale * (along - inner - unit * cross),
        jnp.sum(incoming * unit, axis=0),
        jnp.sum(incoming, axis=0),
    )


def rotate(values, where, sign):
    half = ROT // 2
    freq = BASE ** (-jnp.arange(half, dtype=jnp.float32) / half)
    angle = where.astype(jnp.float32)[:, None] * freq[None, :]
    cosine = jnp.cos(angle)[:, None, :]
    sine = sign * jnp.sin(angle)[:, None, :]
    first = values[..., :half]
    second = values[..., half:ROT]
    return jnp.concatenate(
        [first * cosine - second * sine, second * cosine + first * sine, values[..., ROT:]], axis=-1
    )


def unrotate(lowered, where):
    wide = lowered.astype(jnp.float32)
    turned = jnp.stack(
        [rotate(wide[:, 0], where, -1.0), rotate(wide[:, 1], where, -1.0), wide[:, 2]], axis=1
    )
    return turned.reshape(lowered.shape[0], 3, -1).astype(jnp.bfloat16)


def slot_rows(row_lengths, row_group, group, slots):
    order = jnp.arange(row_lengths.shape[0], dtype=jnp.int32)
    same = row_group == group
    earlier = (order[:, None] > order[None, :]) & same[None, :]
    begin = jnp.sum(jnp.where(earlier, row_lengths[None, :], 0), axis=1)
    finish = begin + row_lengths
    inside = same[None, :] & (slots[:, None] >= begin[None, :]) & (slots[:, None] < finish[None, :])
    label = jnp.sum(jnp.where(inside, order[None, :] + 1, 0), axis=1) - 1
    offset = jnp.sum(jnp.where(inside, slots[:, None] - begin[None, :], 0), axis=1)
    load = jnp.sum(jnp.where(same, row_lengths, 0))
    return (label, jnp.where(label < 0, slots - load, offset))


def block_scores(query, key, label, start, block):
    part = lax.dynamic_slice_in_dim(query, start, block, 0)
    rows = start + jnp.arange(block, dtype=jnp.int32)
    columns = jnp.arange(label.shape[0], dtype=jnp.int32)
    label_rows = lax.dynamic_slice_in_dim(label, start, block, 0)
    allowed = (label_rows[:, None] == label[None, :]) & (rows[:, None] >= columns[None, :])
    scores = jnp.einsum("qhe,khe->hqk", part, key, preferred_element_type=jnp.float32) * (
        1.0 / math.sqrt(query.shape[-1])
    )
    return (part, jnp.where(allowed[None], scores, NEG))


def attend(query, key, value, label, block):

    def one_block(index):
        part, scores = block_scores(query, key, label, index * block, block)
        top = jnp.max(scores, axis=-1, keepdims=True)
        weights = jnp.exp(scores - top)
        totals = jnp.sum(weights, axis=-1, keepdims=True)
        probs = (weights / totals).astype(jnp.bfloat16)
        mixed = jnp.einsum("hqk,khe->qhe", probs, value, preferred_element_type=jnp.float32)
        return (mixed, top[..., 0] + jnp.log(totals[..., 0]))

    mixed, log_totals = lax.map(one_block, jnp.arange(query.shape[0] // block, dtype=jnp.int32))
    return (mixed.reshape(query.shape), log_totals)


def attend_back(query, key, value, label, log_totals, mixed_back, block):
    scale = 1.0 / math.sqrt(query.shape[-1])

    def one_block(carry, index):
        key_back, value_back = carry
        start = index * block
        part, scores = block_scores(query, key, label, start, block)
        back_part = lax.dynamic_slice_in_dim(mixed_back, start, block, 0)
        probs = jnp.exp(scores - log_totals[index][..., None])
        value_back = value_back + jnp.einsum(
            "hqk,qhe->khe",
            probs.astype(jnp.bfloat16),
            back_part,
            preferred_element_type=jnp.float32,
        )
        probs_back = jnp.einsum(
            "qhe,khe->hqk", back_part, value, preferred_element_type=jnp.float32
        )
        inner = jnp.sum(probs_back * probs, axis=-1, keepdims=True)
        score_back = (probs * (probs_back - inner)).astype(jnp.bfloat16)
        query_back = (
            jnp.einsum("hqk,khe->qhe", score_back, key, preferred_element_type=jnp.float32) * scale
        )
        key_back = (
            key_back
            + jnp.einsum("hqk,qhe->khe", score_back, part, preferred_element_type=jnp.float32)
            * scale
        )
        return ((key_back, value_back), query_back)

    empty = jnp.zeros(key.shape, jnp.float32)
    (key_back, value_back), query_back = lax.scan(
        one_block, (empty, empty), jnp.arange(query.shape[0] // block, dtype=jnp.int32)
    )
    return (query_back.reshape(query.shape), key_back, value_back)


def silu_parts(gate_up):
    gate = gate_up[:, 0]
    upper = gate_up[:, 1]
    sigma = jax.nn.sigmoid(gate)
    return (gate * sigma * upper, gate, upper, sigma)


def gate_back(hidden_back, gate, upper, sigma):
    gate_part = hidden_back * upper * sigma * (1.0 + gate * (1.0 - sigma))
    up_part = hidden_back * gate * sigma
    return jnp.stack([gate_part, up_part], axis=1).astype(jnp.bfloat16)


def gather_rows(values):
    return lax.all_gather(values, "seq", axis=0, tiled=True)


def summed_rows(product, left):
    return lax.psum_scatter(
        product(left).astype(jnp.bfloat16), "seq", scatter_dimension=0, tiled=True
    ).astype(jnp.float32)


def plain_device(
    tokens,
    norm_gains,
    norm_biases,
    mix_weight,
    mix_bias,
    out_weight,
    gate_up_weight,
    down_weight,
    row_lengths,
    row_group,
    cotangent,
):
    seq_count = lax.axis_size("seq")
    shard = lax.axis_index("seq")
    group = lax.axis_index("grp")
    slots_dev = tokens.shape[0]
    width = tokens.shape[1]
    group_slots = slots_dev * seq_count
    block = min(512, group_slots)
    local_width = width // seq_count
    local_heads = local_width // HEAD_DIM
    mine = shard * slots_dev + jnp.arange(slots_dev, dtype=jnp.int32)
    label_mine, place_mine = slot_rows(row_lengths, row_group, group, mine)
    label_all, place_all = slot_rows(
        row_lengths, row_group, group, jnp.arange(group_slots, dtype=jnp.int32)
    )
    inputs = tokens.astype(jnp.float32)
    upstream = cotangent.astype(jnp.float32) * (label_mine >= 0).astype(jnp.float32)[:, None]
    upstream_low = upstream.astype(jnp.bfloat16)
    normed, unit_one, scale_one = layer_norm(inputs, norm_gains[0], norm_biases[0])
    normed_all = gather_rows(normed.astype(jnp.bfloat16))
    up_four = lax.all_gather(upstream_low, ("grp", "seq"), axis=0, tiled=True)
    upstream_all = lax.dynamic_slice_in_dim(up_four, group * group_slots, group_slots, 0)
    mixin = jnp.einsum(
        "td,dcf->tcf", normed_all, mix_weight, preferred_element_type=jnp.float32
    ) + mix_bias.astype(jnp.float32)
    heads_in = mixin.reshape(group_slots, 3, local_heads, HEAD_DIM)
    query = rotate(heads_in[:, 0], place_all, 1.0).astype(jnp.bfloat16)
    key = rotate(heads_in[:, 1], place_all, 1.0).astype(jnp.bfloat16)
    value = heads_in[:, 2].astype(jnp.bfloat16)
    mixed, log_totals = attend(query, key, value, label_all, block)
    attended = mixed.reshape(group_slots, local_width).astype(jnp.bfloat16)

    def out_product(part):
        return jnp.dot(part, out_weight, preferred_element_type=jnp.float32)

    resid = inputs + summed_rows(out_product, attended)
    normed_two, unit_two, scale_two = layer_norm(resid, norm_gains[1], norm_biases[1])
    normed_two_low = normed_two.astype(jnp.bfloat16)
    normed_two_all = gather_rows(normed_two_low)
    two_four = lax.all_gather(normed_two_low, ("grp", "seq"), axis=0, tiled=True)

    def up_to_back(two, up):
        gate_up = jnp.einsum("td,dcf->tcf", two, gate_up_weight, preferred_element_type=jnp.float32)
        hidden, gate, upper, sigma = silu_parts(gate_up)
        hidden_back = jnp.einsum("td,fd->tf", up, down_weight, preferred_element_type=jnp.float32)
        return hidden.astype(jnp.bfloat16), gate_back(hidden_back, gate, upper, sigma)

    hidden_low, gate_up_back = up_to_back(normed_two_all, upstream_all)

    def down_product(part):
        return jnp.dot(part, down_weight, preferred_element_type=jnp.float32)

    layer_out = resid + summed_rows(down_product, hidden_low)

    def gate_up_product(part):
        return jnp.einsum("tcf,dcf->td", part, gate_up_weight, preferred_element_type=jnp.float32)

    normed_two_back = summed_rows(gate_up_product, gate_up_back)
    hidden_four, back_four = up_to_back(two_four, up_four)
    down_grad = jnp.einsum("tf,td->fd", hidden_four, up_four, preferred_element_type=jnp.float32)
    gate_up_grad = jnp.einsum(
        "td,tcf->dcf", two_four, back_four, preferred_element_type=jnp.float32
    )
    resid_part, gain_two, bias_two = norm_back(normed_two_back, unit_two, scale_two, norm_gains[1])
    resid_back = upstream + resid_part
    branch_all = gather_rows(resid_back.astype(jnp.bfloat16))
    out_term = jnp.einsum("te,td->ed", attended, branch_all, preferred_element_type=jnp.float32)
    out_grad = lax.psum(out_term.astype(jnp.bfloat16), "grp").astype(jnp.float32)
    attended_back = jnp.einsum(
        "td,ed->te", branch_all, out_weight, preferred_element_type=jnp.float32
    ).astype(jnp.bfloat16)
    heads_back = attended_back.reshape(group_slots, local_heads, HEAD_DIM)
    query_back, key_back, value_back = attend_back(
        query, key, value, label_all, log_totals, heads_back, block
    )
    lowered = jnp.stack([query_back, key_back, value_back], axis=1).astype(jnp.bfloat16)
    mixin_back = unrotate(lowered, place_all)
    mix_term = jnp.einsum("td,tcf->dcf", normed_all, mixin_back, preferred_element_type=jnp.float32)
    mix_grad = lax.psum(mix_term.astype(jnp.bfloat16), "grp").astype(jnp.float32)
    bias_term = jnp.sum(mixin_back, axis=0, dtype=jnp.float32)
    mix_bias_grad = lax.psum(bias_term, "grp")

    def mix_product(part):
        return jnp.einsum("tcf,dcf->td", part, mix_weight, preferred_element_type=jnp.float32)

    normed_back = summed_rows(mix_product, mixin_back)
    tokens_part, gain_one, bias_one = norm_back(normed_back, unit_one, scale_one, norm_gains[0])
    tokens_grad = (resid_back + tokens_part).astype(jnp.bfloat16)
    gains_grad, biases_grad = lax.psum(
        (jnp.stack([gain_one, gain_two]), jnp.stack([bias_one, bias_two])), ("grp", "seq")
    )
    return (
        layer_out.astype(jnp.bfloat16),
        tokens_grad,
        gains_grad,
        biases_grad,
        mix_grad,
        mix_bias_grad,
        out_grad,
        gate_up_grad,
        down_grad,
    )


MESH_ID = pl.DeviceIdType.MESH
N_RS = 10
N_AG = 13


class Ring:
    def __init__(self):
        self.group = lax.axis_index("grp")
        self.me = lax.axis_index("seq")
        core = self.me % 2
        x = (self.me // 2) % 2
        y = self.me // 4
        self.flip = 1 - 2 * core
        self.twin = self.me + self.flip
        self.xn = self.me + 2 - 4 * x
        self.yn = self.me + 4 - 8 * y
        self.dn = self.xn + 4 - 8 * y

    def dev(self, seq):
        return (self.group, seq)

    def greet(self, extra=()):
        sem = pltpu.get_barrier_semaphore()
        peers = [self.dev(self.twin), self.dev(self.xn), self.dev(self.yn)] + list(extra)
        for peer in peers:
            pl.semaphore_signal(sem, inc=1, device_id=peer, device_id_type=MESH_ID)
        return lambda: pl.semaphore_wait(sem, len(peers))

    def barrier(self, extra=()):
        self.greet(extra)()

    def chips(self):
        return [self.dn // 2, self.xn // 2, self.yn // 2, self.me // 2]

    def copy(self, src, dst, send, recv, kind, seq):
        return pltpu.make_async_remote_copy(
            src_ref=src,
            dst_ref=dst,
            send_sem=send.at[kind],
            recv_sem=recv.at[kind],
            device_id=self.dev(seq),
            device_id_type=MESH_ID,
        )


class Line:
    def __init__(self, ring, send, recv):
        self.ring, self.send, self.recv = ring, send, recv
        self.groups = lax.axis_size("grp")
        self.peers = [(self.away(k), ring.me) for k in range(1, self.groups)]

    def away(self, k):
        return lax.rem(self.ring.group + k, self.groups)

    def copy(self, k, src, dst):
        return pltpu.make_async_remote_copy(
            src_ref=src,
            dst_ref=dst,
            send_sem=self.send.at[k - 1],
            recv_sem=self.recv.at[k - 1],
            device_id=self.peers[k - 1],
            device_id_type=MESH_ID,
        )


def line_sems():
    return [pltpu.SemaphoreType.DMA((lax.axis_size("grp"),)), pltpu.SemaphoreType.DMA((lax.axis_size("grp"),))]


class Gather:
    def __init__(self, ring, own, out, send, recv, local):
        self.ring, self.own, self.out = ring, own, out
        self.send, self.recv, self.local = send, recv, local
        self.rows = own.shape[0]
        self.half = self.rows // 2

    def at(self, block, part=None):
        rows, half = self.rows, self.half
        if part is None:
            return self.out.at[pl.ds(pl.multiple_of(block * rows, rows), rows), :]
        return self.out.at[pl.ds(pl.multiple_of(block * rows + part * half, half), half), :]

    def copy(self, kind):
        ring, half = self.ring, self.half
        if kind < 4:
            part, seq = ((0, ring.xn), (1, ring.yn), (1, ring.xn), (0, ring.yn))[kind]
            src, dst = self.own.at[pl.ds(part * half, half), :], self.at(ring.me, part)
        elif kind == 4:
            src, dst, seq = self.own, self.at(ring.me), ring.twin
        else:
            block, part, seq = (
                (ring.xn, 0, ring.yn),
                (ring.xn, 0, ring.twin),
                (ring.yn, 1, ring.xn),
                (ring.yn, 1, ring.twin),
                (ring.xn, 1, ring.twin),
                (ring.yn, 0, ring.twin),
                (ring.dn, 0, ring.twin),
                (ring.dn, 1, ring.twin),
            )[kind - 5]
            src = dst = self.at(block, part)
        return ring.copy(src, dst, self.send, self.recv, kind, seq)

    def keep(self):
        return pltpu.make_async_copy(self.own, self.at(self.ring.me), self.local)

    def stage(self, number):
        if number == 0:
            self.keep().start()
            for kind in range(5):
                self.copy(kind).start()
        elif number == 1:
            self.copy(0).wait_recv()
            self.copy(5).start()
            self.copy(6).start()
            self.copy(1).wait_recv()
            self.copy(7).start()
            self.copy(8).start()
        elif number == 2:
            self.copy(2).wait_recv()
            self.copy(9).start()
            self.copy(3).wait_recv()
            self.copy(10).start()
        elif number == 3:
            self.copy(5).wait_recv()
            self.copy(11).start()
            self.copy(7).wait_recv()
            self.copy(12).start()
        else:
            self.arrive(4, 6, 8, 9, 10, 11, 12)
            self.close()

    def arrive(self, *kinds):
        for kind in kinds:
            self.copy(kind).wait_recv()

    def close_sends(self):
        for kind in range(N_AG):
            self.copy(kind).wait_send()

    def close(self):
        self.keep().wait()
        self.close_sends()

    def all(self):
        for number in range(5):
            self.stage(number)


class Scatter:
    def __init__(self, ring, part, total, own, pair, rx, ry, fx, fy, mid, send, recv, local):
        self.ring, self.part, self.total = ring, part, total
        self.own, self.pair, self.rx, self.ry = own, pair, rx, ry
        self.fx, self.fy, self.mid = fx, fy, mid
        self.send, self.recv, self.local = send, recv, local
        self.rows, self.width = total.shape

    def block(self, index):
        return self.part.at[pl.ds(pl.multiple_of(index * self.rows, self.rows), self.rows), :]

    def index(self, slot):
        ring = self.ring
        return (ring.dn, ring.xn, ring.yn, ring.me)[slot]

    def keep(self, slot):
        return pltpu.make_async_copy(self.block(self.index(slot)), self.own.at[slot], self.local.at[slot])

    def copy(self, kind):
        ring, half = self.ring, self.width // 2
        lo, hi = pl.ds(0, half), pl.ds(half, half)
        if kind < 4:
            src, dst, seq = self.block(self.index(kind) + ring.flip), self.pair.at[kind], ring.twin
        else:
            src, dst, seq = (
                (self.own.at[0, :, lo], self.rx.at[0], ring.xn),
                (self.own.at[0, :, hi], self.ry.at[0], ring.yn),
                (self.own.at[1, :, lo], self.rx.at[1], ring.xn),
                (self.own.at[2, :, hi], self.ry.at[1], ring.yn),
                (self.mid.at[0], self.fy, ring.yn),
                (self.mid.at[1], self.fx, ring.xn),
            )[kind - 4]
        return ring.copy(src, dst, self.send, self.recv, kind, seq)

    def added(self, slot):
        self.keep(slot).wait()
        self.copy(slot).wait_recv()
        return self.own[slot].astype(jnp.float32) + self.pair[slot].astype(jnp.float32)

    def stage(self, number):
        wide, low, half = jnp.float32, self.own.dtype, self.width // 2
        lo, hi = pl.ds(0, half), pl.ds(half, half)
        own, total = self.own, self.total
        if number == 0:
            for slot in range(4):
                self.copy(slot).start()
                self.keep(slot).start()
        elif number == 1:
            own[0] = self.added(0).astype(low)
            self.copy(4).start()
            self.copy(5).start()
            own[1] = self.added(1).astype(low)
            self.copy(6).start()
            own[2] = self.added(2).astype(low)
            self.copy(7).start()
            total[...] = self.added(3)
        elif number == 2:
            self.copy(4).wait_recv()
            self.mid[0] = (own[2, :, lo].astype(wide) + self.rx[0].astype(wide)).astype(low)
            self.copy(8).start()
            self.copy(5).wait_recv()
            self.mid[1] = (own[1, :, hi].astype(wide) + self.ry[0].astype(wide)).astype(low)
            self.copy(9).start()
        else:
            self.copy(6).wait_recv()
            total[:, lo] += self.rx[1].astype(wide)
            self.copy(7).wait_recv()
            total[:, hi] += self.ry[1].astype(wide)
            self.copy(8).wait_recv()
            total[:, lo] += self.fy[...].astype(wide)
            self.copy(9).wait_recv()
            total[:, hi] += self.fx[...].astype(wide)
            for kind in range(N_RS):
                self.copy(kind).wait_send()

    def all(self):
        for number in range(4):
            self.stage(number)


class Stream:
    def __init__(self, ring, tiles, total, pair, rx, ry, fx, fy, mid, send, recv):
        self.ring, self.tiles, self.total, self.pair = ring, tiles, total, pair
        self.rx, self.ry, self.fx, self.fy, self.mid = rx, ry, fx, fy, mid
        self.send, self.recv = send, recv
        self.rows, self.width = total.shape
        self.at = ring.chips()

    def rows_of(self, twin):
        core = self.ring.me % 2
        core = 1 - core if twin else core
        return pl.ds(pl.multiple_of(core * self.rows, self.rows), self.rows)

    def copy(self, kind):
        ring, half = self.ring, self.width // 2
        lo, hi = pl.ds(0, half), pl.ds(half, half)
        mine = self.rows_of(False)
        dn, xn, yn, _ = self.at
        src, dst, seq = (
            (self.tiles.at[dn, mine, lo], self.rx.at[0], ring.xn),
            (self.tiles.at[dn, mine, hi], self.ry.at[0], ring.yn),
            (self.tiles.at[xn, mine, lo], self.rx.at[1], ring.xn),
            (self.tiles.at[yn, mine, hi], self.ry.at[1], ring.yn),
            (self.mid.at[0], self.fy, ring.yn),
            (self.mid.at[1], self.fx, ring.xn),
        )[kind - 4]
        return ring.copy(src, dst, self.send, self.recv, kind, seq)

    def pair_copy(self, chip):
        return self.ring.copy(
            self.tiles.at[chip, self.rows_of(True), :],
            self.pair.at[chip],
            self.send,
            self.recv,
            chip,
            self.ring.twin,
        )

    def ready(self, chip):
        self.pair_copy(chip).start()

    def added(self, chip):
        self.pair_copy(chip).wait_recv()
        mine = self.rows_of(False)
        return self.tiles[chip, mine, :].astype(jnp.float32) + self.pair[chip].astype(jnp.float32)

    def go(self, which):
        chip = self.at[which]
        self.tiles[chip, self.rows_of(False), :] = self.added(chip).astype(self.tiles.dtype)
        for kind in ((4, 5), (6,), (7,))[which]:
            self.copy(kind).start()

    def cross(self):
        wide, low, half = jnp.float32, self.tiles.dtype, self.width // 2
        lo, hi = pl.ds(0, half), pl.ds(half, half)
        mine = self.rows_of(False)
        _, xn, yn, _ = self.at
        self.copy(4).wait_recv()
        self.mid[0] = (self.tiles[yn, mine, lo].astype(wide) + self.rx[0].astype(wide)).astype(low)
        self.copy(8).start()
        self.copy(5).wait_recv()
        self.mid[1] = (self.tiles[xn, mine, hi].astype(wide) + self.ry[0].astype(wide)).astype(low)
        self.copy(9).start()

    def finish(self):
        wide, half = jnp.float32, self.width // 2
        lo, hi = pl.ds(0, half), pl.ds(half, half)
        total = self.total
        total[...] = self.added(self.at[3])
        self.copy(6).wait_recv()
        total[:, lo] += self.rx[1].astype(wide)
        self.copy(7).wait_recv()
        total[:, hi] += self.ry[1].astype(wide)
        self.copy(8).wait_recv()
        total[:, lo] += self.fy[...].astype(wide)
        self.copy(9).wait_recv()
        total[:, hi] += self.fx[...].astype(wide)

    def close(self):
        for chip in range(4):
            self.pair_copy(chip).wait_send()
        for kind in range(4, N_RS):
            self.copy(kind).wait_send()


def stream_scratch(rows, width):
    low = jnp.bfloat16
    half = width // 2
    return [
        pltpu.VMEM((4, 2 * rows, width), low),
        pltpu.VMEM((rows, width), jnp.float32),
        pltpu.VMEM((4, rows, width), low),
        pltpu.VMEM((2, rows, half), low),
        pltpu.VMEM((2, rows, half), low),
        pltpu.VMEM((rows, half), low),
        pltpu.VMEM((rows, half), low),
        pltpu.VMEM((2, rows, half), low),
        pltpu.SemaphoreType.DMA((N_RS,)),
        pltpu.SemaphoreType.DMA((N_RS,)),
    ]


N_STREAM = 10


def scatter_buffers(rows, width):
    low = jnp.bfloat16
    half = width // 2
    return [
        pltpu.VMEM((rows, width), jnp.float32),
        pltpu.VMEM((4, rows, width), low),
        pltpu.VMEM((4, rows, width), low),
        pltpu.VMEM((2, rows, half), low),
        pltpu.VMEM((2, rows, half), low),
        pltpu.VMEM((rows, half), low),
        pltpu.VMEM((rows, half), low),
        pltpu.VMEM((2, rows, half), low),
    ]


def scatter_sems():
    return [
        pltpu.SemaphoreType.DMA((N_RS,)),
        pltpu.SemaphoreType.DMA((N_RS,)),
        pltpu.SemaphoreType.DMA((4,)),
    ]


def scatter_scratch(rows, width):
    return scatter_buffers(rows, width) + scatter_sems()


def gather_sems():
    return [
        pltpu.SemaphoreType.DMA((N_AG,)),
        pltpu.SemaphoreType.DMA((N_AG,)),
        pltpu.SemaphoreType.DMA,
    ]


def gather_scratch(rows, width):
    return [pltpu.VMEM((rows, width), jnp.bfloat16)] + gather_sems()


def unit_of(values):
    centered = values - jnp.mean(values, axis=-1, keepdims=True)
    scale = lax.rsqrt(jnp.mean(centered * centered, axis=-1, keepdims=True) + EPS)
    return centered * scale, scale


def back_of(incoming, unit, scale, gain):
    along = incoming * gain
    inner = jnp.mean(along, axis=-1, keepdims=True)
    cross = jnp.mean(along * unit, axis=-1, keepdims=True)
    return scale * (along - inner - unit * cross)


VM = pl.BlockSpec(memory_space=pltpu.VMEM)
ANY = pl.BlockSpec(memory_space=pltpu.HBM)
SM = pl.BlockSpec(memory_space=pltpu.SMEM)


def call(kernel, number, ins, outs, scratch, limit=60, flops=0, cost=20_000_000, scratch_in=None):
    return pl.pallas_call(
        kernel,
        out_shape=tuple(jax.ShapeDtypeStruct(*shape) for shape, _ in outs),
        in_specs=[spec for _, spec in ins],
        out_specs=tuple(spec for _, spec in outs),
        scratch_shapes=scratch,
        compiler_params=pltpu.CompilerParams(
            collective_id=number,
            has_side_effects=True,
            vmem_limit_bytes=limit << 20,
        ),
        cost_estimate=pl.CostEstimate(flops=flops, bytes_accessed=cost, transcendentals=0),
    )(*[value for value, _ in ins])


TILE = 256
WIDE = jnp.float32
LOW = jnp.bfloat16
NT = (((1,), (1,)), ((), ()))
TN = (((0,), (0,)), ((), ()))


def mm(a, b, dims=(((1,), (0,)), ((), ()))):
    return lax.dot_general(a, b, dims, preferred_element_type=WIDE)


def far_rows(far, ring, away, total):
    groups = lax.axis_size("grp")
    rows = far.shape[0] // groups
    index = lax.rem(ring.group + away, groups)
    return far.at[pl.ds(pl.multiple_of(index * rows, rows), rows), :]


def head_lanes(shape, head):
    return lax.broadcasted_iota(jnp.int32, shape, 1) // HEAD_DIM == head


def turn(u, tables, rows, sign):
    cosine, below, above = (
        jnp.concatenate([tables[i, rows, :]] * (u.shape[1] // 128), axis=1) for i in range(3)
    )
    side = pltpu.roll(u, 8, 1) * below + pltpu.roll(u, u.shape[1] - 8, 1) * above
    return u * cosine + side if sign > 0 else u * cosine - side


def load(pairs, sems):
    copies = []
    for i, (src, dst) in enumerate(pairs):
        copy = pltpu.make_async_copy(src, dst, sems.at[i])
        copy.start()
        copies.append(copy)
    return copies


def rows_layout(row_lengths, row_group, group, tables, lab_col, lab_row):
    total = lab_col.shape[0]
    rows, begin = [], jnp.int32(0)
    for row in range(row_lengths.shape[0]):
        mine = row_group[row] == group
        rows.append((row, mine, begin, begin + row_lengths[row]))
        begin = begin + jnp.where(mine, row_lengths[row], 0)

    def lay(slots):
        label, base = jnp.full(slots.shape, -1, jnp.int32), jnp.full(slots.shape, begin, jnp.int32)
        for row, mine, first, end in rows:
            first, end = jnp.where(mine, first, -1), jnp.where(mine, end, -1)
            inside = (slots >= first) & (slots < end)
            label = jnp.where(inside, row, label)
            base = jnp.where(inside, first, base)
        return label, slots - base

    lab_row[...] = lay(lax.broadcasted_iota(jnp.int32, (1, total), 1))[0]
    half = ROT // 2

    def body(i, carry):
        at = pl.ds(pl.multiple_of(i * TILE, TILE), TILE)
        label, place = lay(i * TILE + lax.broadcasted_iota(jnp.int32, (TILE, 1), 0))
        lab_col[at, :] = label
        lane = lax.broadcasted_iota(jnp.int32, (TILE, 128), 1) % HEAD_DIM
        freq = jnp.ones((TILE, 128), WIDE)
        for e in range(1, half):
            freq = jnp.where(lane % half == e, BASE ** (-e / half), freq)
        angle = place.astype(WIDE) * freq
        cosine, sine = jnp.cos(angle), jnp.sin(angle)
        tables[0, at, :] = jnp.where(lane < ROT, cosine, 1.0)
        tables[1, at, :] = jnp.where((lane >= half) & (lane < ROT), sine, 0.0)
        tables[2, at, :] = jnp.where(lane < half, -sine, 0.0)
        return carry

    lax.fori_loop(0, total // TILE, body, 0)


def attend_kernel(
    row_lengths, row_group, tokens, gains, biases, upstream, weight, out_weight, bias,
    query, key, value, attended, lse, normed_all, up_all, resid, two_all, two_own, tables, lab_col, lab_row,
    normed, own, w, mask, stats, sems, *scratch,
):
    total, width = query.shape
    tiles = total // TILE
    ring = Ring()
    met = ring.greet()
    copy_w = pltpu.make_async_copy(weight, w, sems.at[0])
    copy_w.start()
    stream = Stream(ring, *scratch[:N_STREAM])
    scratch = scratch[N_STREAM:]
    gather = Gather(ring, own, normed, *scratch[0:3])
    upper = Gather(ring, upstream, up_all, *scratch[3:6])
    after = Gather(ring, two_own, two_all, *scratch[6:9])
    unit, _ = unit_of(tokens[...].astype(WIDE))
    own[...] = (unit * gains[0:1] + biases[0:1]).astype(LOW)
    met()
    gather.stage(0)
    rows_layout(row_lengths, row_group, ring.group, tables, lab_col, lab_row)
    gather.keep().wait()
    copy_w.wait()

    def mix(chip):
        rows = pl.ds(pl.multiple_of(chip * TILE, TILE), TILE)
        x = normed[rows, :]
        u = mm(x, w[0]) + bias[0:1].astype(WIDE)
        query[rows, :] = (turn(u, tables, rows, 1).astype(LOW).astype(WIDE) * (1.0 / 8)).astype(LOW)
        u = mm(x, w[1]) + bias[1:2].astype(WIDE)
        key[rows, :] = turn(u, tables, rows, 1).astype(LOW)
        value[rows, :] = (mm(x, w[2]) + bias[2:3].astype(WIDE)).astype(LOW)

    chips = ring.chips()

    def mix_body(step, carry):
        for i, acts in enumerate(
            (
                ((4,), ()),
                ((6, 9), (1, 2)),
                ((8, 10), (3,)),
                ((11, 12), ()),
            )
        ):

            @pl.when(step == i)
            def _():
                for number in acts[1]:
                    gather.stage(number)
                if i == 2:
                    upper.stage(0)
                gather.arrive(*acts[0])

        chip = chips[0]
        for i in range(1, tiles):
            chip = jnp.where(step == tiles - 1 - i, chips[(3, 1, 2)[tiles - 1 - i]], chip)
        mix(chip)
        return carry

    lax.fori_loop(0, tiles, mix_body, 0)
    keep = pltpu.make_async_copy(normed, normed_all, sems.at[1])
    keep.start()
    def tile(i):
        rows = pl.ds(i * TILE, TILE)
        span = (i + 1) * TILE
        q_at = i * TILE + lax.broadcasted_iota(jnp.int32, (TILE, span), 0)
        k_at = lax.broadcasted_iota(jnp.int32, (TILE, span), 1)
        allowed = (lab_col[rows, :] == lab_row[:, :span]) & (q_at >= k_at)
        mask[:, :span] = jnp.where(allowed, 0.0, NEG)
        q = query[rows, :]

        def one_head(head, carry):
            mixed, logs = carry
            mine = head_lanes(q.shape, head)
            s = mm(jnp.where(mine, q, jnp.zeros_like(q)), key[:span, :], NT) + mask[:, :span]
            top = jnp.max(s, axis=1, keepdims=True)
            p = jnp.exp(s - top)
            norm = jnp.sum(p, axis=1, keepdims=True)
            o = mm(p.astype(LOW), value[:span, :]) / norm
            mixed = jnp.where(mine, o, mixed)
            lane = lax.broadcasted_iota(jnp.int32, logs.shape, 1)
            logs = jnp.where(lane == head, top + jnp.log(norm), logs)
            return mixed, logs

        mixed, logs = lax.fori_loop(
            0, width // HEAD_DIM, one_head,
            (jnp.zeros((TILE, width), WIDE), jnp.zeros((TILE, 128), WIDE)),
        )
        low = mixed.astype(LOW)
        attended[rows, :] = low
        stats[rows, :] = logs
        stream.tiles[i] = mm(low, out_weight[...]).astype(LOW)

    def attend_body(step, carry):
        chip = chips[tiles - 1]
        for i in range(tiles - 1):
            chip = jnp.where(step == i, chips[i], chip)
        for i in range(tiles):

            @pl.when(chip == i)
            def _():
                tile(i)

        stream.ready(chip)
        for i in range(tiles):

            @pl.when(step == i)
            def _():
                if i:
                    stream.go(i - 1)
                if i < 3:
                    upper.stage(i + 1)

        return carry

    lax.fori_loop(0, tiles, attend_body, 0)
    stream.cross()
    lse[...] = jnp.transpose(stats[...])[:8, :]
    stream.finish()
    resid[...] = stream.total[...] + tokens[...].astype(WIDE)
    unit, _ = unit_of(resid[...])
    two_own[...] = (unit * gains[1:2] + biases[1:2]).astype(LOW)
    after.all()
    upper.stage(4)
    gather.close_sends()
    stream.close()
    keep.wait()


def attend_heads(
    row_lengths, row_group, tokens, gains, biases, upstream, weight, out_weight, bias, count
):
    rows, width = tokens.shape
    total = rows * count
    local = out_weight.shape[0]
    slab = (((total, local), LOW), VM)
    tall = (((total, width), LOW), ANY)
    return call(
        attend_kernel,
        5,
        [(row_lengths, SM), (row_group, SM), (tokens, VM), (gains, VM), (biases, VM), (upstream, VM)]
        + [(weight, ANY), (out_weight, VM), (bias, VM)],
        [
            slab, slab, slab, slab,
            (((8, total), WIDE), VM),
            tall,
            tall,
            (((rows, width), WIDE), VM),
            tall,
            (((rows, width), LOW), VM),
            (((3, total, 128), WIDE), VM),
            (((total, 1), jnp.int32), VM),
            (((1, total), jnp.int32), VM),
        ],
        [
            pltpu.VMEM((total, width), LOW),
            pltpu.VMEM((rows, width), LOW),
            pltpu.VMEM((3, width, local), LOW),
            pltpu.VMEM((TILE, total), WIDE),
            pltpu.VMEM((total, 128), WIDE),
            pltpu.SemaphoreType.DMA((2,)),
        ]
        + stream_scratch(rows, width)
        + gather_sems() * 3,
        limit=60,
        flops=7 << 30,
    )


def attend_back_kernel(
    branch_all, normed_all, out_weight, tables, lab_col, lab_row,
    query, key, value, attended, lse, far,
    mixin_out, terms, out_sum, bias_term, far_all,
    branch, normed, mask, inner, heads_back, query_back, key_back, value_back, mixin, mixes,
    sems, outs, out_term, out_inbox, *scratch,
):
    total, width = query.shape
    tiles = total // TILE
    heads = width // HEAD_DIM
    ring = Ring()
    line = Line(ring, *scratch[3:5])
    ring.barrier(line.peers)
    gather = Gather(ring, far_rows(far, ring, 1, total), far_all, *scratch[0:3])
    share = out_term.shape[0] // line.groups

    def share_of(group):
        return pl.ds(pl.multiple_of(group * share, share), share)

    def out_copy(k):
        return line.copy(k, out_term.at[share_of(line.away(k)), :], out_inbox.at[k - 1])

    gather.stage(0)
    loads = load(
        [(branch_all.at[pl.ds(i * TILE, TILE), :], branch.at[pl.ds(i * TILE, TILE), :]) for i in range(tiles)]
        + [(normed_all, normed)],
        sems,
    )
    head_of = lax.broadcasted_iota(jnp.int32, (8, width), 1) // HEAD_DIM
    pick = (head_of == lax.broadcasted_iota(jnp.int32, (8, width), 0)).astype(LOW)
    for i in range(tiles):
        rows = pl.ds(i * TILE, TILE)
        loads[i].wait()
        low = mm(branch[rows, :], out_weight[...], NT).astype(LOW)
        heads_back[rows, :] = low
        prod = low.astype(WIDE) * attended[rows, :].astype(WIDE)
        high = prod.astype(LOW)
        rest = (prod - high.astype(WIDE)).astype(LOW)
        inner[:, rows] = mm(pick, high, NT) + mm(pick, rest, NT)
    out_term[...] = mm(attended[...], branch[...], TN).astype(LOW)
    for k in range(1, line.groups):
        out_copy(k).start()
    gather.stage(1)
    key_back[...] = jnp.zeros_like(key_back)
    value_back[...] = jnp.zeros_like(value_back)
    for i in range(tiles):
        rows = pl.ds(i * TILE, TILE)
        span = (i + 1) * TILE
        k_at = lax.broadcasted_iota(jnp.int32, (span, TILE), 0)
        q_at = i * TILE + lax.broadcasted_iota(jnp.int32, (span, TILE), 1)
        allowed = (lab_col[:span, :] == lab_row[:, rows]) & (q_at >= k_at)
        mask[:span, :] = jnp.where(allowed, 0.0, NEG)
        q = query[rows, :]
        d_out = heads_back[rows, :]

        def one_head(head, q_back):
            mine = head_lanes(q.shape, head)
            q_h = jnp.where(mine, q, jnp.zeros_like(q))
            d_h = jnp.where(mine, d_out, jnp.zeros_like(q))
            k = key[:span, :]
            k_h = jnp.where(head_lanes(k.shape, head), k, jnp.zeros_like(k))
            p = jnp.exp(mm(k, q_h, NT) + mask[:span, :] - lse[pl.ds(head, 1), rows])
            d_p = mm(value[:span, :], d_h, NT)
            d_s = (p * (d_p - inner[pl.ds(head, 1), rows])).astype(LOW)
            value_back[:span, :] += mm(p.astype(LOW), d_h)
            key_back[:span, :] += mm(d_s, q_h)
            return q_back + mm(d_s, k_h, TN)

        query_back[rows, :] = lax.fori_loop(0, heads, one_head, jnp.zeros((TILE, width), WIDE))
        if i >= 2:
            gather.stage(i)
    loads[-1].wait()
    copies = []
    sums = [jnp.zeros((1, width), WIDE)] * 3
    for i in range(tiles):
        rows = pl.ds(i * TILE, TILE)
        q_b = (query_back[rows, :] * (1.0 / 8)).astype(LOW).astype(WIDE)
        k_b = key_back[rows, :].astype(LOW).astype(WIDE)
        trio = [
            turn(q_b, tables, rows, -1).astype(LOW),
            turn(k_b, tables, rows, -1).astype(LOW),
            value_back[rows, :].astype(LOW),
        ]
        for c, item in enumerate(trio):
            mixin[c, rows, :] = item
            sums[c] = sums[c] + jnp.sum(item.astype(WIDE), axis=0, keepdims=True)
    copy = pltpu.make_async_copy(mixin, mixin_out, outs.at[3])
    copy.start()
    copies.append(copy)
    for c in range(3):
        bias_term[c : c + 1, :] = sums[c]
        mixes[c] = mm(normed[...], mixin[c], TN).astype(LOW)
        copy = pltpu.make_async_copy(mixes.at[c], terms.at[c], outs.at[c])
        copy.start()
        copies.append(copy)
    summed = out_term[share_of(ring.group), :].astype(WIDE)
    for k in range(1, line.groups):
        out_copy(k).wait_recv()
        summed = summed + out_inbox[k - 1].astype(WIDE)
    out_sum[...] = summed.astype(LOW)
    gather.stage(4)
    for k in range(1, line.groups):
        out_copy(k).wait_send()
    for copy in copies:
        copy.wait()


def attend_heads_back(
    branch_all, normed_all, out_weight, tables, lab_col, lab_row, saved, far
):
    total, width = normed_all.shape
    local = out_weight.shape[0]
    tiles = total // TILE
    groups = lax.axis_size("grp")
    tall = (((total, width), LOW), ANY)
    return call(
        attend_back_kernel,
        6,
        [(item, ANY) for item in (branch_all, normed_all)]
        + [(item, VM) for item in (out_weight, tables, lab_col, lab_row) + tuple(saved)]
        + [(far, ANY)],
        [
            (((3, total, local), LOW), ANY),
            (((3, width, local), LOW), ANY),
            (((local // groups, width), LOW), VM),
            (((3, local), WIDE), VM),
            tall,
        ],
        [
            pltpu.VMEM((total, width), LOW),
            pltpu.VMEM((total, width), LOW),
            pltpu.VMEM((total, TILE), WIDE),
            pltpu.VMEM((8, total), WIDE),
            pltpu.VMEM((total, local), LOW),
            pltpu.VMEM((total, local), WIDE),
            pltpu.VMEM((total, local), WIDE),
            pltpu.VMEM((total, local), WIDE),
            pltpu.VMEM((3, total, local), LOW),
            pltpu.VMEM((3, width, local), LOW),
            pltpu.SemaphoreType.DMA((tiles + 1,)),
            pltpu.SemaphoreType.DMA((4,)),
            pltpu.VMEM((local, width), LOW),
            pltpu.VMEM((groups - 1, local // groups, width), LOW),
        ]
        + gather_sems()
        + line_sems(),
        limit=60,
        flops=16 << 30,
    )


def units(gate, upper, hidden_back):
    sigma = jax.nn.sigmoid(gate)
    silu = gate * sigma
    return (
        (silu * upper).astype(LOW),
        (hidden_back * (upper * (sigma + silu * (1.0 - sigma)))).astype(LOW),
        (hidden_back * silu).astype(LOW),
    )


def forward_units(two, up, wide, down):
    return units(mm(wide[0], two, NT), mm(wide[1], two, NT), mm(down[...], up, NT))


def feed_kernel(
    two_all, up_all, wide_hbm, down_hbm, far, resid, upstream, gains,
    down_part, begun, far_one, resid_back, branch_all, sums,
    two, up, wide, down, kept, acc, own, sems, outs, *scratch,
):
    total = two_all.shape[0]
    tiles = total // TILE
    ring = Ring()
    met = ring.greet()
    stream = Stream(ring, *scratch[:N_STREAM])
    gather = Gather(ring, far_rows(far, ring, 1, total), far_one, *scratch[N_STREAM : N_STREAM + 3])
    branch = Gather(ring, own, branch_all, *scratch[N_STREAM + 3 :])
    chips = ring.chips()

    def rows_of(chip):
        return pl.ds(pl.multiple_of(chip * TILE, TILE), TILE)

    def tile_loads(step, chip):
        rows = rows_of(chip)
        return [
            pltpu.make_async_copy(two_all.at[rows, :], two.at[rows, :], sems.at[0, step]),
            pltpu.make_async_copy(up_all.at[rows, :], up.at[rows, :], sems.at[1, step]),
        ]

    weights = load([(wide_hbm, wide), (down_hbm, down)], sems.at[2])
    for step in range(tiles):
        for copy in tile_loads(step, chips[step]):
            copy.start()
    met()
    gather.stage(0)
    for copy in weights:
        copy.wait()

    def chip_at(step):
        chip = chips[tiles - 1]
        for i in range(tiles - 1):
            chip = jnp.where(step == i, chips[i], chip)
        return chip

    def body(step, carry):
        chip = chip_at(step)
        for copy in tile_loads(step, chip):
            copy.wait()
        trio = forward_units(two[rows_of(chip), :], up[rows_of(chip), :], wide, down)
        for c in range(3):
            kept[c, :, rows_of(chip)] = trio[c]
        for i in range(1, tiles):

            @pl.when(step == i)
            def _():
                stream.go(i - 1)
                if i == tiles - 1:
                    stream.cross()

        stream.tiles[chip] = (mm(trio[1], wide[0], TN) + mm(trio[2], wide[1], TN)).astype(LOW)
        stream.ready(chip)
        for i in range(tiles):

            @pl.when(step == i)
            def _():
                if i < 3:
                    gather.stage(i + 1)

        return carry

    lax.fori_loop(0, tiles, body, 0)
    unit, scale = unit_of(resid[...])
    stream.finish()
    incoming = stream.total[...]
    back = upstream[...].astype(WIDE) + back_of(incoming, unit, scale, gains[1:2])
    resid_back[...] = back
    own[...] = back.astype(LOW)
    branch.stage(0)
    sums[0:1] = jnp.sum(incoming * unit, axis=0, keepdims=True)
    sums[1:2] = jnp.sum(incoming, axis=0, keepdims=True)

    stream.close()

    def acc_body(i, carry):
        columns = pl.ds(pl.multiple_of(i * TILE, TILE), TILE)
        acc[0, :, columns] = mm(kept[1], two[:, columns])
        acc[1, :, columns] = mm(kept[2], two[:, columns])
        acc[2, :, columns] = mm(kept[0], up[:, columns])

        @pl.when(i == pieces - 2)
        def _():
            branch.stage(1)

        return carry

    pieces = two.shape[1] // TILE
    lax.fori_loop(0, pieces, acc_body, 0)
    keep = pltpu.make_async_copy(acc, begun, outs.at[tiles])
    keep.start()

    def down_copy(i):
        start = i * TILE if isinstance(i, int) else pl.multiple_of(i * TILE, TILE)
        rows = pl.ds(start, TILE)
        return pltpu.make_async_copy(stream.tiles.at[i], down_part.at[rows, :], outs.at[i])

    def down_body(i, carry):
        stream.tiles[i] = mm(kept[0, :, rows_of(i)], down[...], TN).astype(LOW)
        down_copy(i).start()
        for number in (2, 3):

            @pl.when(i == number - 1)
            def _():
                branch.stage(number)

        return carry

    lax.fori_loop(0, tiles, down_body, 0)
    branch.stage(4)
    gather.stage(4)
    keep.wait()
    for i in range(tiles):
        down_copy(i).wait()


def feed(two_all, up_all, wide, down, far, resid, upstream, gains):
    total, width = two_all.shape
    rows = resid.shape[0]
    local = down.shape[0]
    tiles = total // TILE
    tall = (((total, width), LOW), ANY)
    return call(
        feed_kernel,
        7,
        [(item, ANY) for item in (two_all, up_all, wide, down, far)]
        + [(item, VM) for item in (resid, upstream, gains)],
        [
            tall,
            (((3, local, width), WIDE), ANY),
            tall,
            (((rows, width), WIDE), VM),
            tall,
            (((2, width), WIDE), VM),
        ],
        [
            pltpu.VMEM((total, width), LOW),
            pltpu.VMEM((total, width), LOW),
            pltpu.VMEM((2, local, width), LOW),
            pltpu.VMEM((local, width), LOW),
            pltpu.VMEM((3, local, total), LOW),
            pltpu.VMEM((3, local, width), WIDE),
            pltpu.VMEM((rows, width), LOW),
            pltpu.SemaphoreType.DMA((3, tiles)),
            pltpu.SemaphoreType.DMA((1 + tiles,)),
        ]
        + stream_scratch(rows, width)
        + gather_sems() * 2,
        limit=62,
        flops=18 << 30,
    )


N_LAST_GATHERS = 4


def last_kernel(
    mixin_hbm, mix_hbm, down_part, tokens, resid, resid_back, gains, sums, bias_term, out_sum,
    begun, two_far, up_far, up_one, two_one, wide_hbm, down_hbm,
    tokens_grad, layer_out, four, out_grad, wide_grad, down_grad, two_two, two_three, up_two, up_three, mix_part,
    two, up, wide, down, acc, mixin, mix, shelf, inbox, mail, sems, outs, mail_send, mail_recv, *scratch,
):
    total = two_one.shape[0]
    per = total // TILE
    one_scratch, two_scratch, ag = scratch[:11], scratch[11:22], scratch[22:34]
    ring = Ring()
    group, groups = ring.group, lax.axis_size("grp")
    line = Line(ring, *scratch[34:36])
    others = line.peers
    ring.barrier(others)

    one = Scatter(ring, mix_part, *one_scratch)
    second_sum = Scatter(ring, down_part, *two_scratch)
    u2, g2, u3, g3 = [
        Gather(ring, far_rows(far, ring, k, total), dst, *ag[3 * i : 3 * i + 3])
        for i, (far, k, dst) in enumerate(
            ((up_far, 2, up_two), (two_far, 2, two_two), (up_far, 3, up_three), (two_far, 3, two_three))
        )
    ]
    two_sources = (two_one, two_two, two_three)
    up_sources = (up_one, up_two, up_three)

    def first_norm():
        unit, scale = unit_of(tokens[...].astype(WIDE))
        incoming = one.total[...]
        tokens_grad[...] = (resid_back[...] + back_of(incoming, unit, scale, gains[0:1])).astype(LOW)
        four[...] = jnp.zeros_like(four)
        four[0:1] = jnp.sum(incoming * unit, axis=0, keepdims=True)
        four[1:2] = sums[0:1]
        four[2:3] = jnp.sum(incoming, axis=0, keepdims=True)
        four[3:4] = sums[1:2]

    def mail_copy(stage):
        peer = (ring.twin, ring.xn, ring.yn)[stage]
        return ring.copy(mail.at[stage], inbox.at[stage], mail_send, mail_recv, stage, peer)

    def mail_start(stage):
        mail[stage] = four[...]
        mail_copy(stage).start()

    def mail_wait(stage):
        mail_copy(stage).wait_recv()
        four[...] += inbox[stage]

    def group_copy(k):
        return pltpu.make_async_remote_copy(
            src_ref=mail.at[3],
            dst_ref=inbox.at[2 + k],
            send_sem=mail_send.at[2 + k],
            recv_sem=mail_recv.at[2 + k],
            device_id=others[k - 1],
            device_id_type=MESH_ID,
        )

    def group_start():
        four[4:5] = jnp.zeros((1, four.shape[1]), WIDE)
        local = bias_term.shape[1]
        for c in range(3):
            four[4:5, c * local : (c + 1) * local] = bias_term[c : c + 1, :]
        mail[3] = four[...]
        for k in range(1, groups):
            group_copy(k).start()

    def group_wait():
        for k in range(1, groups):
            group_copy(k).wait_recv()
        summed = jnp.zeros(four.shape, WIDE)
        for number in range(groups):
            term = mail[3]
            for k in range(1, groups):
                source = lax.rem(group + groups - k, groups)
                term = jnp.where(source == number, inbox[2 + k], term)
            summed = summed + term
        four[...] = summed
        for stage in range(3):
            mail_copy(stage).wait_send()
        for k in range(1, groups):
            group_copy(k).wait_send()

    share = out_sum.shape[0]

    def out_rows(number):
        return out_grad.at[pl.ds(pl.multiple_of(number * share, share), share), :]

    def out_keep():
        return pltpu.make_async_copy(out_sum, out_rows(group), sems.at[2, 2])

    def out_copy(phase, side):
        number = group - phase * side
        at = 0 if side > 0 else groups
        return pltpu.make_async_remote_copy(
            src_ref=out_sum if phase == 0 else out_rows(number),
            dst_ref=out_rows(number),
            send_sem=line.send.at[at + phase],
            recv_sem=line.recv.at[at + phase],
            device_id=(group + side, ring.me),
            device_id_type=MESH_ID,
        )

    def goes(phase, side):
        number, peer = group - phase * side, group + side
        return (number >= 0) & (number < groups) & (peer >= 0) & (peer < groups)

    def comes(phase, side):
        number = group - (phase + 1) * side
        return (number >= 0) & (number < groups)

    def out_phase(phase):
        for side in (1, -1):
            if phase:

                @pl.when(comes(phase - 1, side))
                def _():
                    out_copy(phase - 1, side).wait_recv()

            if phase < groups - 1:

                @pl.when(goes(phase, side))
                def _():
                    out_copy(phase, side).start()

    def out_end():
        out_keep().wait()
        for phase in range(groups - 1):
            for side in (1, -1):

                @pl.when(goes(phase, side))
                def _():
                    out_copy(phase, side).wait_send()

    def layer_end():
        layer_out[...] = (resid[...] + second_sum.total[...]).astype(LOW)

    def product():
        for copy in mix_loads:
            copy.wait()
        copies = []
        for i in range(per):
            rows = pl.ds(i * TILE, TILE)
            if i >= 2:
                copies[i - 2].wait()
            item = jnp.zeros((TILE, shelf.shape[2]), WIDE)
            for c in range(3):
                item = item + mm(mixin[c, rows, :], mix[c], NT)
            shelf[i % 2] = item.astype(LOW)
            copies.append(pltpu.make_async_copy(shelf.at[i % 2], mix_part.at[rows, :], sems.at[3, i % 2]))
            copies[i].start()
        for copy in copies[-2:]:
            copy.wait()

    def stage(item, number):
        return lambda: item.stage(number)

    plan = {
        1: [stage(u2, 1), stage(g2, 0)],
        2: [stage(u2, 2), lambda: out_phase(1)],
        3: [stage(u2, 3), stage(g2, 1)],
        4: [stage(g2, 2), stage(u3, 0), stage(u2, 4), product, stage(g2, 3), stage(g2, 4), stage(g3, 0)],
        5: [stage(u3, 1), lambda: out_phase(2)],
        6: [stage(u3, 2), stage(g3, 1), stage(one, 0)],
        7: [stage(u3, 3), stage(g3, 2), stage(one, 1)],
        8: [stage(g3, 3), stage(u3, 4), stage(g3, 4), stage(second_sum, 0), lambda: out_phase(3)],
        9: [stage(one, 2), stage(second_sum, 1)],
        10: [stage(one, 3), first_norm, lambda: mail_start(0)],
        11: [lambda: mail_wait(0), lambda: mail_start(1), stage(second_sum, 2)],
    }

    def fetch(source, tile, side):
        start = tile * TILE if isinstance(tile, int) else pl.multiple_of(tile * TILE, TILE)
        rows = pl.ds(start, TILE)
        return [
            pltpu.make_async_copy(two_sources[source].at[rows, :], two.at[side], sems.at[side, 0]),
            pltpu.make_async_copy(up_sources[source].at[rows, :], up.at[side], sems.at[side, 1]),
        ]

    weights = load([(wide_hbm, wide), (down_hbm, down)], sems.at[2])
    for copy in fetch(0, 0, 0):
        copy.start()
    resume = pltpu.make_async_copy(begun, acc, outs.at[0])
    resume.start()
    mix_loads = load([(mixin_hbm, mixin), (mix_hbm, mix)], sems.at[4])
    out_keep().start()
    out_phase(0)
    u2.stage(0)

    def add(side, trio):
        acc[2] += mm(trio[0], up[side])
        acc[0] += mm(trio[1], two[side])
        acc[1] += mm(trio[2], two[side])

    steps = per * (groups - 1)

    def start_fetch(step):
        side = lax.rem(step, 2)
        for source in range(groups - 1):

            @pl.when((step < steps) & (step // per == source))
            def _():
                for copy in fetch(source, lax.rem(step, per), side):
                    copy.start()

    def events(step):
        for at, acts in plan.items():

            @pl.when(step == at)
            def _():
                for act in acts:
                    act()


    for copy in weights:
        copy.wait()
    resume.wait()

    def body(step, carry):
        events(step)
        side = lax.rem(step, 2)

        @pl.when((lax.rem(step, per) == 0) & (step > 0))
        def _():
            start_fetch(step)

        for copy in fetch(0, 0, side):
            copy.wait()

        @pl.when(lax.rem(step + 1, per) != 0)
        def _():
            start_fetch(step + 1)

        add(side, forward_units(two[side], up[side], wide, down))
        return carry

    lax.fori_loop(0, steps, body, 0)
    mail_wait(1)
    mail_start(2)
    wide[...] = acc[0:2].astype(LOW)
    copies = load([(wide, wide_grad)], outs)
    mail_wait(2)
    group_start()
    down[...] = acc[2].astype(LOW)
    copies += load([(down, down_grad)], outs.at[pl.ds(1, 1)])
    second_sum.stage(3)
    layer_end()
    group_wait()
    out_end()
    for copy in copies:
        copy.wait()


def last(mixin, mix, down_part, tokens, resid, resid_back, gains, sums, bias_term, out_sum,
         begun, two_far, up_far, up_one, two_one, wide, down):
    total, width = two_one.shape
    rows = tokens.shape[0]
    local = down.shape[0]
    groups = lax.axis_size("grp")
    tall = (((total, width), LOW), ANY)
    block = (((rows, width), LOW), VM)
    return call(
        last_kernel,
        8,
        [(mixin, ANY), (mix, ANY), (down_part, ANY)]
        + [(item, VM) for item in (tokens, resid, resid_back, gains, sums, bias_term, out_sum)]
        + [(item, ANY) for item in (begun, two_far, up_far, up_one, two_one, wide, down)],
        [
            block,
            block,
            (((8, width), WIDE), VM),
            (((out_sum.shape[0] * groups, width), LOW), ANY),
            (((2, local, width), LOW), ANY),
            (((local, width), LOW), ANY),
            tall, tall, tall, tall, tall,
        ],
        [
            pltpu.VMEM((2, TILE, width), LOW),
            pltpu.VMEM((2, TILE, width), LOW),
            pltpu.VMEM((2, local, width), LOW),
            pltpu.VMEM((local, width), LOW),
            pltpu.VMEM((3, local, width), WIDE),
            pltpu.VMEM(mixin.shape, LOW),
            pltpu.VMEM(mix.shape, LOW),
            pltpu.VMEM((2, TILE, width), LOW),
            pltpu.VMEM((2 + groups, 8, width), WIDE),
            pltpu.VMEM((4, 8, width), WIDE),
            pltpu.SemaphoreType.DMA((5, 3)),
            pltpu.SemaphoreType.DMA((2,)),
            pltpu.SemaphoreType.DMA((2 + groups,)),
            pltpu.SemaphoreType.DMA((2 + groups,)),
        ]
        + scatter_scratch(rows, width) * 2
        + gather_sems() * N_LAST_GATHERS
        + [pltpu.SemaphoreType.DMA((2 * groups,)), pltpu.SemaphoreType.DMA((2 * groups,))],
        limit=62,
        flops=72 << 30,
        cost=120 << 20,
    )


RING = 8


def on_device(
    tokens,
    norm_gains,
    norm_biases,
    mix_weight,
    mix_bias,
    out_weight,
    gate_up_weight,
    down_weight,
    row_lengths,
    row_group,
    cotangent,
):
    count = lax.axis_size("seq")
    shard = lax.axis_index("seq")
    group = lax.axis_index("grp")
    slots_dev = tokens.shape[0]
    load = jnp.sum(jnp.where(row_group == group, row_lengths, 0))
    slots = shard * slots_dev + jnp.arange(slots_dev, dtype=jnp.int32)
    upstream = jnp.where(slots[:, None] < load, cotangent, jnp.zeros_like(cotangent))
    mix_t = jnp.transpose(mix_weight, (1, 0, 2))
    wide_t = jnp.transpose(gate_up_weight, (1, 2, 0))

    up_far = lax.all_gather(upstream, "grp", axis=0, tiled=True)
    (
        query, key, value, attended, lse, normed_all, up_all, resid, two_all, two_mine,
        tables, lab_col, lab_row,
    ) = attend_heads(
        row_lengths, row_group, tokens, norm_gains, norm_biases, upstream, mix_t, out_weight, mix_bias, count
    )
    two_far = lax.all_gather(two_mine, "grp", axis=0, tiled=True)
    down_part, begun, up_one, resid_back, branch_all, sums = feed(
        two_all, up_all, wide_t, down_weight, up_far, resid, upstream, norm_gains
    )
    mixin, mix_term, out_sum, bias_term, two_one = attend_heads_back(
        branch_all, normed_all, out_weight, tables, lab_col, lab_row,
        (query, key, value, attended, lse), two_far,
    )
    mix_grad = lax.psum(mix_term, "grp")
    tokens_grad, layer_out, four, out_grad, wide_grad, down_grad = last(
        mixin, mix_t, down_part, tokens, resid, resid_back, norm_gains, sums, bias_term, out_sum,
        begun, two_far, up_far, up_one, two_one, wide_t, down_weight,
    )[:6]
    local = mix_bias.shape[1]
    return (
        layer_out,
        tokens_grad,
        four[0:2],
        four[2:4],
        jnp.transpose(mix_grad, (1, 0, 2)).astype(jnp.float32),
        four[4, : 3 * local].reshape(3, local),
        out_grad.astype(jnp.float32),
        jnp.transpose(wide_grad, (2, 0, 1)).astype(jnp.float32),
        down_grad.astype(jnp.float32),
    )


def solution(mesh):
    placed = (
        P(("grp", "seq"), None),
        P(),
        P(),
        P(None, None, "seq"),
        P(None, "seq"),
        P("seq", None),
        P(None, None, "seq"),
        P("seq", None),
        P(),
        P(),
        P(("grp", "seq"), None),
    )
    return jax.shard_map(
        on_device if mesh.shape["seq"] == RING else plain_device,
        mesh=mesh,
        in_specs=placed,
        out_specs=(
            P(("grp", "seq"), None),
            P(("grp", "seq"), None),
            P(),
            P(),
            P(None, None, "seq"),
            P(None, "seq"),
            P("seq", None),
            P(None, None, "seq"),
            P("seq", None),
        ),
        check_vma=False,
    )
```

```python
import functools
import math

import jax
import jax.numpy as jnp
from jax import lax
from jax.experimental import pallas as pl
from jax.experimental.pallas import tpu as pltpu
from jax.sharding import PartitionSpec as P

HEAD_DIM = 64
ROT = 16


EPS = 1e-05
NEG = -1e30
BASE = 10000.0


def layer_norm(values, gain, bias):
    centered = values - jnp.mean(values, axis=-1, keepdims=True)
    scale = lax.rsqrt(jnp.mean(centered * centered, axis=-1, keepdims=True) + EPS)
    unit = centered * scale
    return (unit * gain + bias, unit, scale)


def norm_back(incoming, unit, scale, gain):
    along = incoming * gain
    inner = jnp.mean(along, axis=-1, keepdims=True)
    cross = jnp.mean(along * unit, axis=-1, keepdims=True)
    return (
        scale * (along - inner - unit * cross),
        jnp.sum(incoming * unit, axis=0),
        jnp.sum(incoming, axis=0),
    )


def rotate(values, where, sign):
    half = ROT // 2
    freq = BASE ** (-jnp.arange(half, dtype=jnp.float32) / half)
    angle = where.astype(jnp.float32)[:, None] * freq[None, :]
    cosine = jnp.cos(angle)[:, None, :]
    sine = sign * jnp.sin(angle)[:, None, :]
    first = values[..., :half]
    second = values[..., half:ROT]
    return jnp.concatenate(
        [first * cosine - second * sine, second * cosine + first * sine, values[..., ROT:]], axis=-1
    )


def unrotate(lowered, where):
    wide = lowered.astype(jnp.float32)
    turned = jnp.stack(
        [rotate(wide[:, 0], where, -1.0), rotate(wide[:, 1], where, -1.0), wide[:, 2]], axis=1
    )
    return turned.reshape(lowered.shape[0], 3, -1).astype(jnp.bfloat16)


def slot_rows(row_lengths, row_group, group, slots):
    order = jnp.arange(row_lengths.shape[0], dtype=jnp.int32)
    same = row_group == group
    earlier = (order[:, None] > order[None, :]) & same[None, :]
    begin = jnp.sum(jnp.where(earlier, row_lengths[None, :], 0), axis=1)
    finish = begin + row_lengths
    inside = same[None, :] & (slots[:, None] >= begin[None, :]) & (slots[:, None] < finish[None, :])
    label = jnp.sum(jnp.where(inside, order[None, :] + 1, 0), axis=1) - 1
    offset = jnp.sum(jnp.where(inside, slots[:, None] - begin[None, :], 0), axis=1)
    load = jnp.sum(jnp.where(same, row_lengths, 0))
    return (label, jnp.where(label < 0, slots - load, offset))


def block_scores(query, key, label, start, block):
    part = lax.dynamic_slice_in_dim(query, start, block, 0)
    rows = start + jnp.arange(block, dtype=jnp.int32)
    columns = jnp.arange(label.shape[0], dtype=jnp.int32)
    label_rows = lax.dynamic_slice_in_dim(label, start, block, 0)
    allowed = (label_rows[:, None] == label[None, :]) & (rows[:, None] >= columns[None, :])
    scores = jnp.einsum("qhe,khe->hqk", part, key, preferred_element_type=jnp.float32) * (
        1.0 / math.sqrt(query.shape[-1])
    )
    return (part, jnp.where(allowed[None], scores, NEG))


def attend(query, key, value, label, block):

    def one_block(index):
        part, scores = block_scores(query, key, label, index * block, block)
        top = jnp.max(scores, axis=-1, keepdims=True)
        weights = jnp.exp(scores - top)
        totals = jnp.sum(weights, axis=-1, keepdims=True)
        probs = (weights / totals).astype(jnp.bfloat16)
        mixed = jnp.einsum("hqk,khe->qhe", probs, value, preferred_element_type=jnp.float32)
        return (mixed, top[..., 0] + jnp.log(totals[..., 0]))

    mixed, log_totals = lax.map(one_block, jnp.arange(query.shape[0] // block, dtype=jnp.int32))
    return (mixed.reshape(query.shape), log_totals)


def attend_back(query, key, value, label, log_totals, mixed_back, block):
    scale = 1.0 / math.sqrt(query.shape[-1])

    def one_block(carry, index):
        key_back, value_back = carry
        start = index * block
        part, scores = block_scores(query, key, label, start, block)
        back_part = lax.dynamic_slice_in_dim(mixed_back, start, block, 0)
        probs = jnp.exp(scores - log_totals[index][..., None])
        value_back = value_back + jnp.einsum(
            "hqk,qhe->khe",
            probs.astype(jnp.bfloat16),
            back_part,
            preferred_element_type=jnp.float32,
        )
        probs_back = jnp.einsum(
            "qhe,khe->hqk", back_part, value, preferred_element_type=jnp.float32
        )
        inner = jnp.sum(probs_back * probs, axis=-1, keepdims=True)
        score_back = (probs * (probs_back - inner)).astype(jnp.bfloat16)
        query_back = (
            jnp.einsum("hqk,khe->qhe", score_back, key, preferred_element_type=jnp.float32) * scale
        )
        key_back = (
            key_back
            + jnp.einsum("hqk,qhe->khe", score_back, part, preferred_element_type=jnp.float32)
            * scale
        )
        return ((key_back, value_back), query_back)

    empty = jnp.zeros(key.shape, jnp.float32)
    (key_back, value_back), query_back = lax.scan(
        one_block, (empty, empty), jnp.arange(query.shape[0] // block, dtype=jnp.int32)
    )
    return (query_back.reshape(query.shape), key_back, value_back)


def silu_parts(gate_up):
    gate = gate_up[:, 0]
    upper = gate_up[:, 1]
    sigma = jax.nn.sigmoid(gate)
    return (gate * sigma * upper, gate, upper, sigma)


def gate_back(hidden_back, gate, upper, sigma):
    gate_part = hidden_back * upper * sigma * (1.0 + gate * (1.0 - sigma))
    up_part = hidden_back * gate * sigma
    return jnp.stack([gate_part, up_part], axis=1).astype(jnp.bfloat16)


def gather_rows(values):
    return lax.all_gather(values, "seq", axis=0, tiled=True)


def summed_rows(product, left):
    return lax.psum_scatter(
        product(left).astype(jnp.bfloat16), "seq", scatter_dimension=0, tiled=True
    ).astype(jnp.float32)


def plain_device(
    tokens,
    norm_gains,
    norm_biases,
    mix_weight,
    mix_bias,
    out_weight,
    gate_up_weight,
    down_weight,
    row_lengths,
    row_group,
    cotangent,
):
    seq_count = lax.axis_size("seq")
    shard = lax.axis_index("seq")
    group = lax.axis_index("grp")
    slots_dev = tokens.shape[0]
    width = tokens.shape[1]
    group_slots = slots_dev * seq_count
    block = min(512, group_slots)
    local_width = width // seq_count
    local_heads = local_width // HEAD_DIM
    mine = shard * slots_dev + jnp.arange(slots_dev, dtype=jnp.int32)
    label_mine, place_mine = slot_rows(row_lengths, row_group, group, mine)
    label_all, place_all = slot_rows(
        row_lengths, row_group, group, jnp.arange(group_slots, dtype=jnp.int32)
    )
    inputs = tokens.astype(jnp.float32)
    upstream = cotangent.astype(jnp.float32) * (label_mine >= 0).astype(jnp.float32)[:, None]
    upstream_low = upstream.astype(jnp.bfloat16)
    normed, unit_one, scale_one = layer_norm(inputs, norm_gains[0], norm_biases[0])
    normed_all = gather_rows(normed.astype(jnp.bfloat16))
    up_four = lax.all_gather(upstream_low, ("grp", "seq"), axis=0, tiled=True)
    upstream_all = lax.dynamic_slice_in_dim(up_four, group * group_slots, group_slots, 0)
    mixin = jnp.einsum(
        "td,dcf->tcf", normed_all, mix_weight, preferred_element_type=jnp.float32
    ) + mix_bias.astype(jnp.float32)
    heads_in = mixin.reshape(group_slots, 3, local_heads, HEAD_DIM)
    query = rotate(heads_in[:, 0], place_all, 1.0).astype(jnp.bfloat16)
    key = rotate(heads_in[:, 1], place_all, 1.0).astype(jnp.bfloat16)
    value = heads_in[:, 2].astype(jnp.bfloat16)
    mixed, log_totals = attend(query, key, value, label_all, block)
    attended = mixed.reshape(group_slots, local_width).astype(jnp.bfloat16)

    def out_product(part):
        return jnp.dot(part, out_weight, preferred_element_type=jnp.float32)

    resid = inputs + summed_rows(out_product, attended)
    normed_two, unit_two, scale_two = layer_norm(resid, norm_gains[1], norm_biases[1])
    normed_two_low = normed_two.astype(jnp.bfloat16)
    normed_two_all = gather_rows(normed_two_low)
    two_four = lax.all_gather(normed_two_low, ("grp", "seq"), axis=0, tiled=True)

    def up_to_back(two, up):
        gate_up = jnp.einsum("td,dcf->tcf", two, gate_up_weight, preferred_element_type=jnp.float32)
        hidden, gate, upper, sigma = silu_parts(gate_up)
        hidden_back = jnp.einsum("td,fd->tf", up, down_weight, preferred_element_type=jnp.float32)
        return hidden.astype(jnp.bfloat16), gate_back(hidden_back, gate, upper, sigma)

    hidden_low, gate_up_back = up_to_back(normed_two_all, upstream_all)

    def down_product(part):
        return jnp.dot(part, down_weight, preferred_element_type=jnp.float32)

    layer_out = resid + summed_rows(down_product, hidden_low)

    def gate_up_product(part):
        return jnp.einsum("tcf,dcf->td", part, gate_up_weight, preferred_element_type=jnp.float32)

    normed_two_back = summed_rows(gate_up_product, gate_up_back)
    hidden_four, back_four = up_to_back(two_four, up_four)
    down_grad = jnp.einsum("tf,td->fd", hidden_four, up_four, preferred_element_type=jnp.float32)
    gate_up_grad = jnp.einsum(
        "td,tcf->dcf", two_four, back_four, preferred_element_type=jnp.float32
    )
    resid_part, gain_two, bias_two = norm_back(normed_two_back, unit_two, scale_two, norm_gains[1])
    resid_back = upstream + resid_part
    branch_all = gather_rows(resid_back.astype(jnp.bfloat16))
    out_term = jnp.einsum("te,td->ed", attended, branch_all, preferred_element_type=jnp.float32)
    out_grad = lax.psum(out_term.astype(jnp.bfloat16), "grp").astype(jnp.float32)
    attended_back = jnp.einsum(
        "td,ed->te", branch_all, out_weight, preferred_element_type=jnp.float32
    ).astype(jnp.bfloat16)
    heads_back = attended_back.reshape(group_slots, local_heads, HEAD_DIM)
    query_back, key_back, value_back = attend_back(
        query, key, value, label_all, log_totals, heads_back, block
    )
    lowered = jnp.stack([query_back, key_back, value_back], axis=1).astype(jnp.bfloat16)
    mixin_back = unrotate(lowered, place_all)
    mix_term = jnp.einsum("td,tcf->dcf", normed_all, mixin_back, preferred_element_type=jnp.float32)
    mix_grad = lax.psum(mix_term.astype(jnp.bfloat16), "grp").astype(jnp.float32)
    bias_term = jnp.sum(mixin_back, axis=0, dtype=jnp.float32)
    mix_bias_grad = lax.psum(bias_term, "grp")

    def mix_product(part):
        return jnp.einsum("tcf,dcf->td", part, mix_weight, preferred_element_type=jnp.float32)

    normed_back = summed_rows(mix_product, mixin_back)
    tokens_part, gain_one, bias_one = norm_back(normed_back, unit_one, scale_one, norm_gains[0])
    tokens_grad = (resid_back + tokens_part).astype(jnp.bfloat16)
    gains_grad, biases_grad = lax.psum(
        (jnp.stack([gain_one, gain_two]), jnp.stack([bias_one, bias_two])), ("grp", "seq")
    )
    return (
        layer_out.astype(jnp.bfloat16),
        tokens_grad,
        gains_grad,
        biases_grad,
        mix_grad,
        mix_bias_grad,
        out_grad,
        gate_up_grad,
        down_grad,
    )


MESH_ID = pl.DeviceIdType.MESH
N_RS = 10
N_AG = 13


class Ring:
    def __init__(self):
        self.group = lax.axis_index("grp")
        self.me = lax.axis_index("seq")
        core = self.me % 2
        x = (self.me // 2) % 2
        y = self.me // 4
        self.flip = 1 - 2 * core
        self.twin = self.me + self.flip
        self.xn = self.me + 2 - 4 * x
        self.yn = self.me + 4 - 8 * y
        self.dn = self.xn + 4 - 8 * y

    def dev(self, seq):
        return (self.group, seq)

    def greet(self, extra=()):
        sem = pltpu.get_barrier_semaphore()
        peers = [self.dev(self.twin), self.dev(self.xn), self.dev(self.yn)] + list(extra)
        for peer in peers:
            pl.semaphore_signal(sem, inc=1, device_id=peer, device_id_type=MESH_ID)
        return lambda: pl.semaphore_wait(sem, len(peers))

    def barrier(self, extra=()):
        self.greet(extra)()

    def chips(self):
        return [self.dn // 2, self.xn // 2, self.yn // 2, self.me // 2]

    def copy(self, src, dst, send, recv, kind, seq):
        return pltpu.make_async_remote_copy(
            src_ref=src,
            dst_ref=dst,
            send_sem=send.at[kind],
            recv_sem=recv.at[kind],
            device_id=self.dev(seq),
            device_id_type=MESH_ID,
        )


class Line:
    def __init__(self, ring, send, recv):
        self.ring, self.send, self.recv = ring, send, recv
        self.groups = lax.axis_size("grp")
        self.peers = [(self.away(k), ring.me) for k in range(1, self.groups)]

    def away(self, k):
        return lax.rem(self.ring.group + k, self.groups)

    def copy(self, k, src, dst):
        return pltpu.make_async_remote_copy(
            src_ref=src,
            dst_ref=dst,
            send_sem=self.send.at[k - 1],
            recv_sem=self.recv.at[k - 1],
            device_id=self.peers[k - 1],
            device_id_type=MESH_ID,
        )


def line_sems():
    return [pltpu.SemaphoreType.DMA((lax.axis_size("grp"),)), pltpu.SemaphoreType.DMA((lax.axis_size("grp"),))]


class Gather:
    def __init__(self, ring, own, out, send, recv, local):
        self.ring, self.own, self.out = ring, own, out
        self.send, self.recv, self.local = send, recv, local
        self.rows = own.shape[0]
        self.half = self.rows // 2

    def at(self, block, part=None):
        rows, half = self.rows, self.half
        if part is None:
            return self.out.at[pl.ds(pl.multiple_of(block * rows, rows), rows), :]
        return self.out.at[pl.ds(pl.multiple_of(block * rows + part * half, half), half), :]

    def copy(self, kind):
        ring, half = self.ring, self.half
        if kind < 4:
            part, seq = ((0, ring.xn), (1, ring.yn), (1, ring.xn), (0, ring.yn))[kind]
            src, dst = self.own.at[pl.ds(part * half, half), :], self.at(ring.me, part)
        elif kind == 4:
            src, dst, seq = self.own, self.at(ring.me), ring.twin
        else:
            block, part, seq = (
                (ring.xn, 0, ring.yn),
                (ring.xn, 0, ring.twin),
                (ring.yn, 1, ring.xn),
                (ring.yn, 1, ring.twin),
                (ring.xn, 1, ring.twin),
                (ring.yn, 0, ring.twin),
                (ring.dn, 0, ring.twin),
                (ring.dn, 1, ring.twin),
            )[kind - 5]
            src = dst = self.at(block, part)
        return ring.copy(src, dst, self.send, self.recv, kind, seq)

    def keep(self):
        return pltpu.make_async_copy(self.own, self.at(self.ring.me), self.local)

    def stage(self, number):
        if number == 0:
            self.keep().start()
            for kind in range(5):
                self.copy(kind).start()
        elif number == 1:
            self.copy(0).wait_recv()
            self.copy(5).start()
            self.copy(6).start()
            self.copy(1).wait_recv()
            self.copy(7).start()
            self.copy(8).start()
        elif number == 2:
            self.copy(2).wait_recv()
            self.copy(9).start()
            self.copy(3).wait_recv()
            self.copy(10).start()
        elif number == 3:
            self.copy(5).wait_recv()
            self.copy(11).start()
            self.copy(7).wait_recv()
            self.copy(12).start()
        else:
            self.arrive(4, 6, 8, 9, 10, 11, 12)
            self.close()

    def arrive(self, *kinds):
        for kind in kinds:
            self.copy(kind).wait_recv()

    def close_sends(self):
        for kind in range(N_AG):
            self.copy(kind).wait_send()

    def close(self):
        self.keep().wait()
        self.close_sends()

    def all(self):
        for number in range(5):
            self.stage(number)


class Scatter:
    def __init__(self, ring, part, total, own, pair, rx, ry, fx, fy, mid, send, recv, local):
        self.ring, self.part, self.total = ring, part, total
        self.own, self.pair, self.rx, self.ry = own, pair, rx, ry
        self.fx, self.fy, self.mid = fx, fy, mid
        self.send, self.recv, self.local = send, recv, local
        self.rows, self.width = total.shape

    def block(self, index):
        return self.part.at[pl.ds(pl.multiple_of(index * self.rows, self.rows), self.rows), :]

    def index(self, slot):
        ring = self.ring
        return (ring.dn, ring.xn, ring.yn, ring.me)[slot]

    def keep(self, slot):
        return pltpu.make_async_copy(self.block(self.index(slot)), self.own.at[slot], self.local.at[slot])

    def copy(self, kind):
        ring, half = self.ring, self.width // 2
        lo, hi = pl.ds(0, half), pl.ds(half, half)
        if kind < 4:
            src, dst, seq = self.block(self.index(kind) + ring.flip), self.pair.at[kind], ring.twin
        else:
            src, dst, seq = (
                (self.own.at[0, :, lo], self.rx.at[0], ring.xn),
                (self.own.at[0, :, hi], self.ry.at[0], ring.yn),
                (self.own.at[1, :, lo], self.rx.at[1], ring.xn),
                (self.own.at[2, :, hi], self.ry.at[1], ring.yn),
                (self.mid.at[0], self.fy, ring.yn),
                (self.mid.at[1], self.fx, ring.xn),
            )[kind - 4]
        return ring.copy(src, dst, self.send, self.recv, kind, seq)

    def added(self, slot):
        self.keep(slot).wait()
        self.copy(slot).wait_recv()
        return self.own[slot].astype(jnp.float32) + self.pair[slot].astype(jnp.float32)

    def stage(self, number):
        wide, low, half = jnp.float32, self.own.dtype, self.width // 2
        lo, hi = pl.ds(0, half), pl.ds(half, half)
        own, total = self.own, self.total
        if number == 0:
            for slot in range(4):
                self.copy(slot).start()
                self.keep(slot).start()
        elif number == 1:
            own[0] = self.added(0).astype(low)
            self.copy(4).start()
            self.copy(5).start()
            own[1] = self.added(1).astype(low)
            self.copy(6).start()
            own[2] = self.added(2).astype(low)
            self.copy(7).start()
            total[...] = self.added(3)
        elif number == 2:
            self.copy(4).wait_recv()
            self.mid[0] = (own[2, :, lo].astype(wide) + self.rx[0].astype(wide)).astype(low)
            self.copy(8).start()
            self.copy(5).wait_recv()
            self.mid[1] = (own[1, :, hi].astype(wide) + self.ry[0].astype(wide)).astype(low)
            self.copy(9).start()
        else:
            self.copy(6).wait_recv()
            total[:, lo] += self.rx[1].astype(wide)
            self.copy(7).wait_recv()
            total[:, hi] += self.ry[1].astype(wide)
            self.copy(8).wait_recv()
            total[:, lo] += self.fy[...].astype(wide)
            self.copy(9).wait_recv()
            total[:, hi] += self.fx[...].astype(wide)
            for kind in range(N_RS):
                self.copy(kind).wait_send()

    def all(self):
        for number in range(4):
            self.stage(number)


class Stream:
    def __init__(self, ring, tiles, total, pair, rx, ry, fx, fy, mid, send, recv):
        self.ring, self.tiles, self.total, self.pair = ring, tiles, total, pair
        self.rx, self.ry, self.fx, self.fy, self.mid = rx, ry, fx, fy, mid
        self.send, self.recv = send, recv
        self.rows, self.width = total.shape
        self.at = ring.chips()

    def rows_of(self, twin):
        core = self.ring.me % 2
        core = 1 - core if twin else core
        return pl.ds(pl.multiple_of(core * self.rows, self.rows), self.rows)

    def copy(self, kind):
        ring, half = self.ring, self.width // 2
        lo, hi = pl.ds(0, half), pl.ds(half, half)
        mine = self.rows_of(False)
        dn, xn, yn, _ = self.at
        src, dst, seq = (
            (self.tiles.at[dn, mine, lo], self.rx.at[0], ring.xn),
            (self.tiles.at[dn, mine, hi], self.ry.at[0], ring.yn),
            (self.tiles.at[xn, mine, lo], self.rx.at[1], ring.xn),
            (self.tiles.at[yn, mine, hi], self.ry.at[1], ring.yn),
            (self.mid.at[0], self.fy, ring.yn),
            (self.mid.at[1], self.fx, ring.xn),
        )[kind - 4]
        return ring.copy(src, dst, self.send, self.recv, kind, seq)

    def pair_copy(self, chip):
        return self.ring.copy(
            self.tiles.at[chip, self.rows_of(True), :],
            self.pair.at[chip],
            self.send,
            self.recv,
            chip,
            self.ring.twin,
        )

    def ready(self, chip):
        self.pair_copy(chip).start()

    def added(self, chip):
        self.pair_copy(chip).wait_recv()
        mine = self.rows_of(False)
        return self.tiles[chip, mine, :].astype(jnp.float32) + self.pair[chip].astype(jnp.float32)

    def go(self, which):
        chip = self.at[which]
        self.tiles[chip, self.rows_of(False), :] = self.added(chip).astype(self.tiles.dtype)
        for kind in ((4, 5), (6,), (7,))[which]:
            self.copy(kind).start()

    def cross(self):
        wide, low, half = jnp.float32, self.tiles.dtype, self.width // 2
        lo, hi = pl.ds(0, half), pl.ds(half, half)
        mine = self.rows_of(False)
        _, xn, yn, _ = self.at
        self.copy(4).wait_recv()
        self.mid[0] = (self.tiles[yn, mine, lo].astype(wide) + self.rx[0].astype(wide)).astype(low)
        self.copy(8).start()
        self.copy(5).wait_recv()
        self.mid[1] = (self.tiles[xn, mine, hi].astype(wide) + self.ry[0].astype(wide)).astype(low)
        self.copy(9).start()

    def finish(self):
        wide, half = jnp.float32, self.width // 2
        lo, hi = pl.ds(0, half), pl.ds(half, half)
        total = self.total
        total[...] = self.added(self.at[3])
        self.copy(6).wait_recv()
        total[:, lo] += self.rx[1].astype(wide)
        self.copy(7).wait_recv()
        total[:, hi] += self.ry[1].astype(wide)
        self.copy(8).wait_recv()
        total[:, lo] += self.fy[...].astype(wide)
        self.copy(9).wait_recv()
        total[:, hi] += self.fx[...].astype(wide)

    def close(self):
        for chip in range(4):
            self.pair_copy(chip).wait_send()
        for kind in range(4, N_RS):
            self.copy(kind).wait_send()


def stream_scratch(rows, width):
    low = jnp.bfloat16
    half = width // 2
    return [
        pltpu.VMEM((4, 2 * rows, width), low),
        pltpu.VMEM((rows, width), jnp.float32),
        pltpu.VMEM((4, rows, width), low),
        pltpu.VMEM((2, rows, half), low),
        pltpu.VMEM((2, rows, half), low),
        pltpu.VMEM((rows, half), low),
        pltpu.VMEM((rows, half), low),
        pltpu.VMEM((2, rows, half), low),
        pltpu.SemaphoreType.DMA((N_RS,)),
        pltpu.SemaphoreType.DMA((N_RS,)),
    ]


N_STREAM = 10


def scatter_buffers(rows, width):
    low = jnp.bfloat16
    half = width // 2
    return [
        pltpu.VMEM((rows, width), jnp.float32),
        pltpu.VMEM((4, rows, width), low),
        pltpu.VMEM((4, rows, width), low),
        pltpu.VMEM((2, rows, half), low),
        pltpu.VMEM((2, rows, half), low),
        pltpu.VMEM((rows, half), low),
        pltpu.VMEM((rows, half), low),
        pltpu.VMEM((2, rows, half), low),
    ]


def scatter_sems():
    return [
        pltpu.SemaphoreType.DMA((N_RS,)),
        pltpu.SemaphoreType.DMA((N_RS,)),
        pltpu.SemaphoreType.DMA((4,)),
    ]


def scatter_scratch(rows, width):
    return scatter_buffers(rows, width) + scatter_sems()


def gather_sems():
    return [
        pltpu.SemaphoreType.DMA((N_AG,)),
        pltpu.SemaphoreType.DMA((N_AG,)),
        pltpu.SemaphoreType.DMA,
    ]


def gather_scratch(rows, width):
    return [pltpu.VMEM((rows, width), jnp.bfloat16)] + gather_sems()


def unit_of(values):
    centered = values - jnp.mean(values, axis=-1, keepdims=True)
    scale = lax.rsqrt(jnp.mean(centered * centered, axis=-1, keepdims=True) + EPS)
    return centered * scale, scale


def back_of(incoming, unit, scale, gain):
    along = incoming * gain
    inner = jnp.mean(along, axis=-1, keepdims=True)
    cross = jnp.mean(along * unit, axis=-1, keepdims=True)
    return scale * (along - inner - unit * cross)


VM = pl.BlockSpec(memory_space=pltpu.VMEM)
ANY = pl.BlockSpec(memory_space=pltpu.HBM)
SM = pl.BlockSpec(memory_space=pltpu.SMEM)


def call(kernel, number, ins, outs, scratch, limit=60, flops=0, cost=20_000_000, scratch_in=None):
    return pl.pallas_call(
        kernel,
        out_shape=tuple(jax.ShapeDtypeStruct(*shape) for shape, _ in outs),
        in_specs=[spec for _, spec in ins],
        out_specs=tuple(spec for _, spec in outs),
        scratch_shapes=scratch,
        compiler_params=pltpu.CompilerParams(
            collective_id=number,
            has_side_effects=True,
            vmem_limit_bytes=limit << 20,
        ),
        cost_estimate=pl.CostEstimate(flops=flops, bytes_accessed=cost, transcendentals=0),
    )(*[value for value, _ in ins])


TILE = 256
WIDE = jnp.float32
LOW = jnp.bfloat16
NT = (((1,), (1,)), ((), ()))
TN = (((0,), (0,)), ((), ()))


def mm(a, b, dims=(((1,), (0,)), ((), ()))):
    return lax.dot_general(a, b, dims, preferred_element_type=WIDE)


def far_rows(far, ring, away, total):
    groups = lax.axis_size("grp")
    rows = far.shape[0] // groups
    index = lax.rem(ring.group + away, groups)
    return far.at[pl.ds(pl.multiple_of(index * rows, rows), rows), :]


def head_lanes(shape, head):
    return lax.broadcasted_iota(jnp.int32, shape, 1) // HEAD_DIM == head


def turn(u, tables, rows, sign):
    cosine, below, above = (
        jnp.concatenate([tables[i, rows, :]] * (u.shape[1] // 128), axis=1) for i in range(3)
    )
    side = pltpu.roll(u, 8, 1) * below + pltpu.roll(u, u.shape[1] - 8, 1) * above
    return u * cosine + side if sign > 0 else u * cosine - side


def load(pairs, sems):
    copies = []
    for i, (src, dst) in enumerate(pairs):
        copy = pltpu.make_async_copy(src, dst, sems.at[i])
        copy.start()
        copies.append(copy)
    return copies


def rows_layout(row_lengths, row_group, group, tables, lab_col, lab_row):
    total = lab_col.shape[0]
    rows, begin = [], jnp.int32(0)
    for row in range(row_lengths.shape[0]):
        mine = row_group[row] == group
        rows.append((row, mine, begin, begin + row_lengths[row]))
        begin = begin + jnp.where(mine, row_lengths[row], 0)

    def lay(slots):
        label, base = jnp.full(slots.shape, -1, jnp.int32), jnp.full(slots.shape, begin, jnp.int32)
        for row, mine, first, end in rows:
            first, end = jnp.where(mine, first, -1), jnp.where(mine, end, -1)
            inside = (slots >= first) & (slots < end)
            label = jnp.where(inside, row, label)
            base = jnp.where(inside, first, base)
        return label, slots - base

    lab_row[...] = lay(lax.broadcasted_iota(jnp.int32, (1, total), 1))[0]
    half = ROT // 2

    def body(i, carry):
        at = pl.ds(pl.multiple_of(i * TILE, TILE), TILE)
        label, place = lay(i * TILE + lax.broadcasted_iota(jnp.int32, (TILE, 1), 0))
        lab_col[at, :] = label
        lane = lax.broadcasted_iota(jnp.int32, (TILE, 128), 1) % HEAD_DIM
        freq = jnp.ones((TILE, 128), WIDE)
        for e in range(1, half):
            freq = jnp.where(lane % half == e, BASE ** (-e / half), freq)
        angle = place.astype(WIDE) * freq
        cosine, sine = jnp.cos(angle), jnp.sin(angle)
        tables[0, at, :] = jnp.where(lane < ROT, cosine, 1.0)
        tables[1, at, :] = jnp.where((lane >= half) & (lane < ROT), sine, 0.0)
        tables[2, at, :] = jnp.where(lane < half, -sine, 0.0)
        return carry

    lax.fori_loop(0, total // TILE, body, 0)


def attend_kernel(
    row_lengths, row_group, tokens, gains, biases, upstream, weight, out_weight, bias,
    query, key, value, attended, lse, normed_all, up_all, resid, two_all, two_own, tables, lab_col, lab_row,
    normed, own, w, mask, stats, sems, *scratch,
):
    total, width = query.shape
    tiles = total // TILE
    ring = Ring()
    met = ring.greet()
    copy_w = pltpu.make_async_copy(weight, w, sems.at[0])
    copy_w.start()
    stream = Stream(ring, *scratch[:N_STREAM])
    scratch = scratch[N_STREAM:]
    gather = Gather(ring, own, normed, *scratch[0:3])
    upper = Gather(ring, upstream, up_all, *scratch[3:6])
    after = Gather(ring, two_own, two_all, *scratch[6:9])
    unit, _ = unit_of(tokens[...].astype(WIDE))
    own[...] = (unit * gains[0:1] + biases[0:1]).astype(LOW)
    met()
    gather.stage(0)
    rows_layout(row_lengths, row_group, ring.group, tables, lab_col, lab_row)
    gather.keep().wait()
    copy_w.wait()

    def mix(chip):
        rows = pl.ds(pl.multiple_of(chip * TILE, TILE), TILE)
        x = normed[rows, :]
        u = mm(x, w[0]) + bias[0:1].astype(WIDE)
        query[rows, :] = (turn(u, tables, rows, 1).astype(LOW).astype(WIDE) * (1.0 / 8)).astype(LOW)
        u = mm(x, w[1]) + bias[1:2].astype(WIDE)
        key[rows, :] = turn(u, tables, rows, 1).astype(LOW)
        value[rows, :] = (mm(x, w[2]) + bias[2:3].astype(WIDE)).astype(LOW)

    chips = ring.chips()

    def mix_body(step, carry):
        for i, acts in enumerate(
            (
                ((4,), ()),
                ((6, 9), (1, 2)),
                ((8, 10), (3,)),
                ((11, 12), ()),
            )
        ):

            @pl.when(step == i)
            def _():
                for number in acts[1]:
                    gather.stage(number)
                if i == 2:
                    upper.stage(0)
                gather.arrive(*acts[0])

        chip = chips[0]
        for i in range(1, tiles):
            chip = jnp.where(step == tiles - 1 - i, chips[(3, 1, 2)[tiles - 1 - i]], chip)
        mix(chip)
        return carry

    lax.fori_loop(0, tiles, mix_body, 0)
    keep = pltpu.make_async_copy(normed, normed_all, sems.at[1])
    keep.start()
    def tile(i):
        rows = pl.ds(i * TILE, TILE)
        span = (i + 1) * TILE
        q_at = i * TILE + lax.broadcasted_iota(jnp.int32, (TILE, span), 0)
        k_at = lax.broadcasted_iota(jnp.int32, (TILE, span), 1)
        allowed = (lab_col[rows, :] == lab_row[:, :span]) & (q_at >= k_at)
        mask[:, :span] = jnp.where(allowed, 0.0, NEG)
        q = query[rows, :]

        def one_head(head, carry):
            mixed, logs = carry
            mine = head_lanes(q.shape, head)
            s = mm(jnp.where(mine, q, jnp.zeros_like(q)), key[:span, :], NT) + mask[:, :span]
            top = jnp.max(s, axis=1, keepdims=True)
            p = jnp.exp(s - top)
            norm = jnp.sum(p, axis=1, keepdims=True)
            o = mm(p.astype(LOW), value[:span, :]) / norm
            mixed = jnp.where(mine, o, mixed)
            lane = lax.broadcasted_iota(jnp.int32, logs.shape, 1)
            logs = jnp.where(lane == head, top + jnp.log(norm), logs)
            return mixed, logs

        mixed, logs = lax.fori_loop(
            0, width // HEAD_DIM, one_head,
            (jnp.zeros((TILE, width), WIDE), jnp.zeros((TILE, 128), WIDE)),
        )
        low = mixed.astype(LOW)
        attended[rows, :] = low
        stats[rows, :] = logs
        stream.tiles[i] = mm(low, out_weight[...]).astype(LOW)

    def attend_body(step, carry):
        chip = chips[tiles - 1]
        for i in range(tiles - 1):
            chip = jnp.where(step == i, chips[i], chip)
        for i in range(tiles):

            @pl.when(chip == i)
            def _():
                tile(i)

        stream.ready(chip)
        for i in range(tiles):

            @pl.when(step == i)
            def _():
                if i:
                    stream.go(i - 1)
                if i < 3:
                    upper.stage(i + 1)

        return carry

    lax.fori_loop(0, tiles, attend_body, 0)
    stream.cross()
    lse[...] = jnp.transpose(stats[...])[:8, :]
    stream.finish()
    resid[...] = stream.total[...] + tokens[...].astype(WIDE)
    unit, _ = unit_of(resid[...])
    two_own[...] = (unit * gains[1:2] + biases[1:2]).astype(LOW)
    after.all()
    upper.stage(4)
    gather.close_sends()
    stream.close()
    keep.wait()


def attend_heads(
    row_lengths, row_group, tokens, gains, biases, upstream, weight, out_weight, bias, count
):
    rows, width = tokens.shape
    total = rows * count
    local = out_weight.shape[0]
    slab = (((total, local), LOW), VM)
    tall = (((total, width), LOW), ANY)
    return call(
        attend_kernel,
        5,
        [(row_lengths, SM), (row_group, SM), (tokens, VM), (gains, VM), (biases, VM), (upstream, VM)]
        + [(weight, ANY), (out_weight, VM), (bias, VM)],
        [
            slab, slab, slab, slab,
            (((8, total), WIDE), VM),
            tall,
            tall,
            (((rows, width), WIDE), VM),
            tall,
            (((rows, width), LOW), VM),
            (((3, total, 128), WIDE), VM),
            (((total, 1), jnp.int32), VM),
            (((1, total), jnp.int32), VM),
        ],
        [
            pltpu.VMEM((total, width), LOW),
            pltpu.VMEM((rows, width), LOW),
            pltpu.VMEM((3, width, local), LOW),
            pltpu.VMEM((TILE, total), WIDE),
            pltpu.VMEM((total, 128), WIDE),
            pltpu.SemaphoreType.DMA((2,)),
        ]
        + stream_scratch(rows, width)
        + gather_sems() * 3,
        limit=60,
        flops=7 << 30,
    )


def attend_back_kernel(
    branch_all, normed_all, out_weight, tables, lab_col, lab_row,
    query, key, value, attended, lse, far,
    mixin_out, terms, out_sum, bias_term, far_all,
    branch, normed, mask, inner, heads_back, query_back, key_back, value_back, mixin, mixes,
    sems, outs, out_term, out_inbox, *scratch,
):
    total, width = query.shape
    tiles = total // TILE
    heads = width // HEAD_DIM
    ring = Ring()
    line = Line(ring, *scratch[3:5])
    ring.barrier(line.peers)
    gather = Gather(ring, far_rows(far, ring, 1, total), far_all, *scratch[0:3])
    share = out_term.shape[0] // line.groups

    def share_of(group):
        return pl.ds(pl.multiple_of(group * share, share), share)

    def out_copy(k):
        return line.copy(k, out_term.at[share_of(line.away(k)), :], out_inbox.at[k - 1])

    gather.stage(0)
    loads = load(
        [(branch_all.at[pl.ds(i * TILE, TILE), :], branch.at[pl.ds(i * TILE, TILE), :]) for i in range(tiles)]
        + [(normed_all, normed)],
        sems,
    )
    head_of = lax.broadcasted_iota(jnp.int32, (8, width), 1) // HEAD_DIM
    pick = (head_of == lax.broadcasted_iota(jnp.int32, (8, width), 0)).astype(LOW)
    for i in range(tiles):
        rows = pl.ds(i * TILE, TILE)
        loads[i].wait()
        low = mm(branch[rows, :], out_weight[...], NT).astype(LOW)
        heads_back[rows, :] = low
        prod = low.astype(WIDE) * attended[rows, :].astype(WIDE)
        high = prod.astype(LOW)
        rest = (prod - high.astype(WIDE)).astype(LOW)
        inner[:, rows] = mm(pick, high, NT) + mm(pick, rest, NT)
    out_term[...] = mm(attended[...], branch[...], TN).astype(LOW)
    for k in range(1, line.groups):
        out_copy(k).start()
    gather.stage(1)
    key_back[...] = jnp.zeros_like(key_back)
    value_back[...] = jnp.zeros_like(value_back)
    for i in range(tiles):
        rows = pl.ds(i * TILE, TILE)
        span = (i + 1) * TILE
        k_at = lax.broadcasted_iota(jnp.int32, (span, TILE), 0)
        q_at = i * TILE + lax.broadcasted_iota(jnp.int32, (span, TILE), 1)
        allowed = (lab_col[:span, :] == lab_row[:, rows]) & (q_at >= k_at)
        mask[:span, :] = jnp.where(allowed, 0.0, NEG)
        q = query[rows, :]
        d_out = heads_back[rows, :]

        def one_head(head, q_back):
            mine = head_lanes(q.shape, head)
            q_h = jnp.where(mine, q, jnp.zeros_like(q))
            d_h = jnp.where(mine, d_out, jnp.zeros_like(q))
            k = key[:span, :]
            k_h = jnp.where(head_lanes(k.shape, head), k, jnp.zeros_like(k))
            p = jnp.exp(mm(k, q_h, NT) + mask[:span, :] - lse[pl.ds(head, 1), rows])
            d_p = mm(value[:span, :], d_h, NT)
            d_s = (p * (d_p - inner[pl.ds(head, 1), rows])).astype(LOW)
            value_back[:span, :] += mm(p.astype(LOW), d_h)
            key_back[:span, :] += mm(d_s, q_h)
            return q_back + mm(d_s, k_h, TN)

        query_back[rows, :] = lax.fori_loop(0, heads, one_head, jnp.zeros((TILE, width), WIDE))
        if i >= 2:
            gather.stage(i)
    loads[-1].wait()
    copies = []
    sums = [jnp.zeros((1, width), WIDE)] * 3
    for i in range(tiles):
        rows = pl.ds(i * TILE, TILE)
        q_b = (query_back[rows, :] * (1.0 / 8)).astype(LOW).astype(WIDE)
        k_b = key_back[rows, :].astype(LOW).astype(WIDE)
        trio = [
            turn(q_b, tables, rows, -1).astype(LOW),
            turn(k_b, tables, rows, -1).astype(LOW),
            value_back[rows, :].astype(LOW),
        ]
        for c, item in enumerate(trio):
            mixin[c, rows, :] = item
            sums[c] = sums[c] + jnp.sum(item.astype(WIDE), axis=0, keepdims=True)
    copy = pltpu.make_async_copy(mixin, mixin_out, outs.at[3])
    copy.start()
    copies.append(copy)
    for c in range(3):
        bias_term[c : c + 1, :] = sums[c]
        mixes[c] = mm(normed[...], mixin[c], TN).astype(LOW)
        copy = pltpu.make_async_copy(mixes.at[c], terms.at[c], outs.at[c])
        copy.start()
        copies.append(copy)
    summed = out_term[share_of(ring.group), :].astype(WIDE)
    for k in range(1, line.groups):
        out_copy(k).wait_recv()
        summed = summed + out_inbox[k - 1].astype(WIDE)
    out_sum[...] = summed.astype(LOW)
    gather.stage(4)
    for k in range(1, line.groups):
        out_copy(k).wait_send()
    for copy in copies:
        copy.wait()


def attend_heads_back(
    branch_all, normed_all, out_weight, tables, lab_col, lab_row, saved, far
):
    total, width = normed_all.shape
    local = out_weight.shape[0]
    tiles = total // TILE
    groups = lax.axis_size("grp")
    tall = (((total, width), LOW), ANY)
    return call(
        attend_back_kernel,
        6,
        [(item, ANY) for item in (branch_all, normed_all)]
        + [(item, VM) for item in (out_weight, tables, lab_col, lab_row) + tuple(saved)]
        + [(far, ANY)],
        [
            (((3, total, local), LOW), ANY),
            (((3, width, local), LOW), ANY),
            (((local // groups, width), LOW), VM),
            (((3, local), WIDE), VM),
            tall,
        ],
        [
            pltpu.VMEM((total, width), LOW),
            pltpu.VMEM((total, width), LOW),
            pltpu.VMEM((total, TILE), WIDE),
            pltpu.VMEM((8, total), WIDE),
            pltpu.VMEM((total, local), LOW),
            pltpu.VMEM((total, local), WIDE),
            pltpu.VMEM((total, local), WIDE),
            pltpu.VMEM((total, local), WIDE),
            pltpu.VMEM((3, total, local), LOW),
            pltpu.VMEM((3, width, local), LOW),
            pltpu.SemaphoreType.DMA((tiles + 1,)),
            pltpu.SemaphoreType.DMA((4,)),
            pltpu.VMEM((local, width), LOW),
            pltpu.VMEM((groups - 1, local // groups, width), LOW),
        ]
        + gather_sems()
        + line_sems(),
        limit=60,
        flops=16 << 30,
    )


def units(gate, upper, hidden_back):
    sigma = jax.nn.sigmoid(gate)
    silu = gate * sigma
    return (
        (silu * upper).astype(LOW),
        (hidden_back * (upper * (sigma + silu * (1.0 - sigma)))).astype(LOW),
        (hidden_back * silu).astype(LOW),
    )


def forward_units(two, up, wide, down):
    return units(mm(wide[0], two, NT), mm(wide[1], two, NT), mm(down[...], up, NT))


def feed_kernel(
    two_all, up_all, wide_hbm, down_hbm, far, resid, upstream, gains,
    down_part, begun, far_one, resid_back, branch_all, sums,
    two, up, wide, down, kept, acc, own, sems, outs, *scratch,
):
    total = two_all.shape[0]
    tiles = total // TILE
    ring = Ring()
    met = ring.greet()
    stream = Stream(ring, *scratch[:N_STREAM])
    gather = Gather(ring, far_rows(far, ring, 1, total), far_one, *scratch[N_STREAM : N_STREAM + 3])
    branch = Gather(ring, own, branch_all, *scratch[N_STREAM + 3 :])
    chips = ring.chips()

    def rows_of(chip):
        return pl.ds(pl.multiple_of(chip * TILE, TILE), TILE)

    def tile_loads(step, chip):
        rows = rows_of(chip)
        return [
            pltpu.make_async_copy(two_all.at[rows, :], two.at[rows, :], sems.at[0, step]),
            pltpu.make_async_copy(up_all.at[rows, :], up.at[rows, :], sems.at[1, step]),
        ]

    weights = load([(wide_hbm, wide), (down_hbm, down)], sems.at[2])
    for step in range(tiles):
        for copy in tile_loads(step, chips[step]):
            copy.start()
    met()
    gather.stage(0)
    for copy in weights:
        copy.wait()

    def chip_at(step):
        chip = chips[tiles - 1]
        for i in range(tiles - 1):
            chip = jnp.where(step == i, chips[i], chip)
        return chip

    def body(step, carry):
        chip = chip_at(step)
        for copy in tile_loads(step, chip):
            copy.wait()
        trio = forward_units(two[rows_of(chip), :], up[rows_of(chip), :], wide, down)
        for c in range(3):
            kept[c, :, rows_of(chip)] = trio[c]
        for i in range(1, tiles):

            @pl.when(step == i)
            def _():
                stream.go(i - 1)
                if i == tiles - 1:
                    stream.cross()

        stream.tiles[chip] = (mm(trio[1], wide[0], TN) + mm(trio[2], wide[1], TN)).astype(LOW)
        stream.ready(chip)
        for i in range(tiles):

            @pl.when(step == i)
            def _():
                if i < 3:
                    gather.stage(i + 1)

        return carry

    lax.fori_loop(0, tiles, body, 0)
    unit, scale = unit_of(resid[...])
    stream.finish()
    incoming = stream.total[...]
    back = upstream[...].astype(WIDE) + back_of(incoming, unit, scale, gains[1:2])
    resid_back[...] = back
    own[...] = back.astype(LOW)
    branch.stage(0)
    sums[0:1] = jnp.sum(incoming * unit, axis=0, keepdims=True)
    sums[1:2] = jnp.sum(incoming, axis=0, keepdims=True)

    stream.close()

    def acc_body(i, carry):
        columns = pl.ds(pl.multiple_of(i * TILE, TILE), TILE)
        acc[0, :, columns] = mm(kept[1], two[:, columns])
        acc[1, :, columns] = mm(kept[2], two[:, columns])
        acc[2, :, columns] = mm(kept[0], up[:, columns])

        @pl.when(i == pieces - 2)
        def _():
            branch.stage(1)

        return carry

    pieces = two.shape[1] // TILE
    lax.fori_loop(0, pieces, acc_body, 0)
    keep = pltpu.make_async_copy(acc, begun, outs.at[tiles])
    keep.start()

    def down_copy(i):
        start = i * TILE if isinstance(i, int) else pl.multiple_of(i * TILE, TILE)
        rows = pl.ds(start, TILE)
        return pltpu.make_async_copy(stream.tiles.at[i], down_part.at[rows, :], outs.at[i])

    def down_body(i, carry):
        stream.tiles[i] = mm(kept[0, :, rows_of(i)], down[...], TN).astype(LOW)
        down_copy(i).start()
        for number in (2, 3):

            @pl.when(i == number - 1)
            def _():
                branch.stage(number)

        return carry

    lax.fori_loop(0, tiles, down_body, 0)
    branch.stage(4)
    gather.stage(4)
    keep.wait()
    for i in range(tiles):
        down_copy(i).wait()


def feed(two_all, up_all, wide, down, far, resid, upstream, gains):
    total, width = two_all.shape
    rows = resid.shape[0]
    local = down.shape[0]
    tiles = total // TILE
    tall = (((total, width), LOW), ANY)
    return call(
        feed_kernel,
        7,
        [(item, ANY) for item in (two_all, up_all, wide, down, far)]
        + [(item, VM) for item in (resid, upstream, gains)],
        [
            tall,
            (((3, local, width), WIDE), ANY),
            tall,
            (((rows, width), WIDE), VM),
            tall,
            (((2, width), WIDE), VM),
        ],
        [
            pltpu.VMEM((total, width), LOW),
            pltpu.VMEM((total, width), LOW),
            pltpu.VMEM((2, local, width), LOW),
            pltpu.VMEM((local, width), LOW),
            pltpu.VMEM((3, local, total), LOW),
            pltpu.VMEM((3, local, width), WIDE),
            pltpu.VMEM((rows, width), LOW),
            pltpu.SemaphoreType.DMA((3, tiles)),
            pltpu.SemaphoreType.DMA((1 + tiles,)),
        ]
        + stream_scratch(rows, width)
        + gather_sems() * 2,
        limit=62,
        flops=18 << 30,
    )


N_LAST_GATHERS = 4


def last_kernel(
    mixin_hbm, mix_hbm, down_part, tokens, resid, resid_back, gains, sums, bias_term, out_sum,
    begun, two_far, up_far, up_one, two_one, wide_hbm, down_hbm,
    tokens_grad, layer_out, four, out_grad, wide_grad, down_grad, two_two, two_three, up_two, up_three, mix_part,
    two, up, wide, down, acc, mixin, mix, shelf, inbox, mail, sems, outs, mail_send, mail_recv, *scratch,
):
    total = two_one.shape[0]
    per = total // TILE
    one_scratch, two_scratch, ag = scratch[:11], scratch[11:22], scratch[22:34]
    ring = Ring()
    group, groups = ring.group, lax.axis_size("grp")
    line = Line(ring, *scratch[34:36])
    others = line.peers
    ring.barrier(others)

    one = Scatter(ring, mix_part, *one_scratch)
    second_sum = Scatter(ring, down_part, *two_scratch)
    u2, g2, u3, g3 = [
        Gather(ring, far_rows(far, ring, k, total), dst, *ag[3 * i : 3 * i + 3])
        for i, (far, k, dst) in enumerate(
            ((up_far, 2, up_two), (two_far, 2, two_two), (up_far, 3, up_three), (two_far, 3, two_three))
        )
    ]
    two_sources = (two_one, two_two, two_three)
    up_sources = (up_one, up_two, up_three)

    def first_norm():
        unit, scale = unit_of(tokens[...].astype(WIDE))
        incoming = one.total[...]
        tokens_grad[...] = (resid_back[...] + back_of(incoming, unit, scale, gains[0:1])).astype(LOW)
        four[...] = jnp.zeros_like(four)
        four[0:1] = jnp.sum(incoming * unit, axis=0, keepdims=True)
        four[1:2] = sums[0:1]
        four[2:3] = jnp.sum(incoming, axis=0, keepdims=True)
        four[3:4] = sums[1:2]

    def mail_copy(stage):
        peer = (ring.twin, ring.xn, ring.yn)[stage]
        return ring.copy(mail.at[stage], inbox.at[stage], mail_send, mail_recv, stage, peer)

    def mail_start(stage):
        mail[stage] = four[...]
        mail_copy(stage).start()

    def mail_wait(stage):
        mail_copy(stage).wait_recv()
        four[...] += inbox[stage]

    def group_copy(k):
        return pltpu.make_async_remote_copy(
            src_ref=mail.at[3],
            dst_ref=inbox.at[2 + k],
            send_sem=mail_send.at[2 + k],
            recv_sem=mail_recv.at[2 + k],
            device_id=others[k - 1],
            device_id_type=MESH_ID,
        )

    def group_start():
        four[4:5] = jnp.zeros((1, four.shape[1]), WIDE)
        local = bias_term.shape[1]
        for c in range(3):
            four[4:5, c * local : (c + 1) * local] = bias_term[c : c + 1, :]
        mail[3] = four[...]
        for k in range(1, groups):
            group_copy(k).start()

    def group_wait():
        for k in range(1, groups):
            group_copy(k).wait_recv()
        summed = jnp.zeros(four.shape, WIDE)
        for number in range(groups):
            term = mail[3]
            for k in range(1, groups):
                source = lax.rem(group + groups - k, groups)
                term = jnp.where(source == number, inbox[2 + k], term)
            summed = summed + term
        four[...] = summed
        for stage in range(3):
            mail_copy(stage).wait_send()
        for k in range(1, groups):
            group_copy(k).wait_send()

    share = out_sum.shape[0]

    def out_rows(number):
        return out_grad.at[pl.ds(pl.multiple_of(number * share, share), share), :]

    def out_keep():
        return pltpu.make_async_copy(out_sum, out_rows(group), sems.at[2, 2])

    def out_copy(phase, side):
        number = group - phase * side
        at = 0 if side > 0 else groups
        return pltpu.make_async_remote_copy(
            src_ref=out_sum if phase == 0 else out_rows(number),
            dst_ref=out_rows(number),
            send_sem=line.send.at[at + phase],
            recv_sem=line.recv.at[at + phase],
            device_id=(group + side, ring.me),
            device_id_type=MESH_ID,
        )

    def goes(phase, side):
        number, peer = group - phase * side, group + side
        return (number >= 0) & (number < groups) & (peer >= 0) & (peer < groups)

    def comes(phase, side):
        number = group - (phase + 1) * side
        return (number >= 0) & (number < groups)

    def out_phase(phase):
        for side in (1, -1):
            if phase:

                @pl.when(comes(phase - 1, side))
                def _():
                    out_copy(phase - 1, side).wait_recv()

            if phase < groups - 1:

                @pl.when(goes(phase, side))
                def _():
                    out_copy(phase, side).start()

    def out_end():
        out_keep().wait()
        for phase in range(groups - 1):
            for side in (1, -1):

                @pl.when(goes(phase, side))
                def _():
                    out_copy(phase, side).wait_send()

    def layer_end():
        layer_out[...] = (resid[...] + second_sum.total[...]).astype(LOW)

    def product():
        for copy in mix_loads:
            copy.wait()
        copies = []
        for i in range(per):
            rows = pl.ds(i * TILE, TILE)
            if i >= 2:
                copies[i - 2].wait()
            item = jnp.zeros((TILE, shelf.shape[2]), WIDE)
            for c in range(3):
                item = item + mm(mixin[c, rows, :], mix[c], NT)
            shelf[i % 2] = item.astype(LOW)
            copies.append(pltpu.make_async_copy(shelf.at[i % 2], mix_part.at[rows, :], sems.at[3, i % 2]))
            copies[i].start()
        for copy in copies[-2:]:
            copy.wait()

    def stage(item, number):
        return lambda: item.stage(number)

    plan = {
        1: [stage(u2, 1), stage(g2, 0)],
        2: [stage(u2, 2), lambda: out_phase(1)],
        3: [stage(u2, 3), stage(g2, 1)],
        4: [stage(g2, 2), stage(u3, 0), stage(u2, 4), stage(g2, 3), stage(g2, 4), stage(g3, 0)],
        5: [stage(u3, 1), lambda: out_phase(2)],
        6: [stage(u3, 2), stage(g3, 1), stage(one, 0)],
        7: [stage(u3, 3), stage(g3, 2), stage(one, 1)],
        8: [stage(g3, 3), stage(u3, 4), stage(g3, 4), stage(second_sum, 0), lambda: out_phase(3)],
        9: [stage(one, 2), stage(second_sum, 1)],
        10: [stage(one, 3), first_norm, lambda: mail_start(0)],
        11: [lambda: mail_wait(0), lambda: mail_start(1), stage(second_sum, 2)],
    }

    def fetch(source, tile, side):
        start = tile * TILE if isinstance(tile, int) else pl.multiple_of(tile * TILE, TILE)
        rows = pl.ds(start, TILE)
        return [
            pltpu.make_async_copy(two_sources[source].at[rows, :], two.at[side], sems.at[side, 0]),
            pltpu.make_async_copy(up_sources[source].at[rows, :], up.at[side], sems.at[side, 1]),
        ]

    mix_loads = load([(mixin_hbm, mixin), (mix_hbm, mix)], sems.at[4])
    weights = load([(wide_hbm, wide), (down_hbm, down)], sems.at[2])
    for copy in fetch(0, 0, 0):
        copy.start()
    resume = pltpu.make_async_copy(begun, acc, outs.at[0])
    resume.start()
    out_keep().start()
    out_phase(0)
    u2.stage(0)

    def add(side, trio):
        acc[2] += mm(trio[0], up[side])
        acc[0] += mm(trio[1], two[side])
        acc[1] += mm(trio[2], two[side])

    steps = per * (groups - 1)

    def start_fetch(step):
        side = lax.rem(step, 2)
        for source in range(groups - 1):

            @pl.when((step < steps) & (step // per == source))
            def _():
                for copy in fetch(source, lax.rem(step, per), side):
                    copy.start()

    def events(step):
        for at, acts in plan.items():

            @pl.when(step == at)
            def _():
                for act in acts:
                    act()


    product()
    for copy in weights:
        copy.wait()
    resume.wait()

    def body(step, carry):
        events(step)
        side = lax.rem(step, 2)

        @pl.when((lax.rem(step, per) == 0) & (step > 0))
        def _():
            start_fetch(step)

        for copy in fetch(0, 0, side):
            copy.wait()

        @pl.when(lax.rem(step + 1, per) != 0)
        def _():
            start_fetch(step + 1)

        add(side, forward_units(two[side], up[side], wide, down))
        return carry

    lax.fori_loop(0, steps, body, 0)
    mail_wait(1)
    mail_start(2)
    wide[...] = acc[0:2].astype(LOW)
    copies = load([(wide, wide_grad)], outs)
    mail_wait(2)
    group_start()
    down[...] = acc[2].astype(LOW)
    copies += load([(down, down_grad)], outs.at[pl.ds(1, 1)])
    second_sum.stage(3)
    layer_end()
    group_wait()
    out_end()
    for copy in copies:
        copy.wait()


def last(mixin, mix, down_part, tokens, resid, resid_back, gains, sums, bias_term, out_sum,
         begun, two_far, up_far, up_one, two_one, wide, down):
    total, width = two_one.shape
    rows = tokens.shape[0]
    local = down.shape[0]
    groups = lax.axis_size("grp")
    tall = (((total, width), LOW), ANY)
    block = (((rows, width), LOW), VM)
    return call(
        last_kernel,
        8,
        [(mixin, ANY), (mix, ANY), (down_part, ANY)]
        + [(item, VM) for item in (tokens, resid, resid_back, gains, sums, bias_term, out_sum)]
        + [(item, ANY) for item in (begun, two_far, up_far, up_one, two_one, wide, down)],
        [
            block,
            block,
            (((8, width), WIDE), VM),
            (((out_sum.shape[0] * groups, width), LOW), ANY),
            (((2, local, width), LOW), ANY),
            (((local, width), LOW), ANY),
            tall, tall, tall, tall, tall,
        ],
        [
            pltpu.VMEM((2, TILE, width), LOW),
            pltpu.VMEM((2, TILE, width), LOW),
            pltpu.VMEM((2, local, width), LOW),
            pltpu.VMEM((local, width), LOW),
            pltpu.VMEM((3, local, width), WIDE),
            pltpu.VMEM(mixin.shape, LOW),
            pltpu.VMEM(mix.shape, LOW),
            pltpu.VMEM((2, TILE, width), LOW),
            pltpu.VMEM((2 + groups, 8, width), WIDE),
            pltpu.VMEM((4, 8, width), WIDE),
            pltpu.SemaphoreType.DMA((5, 3)),
            pltpu.SemaphoreType.DMA((2,)),
            pltpu.SemaphoreType.DMA((2 + groups,)),
            pltpu.SemaphoreType.DMA((2 + groups,)),
        ]
        + scatter_scratch(rows, width) * 2
        + gather_sems() * N_LAST_GATHERS
        + [pltpu.SemaphoreType.DMA((2 * groups,)), pltpu.SemaphoreType.DMA((2 * groups,))],
        limit=62,
        flops=72 << 30,
        cost=120 << 20,
    )


RING = 8


def mask_kernel(row_lengths, row_group, cotangent, upstream):
    group = lax.axis_index("grp")
    load = jnp.int32(0)
    for row in range(row_lengths.shape[0]):
        load = load + jnp.where(row_group[row] == group, row_lengths[row], 0)
    first = lax.axis_index("seq") * cotangent.shape[0]
    slots = first + lax.broadcasted_iota(jnp.int32, cotangent.shape, 0)
    wide = cotangent[...].astype(jnp.float32)
    upstream[...] = jnp.where(slots < load, wide, 0.0).astype(upstream.dtype)


def mask_rows(row_lengths, row_group, cotangent):
    return pl.pallas_call(
        mask_kernel,
        out_shape=jax.ShapeDtypeStruct(cotangent.shape, cotangent.dtype),
        in_specs=[SM, SM, VM],
        out_specs=VM,
    )(row_lengths, row_group, cotangent)


def widen_kernel(low, wide):
    wide[...] = low[...].astype(jnp.float32)


def widen(low, pieces):
    rows, width = low.shape
    spec = pl.BlockSpec((rows // pieces, width), lambda i: (i, 0))
    return pl.pallas_call(
        widen_kernel,
        grid=(pieces,),
        out_shape=jax.ShapeDtypeStruct(low.shape, jnp.float32),
        in_specs=[spec],
        out_specs=spec,
        compiler_params=pltpu.CompilerParams(vmem_limit_bytes=32 << 20),
        cost_estimate=pl.CostEstimate(flops=low.size, bytes_accessed=6 * low.size, transcendentals=0),
    )(low)


def on_device(
    tokens,
    norm_gains,
    norm_biases,
    mix_weight,
    mix_bias,
    out_weight,
    gate_up_weight,
    down_weight,
    row_lengths,
    row_group,
    cotangent,
):
    count = lax.axis_size("seq")
    upstream = mask_rows(row_lengths, row_group, cotangent)
    mix_t = jnp.transpose(mix_weight, (1, 0, 2))
    wide_t = jnp.transpose(gate_up_weight, (1, 2, 0))

    up_far = lax.all_gather(upstream, "grp", axis=0, tiled=True)
    (
        query, key, value, attended, lse, normed_all, up_all, resid, two_all, two_mine,
        tables, lab_col, lab_row,
    ) = attend_heads(
        row_lengths, row_group, tokens, norm_gains, norm_biases, upstream, mix_t, out_weight, mix_bias, count
    )
    two_far = lax.all_gather(two_mine, "grp", axis=0, tiled=True)
    down_part, begun, up_one, resid_back, branch_all, sums = feed(
        two_all, up_all, wide_t, down_weight, up_far, resid, upstream, norm_gains
    )
    mixin, mix_term, out_sum, bias_term, two_one = attend_heads_back(
        branch_all, normed_all, out_weight, tables, lab_col, lab_row,
        (query, key, value, attended, lse), two_far,
    )
    mix_grad = lax.psum(mix_term, "grp")
    tokens_grad, layer_out, four, out_grad, wide_grad, down_grad = last(
        mixin, mix_t, down_part, tokens, resid, resid_back, norm_gains, sums, bias_term, out_sum,
        begun, two_far, up_far, up_one, two_one, wide_t, down_weight,
    )[:6]
    local = mix_bias.shape[1]
    return (
        layer_out,
        tokens_grad,
        four[0:2],
        four[2:4],
        jnp.transpose(widen(mix_grad.reshape(-1, mix_grad.shape[2]), 6).reshape(mix_grad.shape), (1, 0, 2)),
        four[4, : 3 * local].reshape(3, local),
        widen(out_grad, 4),
        jnp.transpose(widen(wide_grad.reshape(-1, wide_grad.shape[2]), 8).reshape(wide_grad.shape), (2, 0, 1)),
        widen(down_grad, 4),
    )


def solution(mesh):
    placed = (
        P(("grp", "seq"), None),
        P(),
        P(),
        P(None, None, "seq"),
        P(None, "seq"),
        P("seq", None),
        P(None, None, "seq"),
        P("seq", None),
        P(),
        P(),
        P(("grp", "seq"), None),
    )
    return jax.shard_map(
        on_device if mesh.shape["seq"] == RING else plain_device,
        mesh=mesh,
        in_specs=placed,
        out_specs=(
            P(("grp", "seq"), None),
            P(("grp", "seq"), None),
            P(),
            P(),
            P(None, None, "seq"),
            P(None, "seq"),
            P("seq", None),
            P(None, None, "seq"),
            P("seq", None),
        ),
        check_vma=False,
    )
```
